128 devices in a mesh: dev: 128 (over y, x, z, core).
Axes of the slice: x: 4, y: 4, z: 4, core: 2. Of those that a mesh axis runs over, the one named last changes fastest.
Arguments:
- field_in: float32 [32, 8, 512, 128], P(None, None, 'dev'), may hold values from -6 to 6
- source: float32 [32, 8, 512, 128], P(None, None, 'dev'), may hold values from -12 to 12
- cell_factor: float32 [8, 512, 128], P(None, 'dev'), may hold values from 0.5 to 2
- layer_material: int32 [8], replicated, may hold values from 0 to 3
- material_scale: float32 [4], replicated, may hold values from 0.25 to 4
- panel_cell: int32 [131072], P('dev'), may hold values from 0 to 65535
- panel_pos: float32 [3, 131072], replicated, may hold values from 0 to 1
- panel_area: float32 [131072], replicated, may hold values from 0.5 to 2
- flux_in: float32 [32, 131072], P(None, 'dev'), may hold values from -6 to 6
- pair_list: int32 [2048, 2], P('dev'), may hold values from -1 to 63, as said below
Outputs:
- field_out: float32 [32, 8, 512, 128], P(None, None, 'dev')
- flux_out: float32 [32, 131072], P(None, 'dev')
The draws below stay inside these ranges and needn't reach their ends.
Inputs may be any that keep to these rules, and one draw needn't show every extreme that they name: `pair_list`: each row is a tile pair (i, j) with i >= j, or (-1, -1) for an empty slot. No pair is listed twice. In each device's 16 rows the pairs come first, then the empty slots; at least a quarter of every device's slots are filled, and some device has all 16 filled.
All inputs are finite; a program needn't handle non-finite values.
Results may differ from the reference program's by a relative error of at most 0.0038.
Values may be sent and summed in bfloat16 or wider, within the bound.
A program may use at most 192 MiB of HBM per device.

```python
import math
import jax
import jax.numpy as jnp
from jax import lax

LOADS = 32
LAYERS = 8
NY = 128
MATS = 4
TILE = 2048
NX = 512
PANELS = 131072
SLOTS = 16
N_DEV = 128


def draw_pair_list(key, part):
    num_tiles = PANELS // TILE
    total_pairs = num_tiles * (num_tiles + 1) // 2
    count_key, full_key, order_key = jax.random.split(key, 3)
    lowest = max(1, (SLOTS + 3) // 4)
    counts = jax.random.randint(count_key, (N_DEV,), lowest, SLOTS + 1)
    fullest = jax.random.randint(full_key, (), 0, N_DEV)
    counts = jnp.where(jnp.arange(N_DEV, dtype=jnp.int32) == fullest, SLOTS, counts).astype(jnp.int32)
    offsets = jnp.cumsum(counts) - counts
    ordering = jax.random.permutation(order_key, total_pairs).astype(jnp.int32)
    slot_ids = jnp.arange(SLOTS, dtype=jnp.int32)
    position = jnp.clip(offsets[:, None] + slot_ids[None, :], 0, total_pairs - 1)
    filled = slot_ids[None, :] < counts[:, None]
    chosen = ordering[position]
    tile_ids = jnp.arange(num_tiles, dtype=jnp.int32)
    bases = tile_ids * (tile_ids + 1) // 2
    upper = jnp.sum((bases[None, None, :] <= chosen[:, :, None]).astype(jnp.int32), axis=2) - 1
    lower = chosen - upper * (upper + 1) // 2
    upper = jnp.where(filled, upper, -1)
    lower = jnp.where(filled, lower, -1)
    return jnp.stack([upper.reshape(-1), lower.reshape(-1)], axis=1).astype(jnp.int32)


def touch_ends(values, rng, smallest, top_value):
    extent = values.shape
    place = [jax.random.randint(jax.random.fold_in(rng, axis), (), 0, extent[axis]) for axis in range(len(extent))]
    values = values.at[tuple(place)].set(smallest)
    longest = extent.index(max(extent))
    place[longest] = (place[longest] + 1) % extent[longest]
    return values.at[tuple(place)].set(top_value)


def steps_of(own_key, dims, cuts, low, high):
    gain, own = 1.0, jax.random.fold_in(own_key, 6)
    for axis_at, parts in cuts:
        steps = jnp.exp(jax.random.uniform(jax.random.fold_in(own, axis_at), (parts,), jnp.float32, low / len(cuts), high / len(cuts)))
        gain = gain * jnp.repeat(steps, dims[axis_at] // parts).reshape([-1 if axis == axis_at else 1 for axis in range(len(dims))])
    return gain


def normal_values(rng, extent, deviation, bound, shards=(), kind=jnp.bfloat16):
    array = jax.random.normal(rng, extent, jnp.float32) * deviation
    if len(shards) > 0:
        array = steps_of(rng, extent, shards, -0.22, 0.18) * array
    return jnp.clip(array, min=-bound, max=bound).astype(kind)


def setup_inputs(seed: int = 0) -> dict:
    arg_keys = jax.random.split(jax.random.key(seed), 11)
    field_in = normal_values(arg_keys[0], (LOADS, LAYERS, NX, NY), 1.0, 6.0, ((2, 128),), jnp.float32)
    source = normal_values(arg_keys[1], (LOADS, LAYERS, NX, NY), 2.0, 12.0, ((2, 128),), jnp.float32)
    cell_factor = jnp.clip(jnp.exp(math.log(2.0) - 1.3862944 * jax.random.uniform(arg_keys[2], (LAYERS, NX, NY), jnp.float32) ** steps_of(arg_keys[2], (LAYERS, NX, NY), ((1, 128),), -0.2, 0.2)), 0.5, 2.0)
    layer_material = touch_ends(jax.random.randint(arg_keys[3], (LAYERS,), 0, MATS), jax.random.fold_in(arg_keys[3], 1), 0, MATS - 1).astype(jnp.int32)
    material_scale = jnp.clip(jnp.exp(jax.random.uniform(arg_keys[4], (MATS,), jnp.float32, math.log(0.25), math.log(4.0))), 0.25, 4.0)
    panel_cell = touch_ends(jax.random.randint(arg_keys[5], (PANELS,), 0, NX * NY), jax.random.fold_in(arg_keys[5], 1), 0, (NX * NY) - 1).astype(jnp.int32)
    panel_pos = jnp.clip(jax.random.uniform(arg_keys[6], (3, PANELS), jnp.float32, 0.0, 1.0), 0.0, 1.0)
    panel_area = jnp.clip(jnp.exp(jax.random.uniform(arg_keys[7], (PANELS,), jnp.float32, math.log(0.5), math.log(2.0))), 0.5, 2.0)
    flux_in = normal_values(arg_keys[8], (LOADS, PANELS), 1.0, 6.0, ((1, 128),), jnp.float32)
    pair_list = draw_pair_list(jax.random.fold_in(arg_keys[10], 71), 0)
    return dict(field_in=field_in, source=source, cell_factor=cell_factor, layer_material=layer_material, material_scale=material_scale, panel_cell=panel_cell, panel_pos=panel_pos, panel_area=panel_area, flux_in=flux_in, pair_list=pair_list)


softening = 0.0004
relax_rate = 0.8
update_rate = 0.5
kernel_gain = 0.25

def coefficient(cell_factor, layer_material, material_scale):
    matched = layer_material[:, None] == jnp.arange(material_scale.shape[0], dtype=jnp.int32)[None, :]
    layer_scale = lax.optimization_barrier(jnp.sum(jnp.where(matched, material_scale[None, :], 0.0), axis=1))
    return layer_scale[:, None, None] * cell_factor

def relax_rows(widened, source, conduct):
    centre = widened[:, :, 1:-1, :]
    padded = jnp.pad(centre, ((0, 0), (1, 1), (0, 0), (1, 1)))
    beside = padded[:, 2:, :, 1:-1] + padded[:, :-2, :, 1:-1] + (widened[:, :, 2:, :] + widened[:, :, :-2, :]) + (padded[:, 1:-1, :, 2:] + padded[:, 1:-1, :, :-2])
    applied = conduct * (6.0 * centre - beside) + centre
    return centre + relax_rate * (source - applied) / (6.0 * conduct + 1.0)

def kernel_tile(row_pos, row_area, col_pos, col_area):
    delta_x = row_pos[0][:, None] - col_pos[0][None, :]
    delta_y = row_pos[1][:, None] - col_pos[1][None, :]
    delta_z = row_pos[2][:, None] - col_pos[2][None, :]
    distance = delta_x * delta_x + delta_y * delta_y + delta_z * delta_z
    weight = row_area[:, None] * col_area[None, :]
    return (weight * lax.rsqrt(distance + softening) * (kernel_gain / math.sqrt(TILE))).astype(jnp.bfloat16)

def apply_pairs(pair_rows, flux_half, panel_pos, panel_area, totals):
    load_count = flux_half.shape[0]

    def visit(totals, pair_row):
        upper = pair_row[0]
        lower = pair_row[1]

        def work(totals):
            anchor = jnp.int32(0)
            row_start = (upper * TILE).astype(jnp.int32)
            col_start = (lower * TILE).astype(jnp.int32)
            tile_block = kernel_tile(lax.dynamic_slice(panel_pos, (anchor, row_start), (3, TILE)), lax.dynamic_slice(panel_area, (row_start,), (TILE,)), lax.dynamic_slice(panel_pos, (anchor, col_start), (3, TILE)), lax.dynamic_slice(panel_area, (col_start,), (TILE,)))
            row_flux = lax.dynamic_slice(flux_half, (anchor, row_start), (load_count, TILE))
            col_flux = lax.dynamic_slice(flux_half, (anchor, col_start), (load_count, TILE))
            onward = jnp.dot(row_flux, tile_block, preferred_element_type=jnp.float32)
            current = lax.dynamic_slice(totals, (anchor, col_start), (load_count, TILE))
            totals = lax.dynamic_update_slice(totals, current + onward, (anchor, col_start))

            def transposed(totals):
                backward = lax.dot_general(col_flux, tile_block, (((1,), (1,)), ((), ())), preferred_element_type=jnp.float32)
                present = lax.dynamic_slice(totals, (anchor, row_start), (load_count, TILE))
                return lax.dynamic_update_slice(totals, present + backward, (anchor, row_start))
            return lax.cond(upper != lower, transposed, lambda kept: kept, totals)
        return (lax.cond(upper >= 0, work, lambda kept: kept, totals), None)
    totals, unused = lax.scan(visit, totals, pair_rows)
    return totals

def reference(field_in, source, cell_factor, layer_material, material_scale, panel_cell, panel_pos, panel_area, flux_in, pair_list):
    conduct = coefficient(cell_factor, layer_material, material_scale)
    field_now = field_in
    for repeat in range(2):
        widened = jnp.pad(field_now, ((0, 0), (0, 0), (1, 1), (0, 0)))
        field_now = relax_rows(widened, source, conduct)
    surface_top = field_now[:, -1].astype(jnp.bfloat16)
    flattened = surface_top.reshape(surface_top.shape[0], -1)
    traces = jnp.take(flattened, panel_cell, axis=1)
    flux_half = flux_in.astype(jnp.bfloat16)
    totals = jnp.zeros(flux_in.shape, jnp.float32)
    potential = apply_pairs(pair_list, flux_half, panel_pos, panel_area, totals)
    flux_out = flux_in + update_rate * (traces.astype(jnp.float32) - potential)
    return (field_now, flux_out)
```

```python
import functools
import math

import jax
import jax.numpy as jnp
from jax import lax
from jax.experimental import pallas as pl
from jax.experimental.pallas import tpu as pltpu
from jax.sharding import PartitionSpec as P

TILE = 2048
TILES = 64
LINE = 8
PLANE = 16
COLS = 4 * TILE

softening = 0.0004
relax_rate = 0.8
update_rate = 0.5
kernel_gain = 0.25


def padded_2(array, sides, width):
    for axis, dim in sides:
        size, length = (lax.axis_size(axis), array.shape[dim])
        up = [(i, (i + 1) % size) for i in range(size - 1)]
        down = [(j, i) for i, j in up]
        last = lax.slice_in_dim(array, length - width, length, axis=dim)
        first = lax.slice_in_dim(array, 0, width, axis=dim)
        before = lax.ppermute(last, axis, up)
        after = lax.ppermute(first, axis, down)
        array = jnp.concatenate([before, array, after], axis=dim)
    return array


def coefficient(cell_factor, layer_material, material_scale):
    matched = (
        layer_material[:, None] == jnp.arange(material_scale.shape[0], dtype=jnp.int32)[None, :]
    )
    layer_scale = jnp.sum(jnp.where(matched, material_scale[None, :], 0.0), axis=1)
    return layer_scale[:, None, None] * cell_factor


def relax_rows(widened, source, conduct):
    centre = widened[:, :, 1:-1, :]
    padded = jnp.pad(centre, ((0, 0), (1, 1), (0, 0), (1, 1)))
    beside = (
        padded[:, 2:, :, 1:-1]
        + padded[:, :-2, :, 1:-1]
        + (widened[:, :, 2:, :] + widened[:, :, :-2, :])
        + (padded[:, 1:-1, :, 2:] + padded[:, 1:-1, :, :-2])
    )
    applied = conduct * (6.0 * centre - beside) + centre
    return centre + relax_rate * (source - applied) / (6.0 * conduct + 1.0)


def split3(value):
    high = lax.reduce_precision(value, 8, 7)
    rest = value - high
    middle = lax.reduce_precision(rest, 8, 7)
    low = lax.reduce_precision(rest - middle, 8, 7)
    return high, middle, low


def features(pos, area, row_side):
    pos = pos - 0.5
    scale = math.sqrt(TILE) / kernel_gain / (area * area)
    norm = jnp.sum(pos * pos, axis=0)
    if row_side:
        parts = jnp.stack(
            [scale * (norm + softening), scale] + [-2.0 * scale * pos[a] for a in range(3)]
        )
    else:
        parts = jnp.stack([scale, scale * norm] + [scale * pos[a] for a in range(3)])
    high, middle, low = split3(parts)
    if row_side:
        stack = [high, high, middle, middle, high, low]
    else:
        stack = [high, middle, high, middle, low, high]
    stack.append(jnp.zeros((2,) + parts.shape[1:], jnp.float32))
    return jnp.concatenate(stack, axis=0).astype(jnp.bfloat16)


def pair_kernel(mask_ref, f_ref, pt_ref, q_ref, o_ref, order_ref):
    for j in range(4):

        def note(i, count):
            order_ref[count] = i
            return count + mask_ref[j * TILES + i]

        count = lax.fori_loop(0, TILES, note, jnp.int32(0))
        order_ref[count] = TILES
        o_ref[:, j * TILE : (j + 1) * TILE] = jnp.zeros((32, TILE), jnp.float32)

        def step(b, carry):
            first = order_ref[2 * b]
            second = order_ref[2 * b + 1]
            flux = jnp.concatenate([f_ref[first], f_ref[second]], axis=1)
            for c in range(2):
                columns = pl.ds(j * TILE + c * 1024, 1024)
                block = []
                for which in (first, second):
                    distance = jnp.dot(
                        pt_ref[which], q_ref[:, columns], preferred_element_type=jnp.float32
                    )
                    block.append(lax.rsqrt(distance).astype(jnp.bfloat16))
                o_ref[:, columns] += jnp.dot(
                    flux, jnp.concatenate(block, axis=0), preferred_element_type=jnp.float32
                )
            return carry

        lax.fori_loop(0, (count + 1) // 2, step, 0)


def apply_pairs(mask, flux_rows, row_features, col_features):
    vmem = pl.BlockSpec(memory_space=pltpu.VMEM)
    return pl.pallas_call(
        pair_kernel,
        out_shape=jax.ShapeDtypeStruct((32, COLS), jnp.float32),
        in_specs=[pl.BlockSpec(memory_space=pltpu.SMEM), vmem, vmem, vmem],
        out_specs=vmem,
        scratch_shapes=[pltpu.SMEM((TILES + 2,), jnp.int32)],
        compiler_params=pltpu.CompilerParams(vmem_limit_bytes=40 << 20),
        cost_estimate=pl.CostEstimate(
            flops=100_000_000_000, bytes_accessed=8 << 20, transcendentals=0
        ),
    )(mask, flux_rows, row_features, col_features)


def body(
    field_in,
    source,
    cell_factor,
    layer_material,
    material_scale,
    panel_cell,
    panel_pos,
    panel_area,
    flux_in,
    pair_list,
):
    lines = [[LINE * m + r for r in range(LINE)] for m in range(PLANE)]
    planes = [[LINE * m + r for m in range(PLANE)] for r in range(LINE)]
    me = lax.axis_index("dev")
    m, r = me // LINE, me % LINE

    pairs = lax.all_gather(pair_list, "dev", axis=0, tiled=True)
    tile_ids = jnp.arange(TILES, dtype=jnp.int32)
    upper = (pairs[:, 0:1] == tile_ids[None, :]).astype(jnp.bfloat16)
    lower = (pairs[:, 1:2] == tile_ids[None, :]).astype(jnp.bfloat16)
    listed = lax.dot_general(
        upper, lower, (((0,), (0,)), ((), ())), preferred_element_type=jnp.float32
    )
    listed = (listed + listed.T > 0.0).astype(jnp.int32)
    mask = lax.dynamic_slice(listed, (4 * m, 0), (4, TILES)).reshape(-1)

    flux_half = flux_in.astype(jnp.bfloat16).reshape(32, LINE, 128).transpose(1, 0, 2)
    shared = lax.all_to_all(flux_half, "dev", 0, 0, axis_index_groups=lines)
    rows = lax.all_gather(shared, "dev", axis=0, tiled=True, axis_index_groups=planes)
    rows = rows.reshape(TILES, 2, 32, 128).transpose(0, 2, 1, 3).reshape(TILES, 32, 256)
    rows = jnp.concatenate([rows, jnp.zeros((1, 32, 256), jnp.bfloat16)], axis=0)

    row_pos = lax.dynamic_index_in_dim(panel_pos.reshape(3, 128, LINE, 128), r, 2, False)
    row_area = lax.dynamic_index_in_dim(panel_area.reshape(128, LINE, 128), r, 1, False)
    row_features = features(row_pos.reshape(3, -1), row_area.reshape(-1), True)
    row_features = row_features.reshape(32, TILES, 256).transpose(1, 2, 0)
    row_features = jnp.concatenate([row_features, row_features[:1]], axis=0)
    col_features = features(
        lax.dynamic_slice(panel_pos, (0, m * COLS), (3, COLS)),
        lax.dynamic_slice(panel_area, (m * COLS,), (COLS,)),
        False,
    )

    conduct = coefficient(cell_factor, layer_material, material_scale)
    field_now = field_in
    for repeat in range(2):
        widened = padded_2(field_now, (("dev", 2),), 1)
        field_now = relax_rows(widened, source, conduct)
    surface_top = field_now[:, -1].astype(jnp.bfloat16)
    gathered = lax.all_gather(surface_top, "dev", axis=1, tiled=True)
    flattened = gathered.reshape(gathered.shape[0], -1)

    partial = apply_pairs(mask, rows, row_features, col_features)
    potential = lax.psum_scatter(
        partial, "dev", scatter_dimension=1, axis_index_groups=lines, tiled=True
    )
    traces = jnp.take(flattened, panel_cell, axis=1)
    flux_out = flux_in + update_rate * (traces.astype(jnp.float32) - potential)
    return (field_now, flux_out)


def solution(mesh):
    in_specs = (
        P(None, None, "dev", None),
        P(None, None, "dev", None),
        P(None, "dev", None),
        P(),
        P(),
        P("dev"),
        P(),
        P(),
        P(None, "dev"),
        P("dev", None),
    )
    out_specs = (P(None, None, "dev", None), P(None, "dev"))
    return jax.shard_map(body, mesh=mesh, in_specs=in_specs, out_specs=out_specs, check_vma=False)
```

```python
import math

import jax
import jax.numpy as jnp
from jax import lax
from jax.experimental import pallas as pl
from jax.experimental.pallas import tpu as pltpu
from jax.sharding import PartitionSpec as P

TILE = 2048
TILES = 64
LAYERS = 8
LINE = 8
PLANE = 16
COLS = 4 * TILE

softening = 0.0004
relax_rate = 0.8
update_rate = 0.5
kernel_gain = 0.25


def coefficient(cell_factor, layer_material, material_scale):
    matched = (
        layer_material[:, None] == jnp.arange(material_scale.shape[0], dtype=jnp.int32)[None, :]
    )
    layer_scale = jnp.sum(jnp.where(matched, material_scale[None, :], 0.0), axis=1)
    return layer_scale[:, None, None] * cell_factor


def relax_rows(widened, source, conduct):
    centre = widened[:, :, 1:-1, :]
    padded = jnp.pad(centre, ((0, 0), (1, 1), (0, 0), (1, 1)))
    beside = (
        padded[:, 2:, :, 1:-1]
        + padded[:, :-2, :, 1:-1]
        + (widened[:, :, 2:, :] + widened[:, :, :-2, :])
        + (padded[:, 1:-1, :, 2:] + padded[:, 1:-1, :, :-2])
    )
    applied = conduct * (6.0 * centre - beside) + centre
    return centre + relax_rate * (source - applied) / (6.0 * conduct + 1.0)


def split3(value):
    high = lax.reduce_precision(value, 8, 7)
    rest = value - high
    middle = lax.reduce_precision(rest, 8, 7)
    low = lax.reduce_precision(rest - middle, 8, 7)
    return high, middle, low


def features(pos, area, row_side):
    pos = pos - 0.5
    scale = math.sqrt(TILE) / kernel_gain / (area * area)
    norm = jnp.sum(pos * pos, axis=0)
    if row_side:
        parts = jnp.stack(
            [scale * (norm + softening), scale] + [-2.0 * scale * pos[a] for a in range(3)]
        )
    else:
        parts = jnp.stack([scale, scale * norm] + [scale * pos[a] for a in range(3)])
    high, middle, low = split3(parts)
    if row_side:
        stack = [high, high, middle, middle, high, low]
    else:
        stack = [high, middle, high, middle, low, high]
    stack.append(jnp.zeros((2,) + parts.shape[1:], jnp.float32))
    return jnp.concatenate(stack, axis=0).astype(jnp.bfloat16)


def pair_kernel(mask_ref, f_ref, pt_ref, q_ref, o_ref, total_ref, order_ref):
    for j in range(4):

        def note(i, count):
            order_ref[count] = i
            return count + mask_ref[j * TILES + i]

        count = lax.fori_loop(0, TILES, note, jnp.int32(0))
        order_ref[count] = 0
        total_ref[...] = jnp.zeros((32, TILE), jnp.float32)

        def flux_of(i):
            at = pl.multiple_of((i % 4) * 64, 64)
            return [f_ref[i // 4, pl.ds(at, 32), :], f_ref[i // 4, pl.ds(at + 32, 32), :]]

        def step(b, carry):
            first = order_ref[2 * b]
            second = order_ref[2 * b + 1]
            there = 2 * b + 1 < count
            later = [jnp.where(there, part, jnp.zeros_like(part)) for part in flux_of(second)]
            flux = jnp.concatenate(flux_of(first) + later, axis=1)
            for c in range(2):
                columns = pl.ds(j * TILE + c * 1024, 1024)
                block = []
                for which in (first, second):
                    distance = jnp.dot(
                        pt_ref[which], q_ref[:, columns], preferred_element_type=jnp.float32
                    )
                    block.append(lax.rsqrt(distance).astype(jnp.bfloat16))
                total_ref[:, c * 1024 : (c + 1) * 1024] += jnp.dot(
                    flux, jnp.concatenate(block, axis=0), preferred_element_type=jnp.float32
                )
            return carry

        lax.fori_loop(0, (count + 1) // 2, step, 0)
        for c in range(2):
            o_ref[2 * j + c] = total_ref[:, c * 1024 : (c + 1) * 1024].astype(jnp.bfloat16)


def apply_pairs(mask, flux_rows, row_features, col_features):
    vmem = pl.BlockSpec(memory_space=pltpu.VMEM)
    return pl.pallas_call(
        pair_kernel,
        out_shape=jax.ShapeDtypeStruct((LINE, 32, 1024), jnp.bfloat16),
        in_specs=[pl.BlockSpec(memory_space=pltpu.SMEM), vmem, vmem, vmem],
        out_specs=vmem,
        scratch_shapes=[
            pltpu.VMEM((32, TILE), jnp.float32),
            pltpu.SMEM((TILES + 2,), jnp.int32),
        ],
        compiler_params=pltpu.CompilerParams(vmem_limit_bytes=40 << 20),
        cost_estimate=pl.CostEstimate(
            flops=100_000_000_000, bytes_accessed=8 << 20, transcendentals=0
        ),
    )(mask, flux_rows, row_features, col_features)


def remote(src, dst, sends, recvs, at, device):
    return pltpu.make_async_remote_copy(
        src_ref=src,
        dst_ref=dst,
        send_sem=sends.at[at],
        recv_sem=recvs.at[at],
        device_id=(device,),
        device_id_type=pl.DeviceIdType.MESH,
    )


def greet(devices):
    barrier = pltpu.get_barrier_semaphore()
    for device in devices:
        pl.semaphore_signal(
            barrier, inc=1, device_id=(device,), device_id_type=pl.DeviceIdType.MESH
        )
    pl.semaphore_wait(barrier, len(devices))


def exchange_kernel(
    flux_ref,
    edge_ref,
    rows_ref,
    halo_ref,
    shared,
    line_send,
    line_recv,
    plane_send,
    plane_recv,
    edge_send,
    edge_recv,
):
    me = lax.axis_index("dev")
    m, r = me // LINE, lax.rem(me, LINE)
    line = [LINE * m + lax.rem(r + k, LINE) for k in range(1, LINE)]
    plane = [LINE * lax.rem(m + k, PLANE) + r for k in range(1, PLANE)]
    after = lax.rem(me + 1, LINE * PLANE)
    before = lax.rem(me + LINE * PLANE - 1, LINE * PLANE)
    greet(line + plane + [after, before])

    copies = []
    for k in range(1, LINE):
        there = lax.rem(r + k, LINE)
        copy = remote(
            flux_ref.at[there], shared.at[r], line_send, line_recv, k - 1, line[k - 1]
        )
        copy.start()
        copies.append(copy)
    edges = [
        remote(edge_ref.at[0], halo_ref.at[0], edge_send, edge_recv, 0, after),
        remote(edge_ref.at[1], halo_ref.at[1], edge_send, edge_recv, 1, before),
    ]
    for copy in edges:
        copy.start()
    shared[r] = flux_ref[r]
    for copy in copies:
        copy.wait()

    lists = jnp.zeros((16, 128), jnp.float32)
    for s in range(LINE):
        rows_ref[m, 32 * s : 32 * s + 32, :] = shared[s, 0:32, :]
        lists = lists + shared[s, 32:48, :].astype(jnp.float32)
    rows_ref[m, 256:272, :] = lists.astype(jnp.bfloat16)

    copies = []
    for k in range(1, PLANE):
        copy = remote(
            rows_ref.at[m], rows_ref.at[m], plane_send, plane_recv, k - 1, plane[k - 1]
        )
        copy.start()
        copies.append(copy)
    for copy in copies + edges:
        copy.wait()


def exchange(flux, edge):
    vmem = pl.BlockSpec(memory_space=pltpu.VMEM)
    return pl.pallas_call(
        exchange_kernel,
        out_shape=(
            jax.ShapeDtypeStruct((PLANE, 272, 128), jnp.bfloat16),
            jax.ShapeDtypeStruct(edge.shape, jnp.float32),
        ),
        in_specs=[vmem, vmem],
        out_specs=(vmem, vmem),
        scratch_shapes=[
            pltpu.VMEM((LINE, 48, 128), jnp.bfloat16),
            pltpu.SemaphoreType.DMA((LINE - 1,)),
            pltpu.SemaphoreType.DMA((LINE - 1,)),
            pltpu.SemaphoreType.DMA((PLANE - 1,)),
            pltpu.SemaphoreType.DMA((PLANE - 1,)),
            pltpu.SemaphoreType.DMA((2,)),
            pltpu.SemaphoreType.DMA((2,)),
        ],
        compiler_params=pltpu.CompilerParams(
            collective_id=0, has_side_effects=True, vmem_limit_bytes=16 << 20
        ),
    )(flux, edge)


def finish_kernel(
    cell_ref, part_ref, table_ref, flux_ref, out_ref, table, landed, traces, load_sem, sends, recvs
):
    me = lax.axis_index("dev")
    m, r = me // LINE, lax.rem(me, LINE)
    load = pltpu.make_async_copy(table_ref, table, load_sem)
    load.start()
    line = [LINE * m + lax.rem(r + k, LINE) for k in range(1, LINE)]
    greet(line)
    copies = []
    for k in range(1, LINE):
        there = lax.rem(r + k, LINE)
        copy = remote(part_ref.at[there], landed.at[k - 1], sends, recvs, k - 1, line[k - 1])
        copy.start()
        copies.append(copy)
    load.wait()
    lane = lax.broadcasted_iota(jnp.int32, (32, 128), 1)

    def group(g, carry):
        def pick(step, held):
            for u in range(8):
                at = step * 8 + u
                cell = cell_ref[g * 128 + at]
                block = table[cell // 128].astype(jnp.float32)
                moved = pltpu.roll(block, lax.rem(at + 128 - lax.rem(cell, 128), 128), axis=1)
                held = jnp.where(lane == at, moved, held)
            return held

        traces[g] = lax.fori_loop(0, 16, pick, jnp.zeros((32, 128), jnp.float32))
        return carry

    lax.fori_loop(0, 8, group, 0)
    for copy in copies:
        copy.wait()
    total = part_ref[r].astype(jnp.float32)
    for k in range(LINE - 1):
        total = total + landed[k].astype(jnp.float32)
    for g in range(8):
        at = slice(g * 128, (g + 1) * 128)
        out_ref[:, at] = flux_ref[:, at] + update_rate * (traces[g] - total[:, at])


def finish(cells, partial, table, flux_in):
    vmem = pl.BlockSpec(memory_space=pltpu.VMEM)
    return pl.pallas_call(
        finish_kernel,
        out_shape=jax.ShapeDtypeStruct(flux_in.shape, jnp.float32),
        in_specs=[
            pl.BlockSpec(memory_space=pltpu.SMEM),
            vmem,
            pl.BlockSpec(memory_space=pl.ANY),
            vmem,
        ],
        out_specs=vmem,
        scratch_shapes=[
            pltpu.VMEM(table.shape, jnp.bfloat16),
            pltpu.VMEM((LINE - 1, 32, 1024), jnp.bfloat16),
            pltpu.VMEM((8, 32, 128), jnp.float32),
            pltpu.SemaphoreType.DMA,
            pltpu.SemaphoreType.DMA((LINE - 1,)),
            pltpu.SemaphoreType.DMA((LINE - 1,)),
        ],
        compiler_params=pltpu.CompilerParams(
            collective_id=1, has_side_effects=True, vmem_limit_bytes=16 << 20
        ),
    )(cells, partial, table, flux_in)


def body(
    field_in,
    source,
    cell_factor,
    layer_material,
    material_scale,
    panel_cell,
    panel_pos,
    panel_area,
    flux_in,
    pair_list,
):
    me = lax.axis_index("dev")
    m, r = me // LINE, me % LINE

    flux_half = flux_in.astype(jnp.bfloat16).reshape(32, LINE, 128).transpose(1, 0, 2)
    own_list = jnp.pad(pair_list.astype(jnp.bfloat16).reshape(1, 32), ((0, 0), (0, 96)))
    in_row = jnp.arange(16, dtype=jnp.int32)[:, None] == r
    own_list = jnp.where(in_row, own_list, jnp.zeros_like(own_list))
    own_list = jnp.broadcast_to(own_list, (LINE, 16, 128))
    edge = [
        [
            field_in[:, :, at : at + 2].reshape(-1, 128),
            source[:, :, one].reshape(-1, 128),
            cell_factor[:, one].reshape(-1, 128),
        ]
        for at, one in ((2, 3), (0, 0))
    ]
    edge = jnp.stack([jnp.concatenate(side, axis=0) for side in edge], axis=0)
    rows, halo = exchange(jnp.concatenate([flux_half, own_list], axis=1), edge)

    pairs = rows[:, 256:264, 0:32].reshape(-1, 2)
    tile_ids = jnp.arange(TILES, dtype=jnp.bfloat16)
    upper = (pairs[:, 0:1] == tile_ids[None, :]).astype(jnp.bfloat16)
    lower = (pairs[:, 1:2] == tile_ids[None, :]).astype(jnp.bfloat16)
    listed = lax.dot_general(
        upper, lower, (((0,), (0,)), ((), ())), preferred_element_type=jnp.float32
    )
    listed = (listed + listed.T > 0.0).astype(jnp.int32)
    mask = lax.dynamic_slice(listed, (4 * m, 0), (4, TILES)).reshape(-1)

    row_pos = lax.dynamic_index_in_dim(panel_pos.reshape(3, 128, LINE, 128), r, 2, False)
    row_area = lax.dynamic_index_in_dim(panel_area.reshape(128, LINE, 128), r, 1, False)
    row_features = features(row_pos.reshape(3, -1), row_area.reshape(-1), True)
    row_features = row_features.reshape(32, TILES, 256).transpose(1, 2, 0)
    col_features = features(
        lax.dynamic_slice(panel_pos, (0, m * COLS), (3, COLS)),
        lax.dynamic_slice(panel_area, (m * COLS,), (COLS,)),
        False,
    )

    inner = jnp.array([me > 0, me < LINE * PLANE - 1])
    halo = jnp.where(inner[:, None, None], halo, 0.0)
    halo_field = halo[:, 0:512].reshape(2, 32, LAYERS, 2, 128)
    halo_source = halo[:, 512:768].reshape(2, 32, LAYERS, 1, 128)
    halo_factor = halo[:, 768:776].reshape(2, LAYERS, 1, 128)
    wide_field = jnp.concatenate([halo_field[0], field_in, halo_field[1]], axis=2)
    wide_source = jnp.concatenate([halo_source[0], source, halo_source[1]], axis=2)
    wide_factor = jnp.concatenate([halo_factor[0], cell_factor, halo_factor[1]], axis=1)
    conduct = coefficient(wide_factor, layer_material, material_scale)
    once = relax_rows(wide_field, wide_source, conduct)
    place = jnp.arange(6, dtype=jnp.int32)[:, None]
    kept = ((place > 0) | inner[0]) & ((place < 5) | inner[1])
    once = jnp.where(kept, once, 0.0)
    field_now = relax_rows(once, source, conduct[:, 1:-1])
    surface_top = field_now[:, -1].astype(jnp.bfloat16).transpose(1, 0, 2)
    table = lax.all_gather(surface_top, "dev", axis=0, tiled=True)

    partial = apply_pairs(mask, rows, row_features, col_features)
    flux_out = finish(panel_cell, partial, table, flux_in)
    return (field_now, flux_out)


def solution(mesh):
    in_specs = (
        P(None, None, "dev", None),
        P(None, None, "dev", None),
        P(None, "dev", None),
        P(),
        P(),
        P("dev"),
        P(),
        P(),
        P(None, "dev"),
        P("dev", None),
    )
    out_specs = (P(None, None, "dev", None), P(None, "dev"))
    return jax.shard_map(body, mesh=mesh, in_specs=in_specs, out_specs=out_specs, check_vma=False)
```

```python
import math

import jax
import jax.numpy as jnp
from jax import lax
from jax.experimental import pallas as pl
from jax.experimental.pallas import tpu as pltpu
from jax.sharding import PartitionSpec as P

TILE = 2048
TILES = 64
LAYERS = 8
UNROLL = 4
LINE = 8
PLANE = 16
COLS = 4 * TILE

softening = 0.0004
relax_rate = 0.8
update_rate = 0.5
kernel_gain = 0.25


def coefficient(cell_factor, layer_material, material_scale):
    matched = (
        layer_material[:, None] == jnp.arange(material_scale.shape[0], dtype=jnp.int32)[None, :]
    )
    layer_scale = jnp.sum(jnp.where(matched, material_scale[None, :], 0.0), axis=1)
    return layer_scale[:, None, None] * cell_factor


def relax_rows(widened, source, conduct):
    centre = widened[:, :, 1:-1, :]
    padded = jnp.pad(centre, ((0, 0), (1, 1), (0, 0), (1, 1)))
    beside = (
        padded[:, 2:, :, 1:-1]
        + padded[:, :-2, :, 1:-1]
        + (widened[:, :, 2:, :] + widened[:, :, :-2, :])
        + (padded[:, 1:-1, :, 2:] + padded[:, 1:-1, :, :-2])
    )
    applied = conduct * (6.0 * centre - beside) + centre
    return centre + relax_rate * (source - applied) / (6.0 * conduct + 1.0)


def pair_kernel(mask_ref, f_ref, pt_ref, q_ref, o_ref, total_ref, held_ref, order_ref):
    order_ref[0] = 0

    def note(at, count):
        order_ref[count + 1] = at
        return count + mask_ref[at]

    count = lax.fori_loop(0, 4 * TILES, note, jnp.int32(0))
    for u in range(UNROLL + 1):
        order_ref[count + 1 + u] = 0
    total_ref[...] = jnp.zeros(total_ref.shape, jnp.float32)
    held_ref[1] = jnp.zeros((256, TILE), jnp.bfloat16)

    def step(b, carry):
        for u in range(UNROLL):
            t = b * UNROLL + u
            new, old = order_ref[t + 1], order_ref[t]
            valid = (t >= 1) & (t <= count)
            i = old % TILES
            at = pl.multiple_of((i % 4) * 64, 64)
            flux = jnp.concatenate(
                [f_ref[i // 4, pl.ds(at, 32), :], f_ref[i // 4, pl.ds(at + 32, 32), :]], axis=1
            )
            flux = jnp.where(valid, flux, jnp.zeros_like(flux))
            for c in range(4):
                columns = slice(c * 512, (c + 1) * 512)
                distance = jnp.dot(
                    pt_ref[new % TILES],
                    q_ref[new // TILES, :, columns],
                    preferred_element_type=jnp.float32,
                )
                held_ref[u % 2, :, columns] = lax.rsqrt(distance).astype(jnp.bfloat16)
                total_ref[old // TILES, :, columns] += jnp.dot(
                    flux, held_ref[1 - u % 2, :, columns], preferred_element_type=jnp.float32
                )
        return carry

    lax.fori_loop(0, (count + UNROLL) // UNROLL, step, 0)
    for j in range(4):
        for c in range(2):
            o_ref[2 * j + c] = total_ref[j, :, c * 1024 : (c + 1) * 1024].astype(jnp.bfloat16)


def apply_pairs(mask, flux_rows, row_features, col_features):
    vmem = pl.BlockSpec(memory_space=pltpu.VMEM)
    return pl.pallas_call(
        pair_kernel,
        out_shape=jax.ShapeDtypeStruct((LINE, 32, 1024), jnp.bfloat16),
        in_specs=[pl.BlockSpec(memory_space=pltpu.SMEM), vmem, vmem, vmem],
        out_specs=vmem,
        scratch_shapes=[
            pltpu.VMEM((4, 32, TILE), jnp.float32),
            pltpu.VMEM((2, 256, TILE), jnp.bfloat16),
            pltpu.SMEM((4 * TILES + UNROLL + 2,), jnp.int32),
        ],
        compiler_params=pltpu.CompilerParams(vmem_limit_bytes=20 << 20),
        cost_estimate=pl.CostEstimate(
            flops=100_000_000_000, bytes_accessed=8 << 20, transcendentals=0
        ),
    )(mask, flux_rows, row_features, col_features)


def remote(src, dst, sends, recvs, at, device):
    return pltpu.make_async_remote_copy(
        src_ref=src,
        dst_ref=dst,
        send_sem=sends.at[at],
        recv_sem=recvs.at[at],
        device_id=(device,),
        device_id_type=pl.DeviceIdType.MESH,
    )


def greet(devices):
    barrier = pltpu.get_barrier_semaphore()
    for device in devices:
        pl.semaphore_signal(
            barrier, inc=1, device_id=(device,), device_id_type=pl.DeviceIdType.MESH
        )
    pl.semaphore_wait(barrier, len(devices))


def line_kernel(
    flux_ref, edge_ref, stage_ref, halo_ref, shared, line_send, line_recv, edge_send, edge_recv
):
    me = lax.axis_index("dev")
    m, r = me // LINE, lax.rem(me, LINE)
    line = [LINE * m + lax.rem(r + k, LINE) for k in range(1, LINE)]
    after = lax.rem(me + 1, LINE * PLANE)
    before = lax.rem(me + LINE * PLANE - 1, LINE * PLANE)
    greet(line + [after, before])
    edges = [
        remote(edge_ref.at[0], halo_ref.at[0], edge_send, edge_recv, 0, after),
        remote(edge_ref.at[1], halo_ref.at[1], edge_send, edge_recv, 1, before),
    ]
    copies = []
    for k in range(1, LINE):
        there = lax.rem(r + k, LINE)
        copies.append(
            remote(flux_ref.at[there], shared.at[r], line_send, line_recv, k - 1, line[k - 1])
        )
    for copy in edges + copies:
        copy.start()
    shared[r] = flux_ref[r]
    for copy in copies:
        copy.wait()
    lists = jnp.zeros((16, 128), jnp.float32)
    for s in range(LINE):
        stage_ref[32 * s : 32 * s + 32, :] = shared[s, 0:32, :]
        lists = lists + shared[s, 32:48, :].astype(jnp.float32)
    stage_ref[256:272, :] = lists.astype(jnp.bfloat16)
    for copy in edges:
        copy.wait()


def exchange_line(flux, edge):
    vmem = pl.BlockSpec(memory_space=pltpu.VMEM)
    return pl.pallas_call(
        line_kernel,
        out_shape=(
            jax.ShapeDtypeStruct((272, 128), jnp.bfloat16),
            jax.ShapeDtypeStruct(edge.shape, jnp.float32),
        ),
        in_specs=[vmem, vmem],
        out_specs=(vmem, vmem),
        scratch_shapes=[
            pltpu.VMEM((LINE, 48, 128), jnp.bfloat16),
            pltpu.SemaphoreType.DMA((LINE - 1,)),
            pltpu.SemaphoreType.DMA((LINE - 1,)),
            pltpu.SemaphoreType.DMA((2,)),
            pltpu.SemaphoreType.DMA((2,)),
        ],
        compiler_params=pltpu.CompilerParams(
            collective_id=0, has_side_effects=True, vmem_limit_bytes=16 << 20
        ),
    )(flux, edge)


def split3(value):
    high = value.astype(jnp.bfloat16).astype(jnp.float32)
    rest = value - high
    middle = rest.astype(jnp.bfloat16).astype(jnp.float32)
    return high, middle, rest - middle


def factors(pos, area, row_side):
    pos = pos - 0.5
    scale = (math.sqrt(TILE) / kernel_gain) / (area * area)
    norm = pos[0:1] * pos[0:1] + pos[1:2] * pos[1:2] + pos[2:3] * pos[2:3]
    one = jnp.ones_like(norm)
    rest = jnp.zeros((3, norm.shape[1]), jnp.float32)
    if row_side:
        parts = jnp.concatenate([norm + softening, one, -2.0 * pos, rest], axis=0) * scale
    else:
        parts = jnp.concatenate([one, norm, pos, rest], axis=0) * scale
    high, middle, low = split3(parts)
    if row_side:
        return jnp.concatenate([high, high, middle, middle, high, low], axis=0)
    return jnp.concatenate([high, middle, high, middle, low, high], axis=0)


def plane_kernel(
    stage_ref, pos_ref, area_ref, rows_ref, pt_ref, q_ref, plane_send, plane_recv
):
    me = lax.axis_index("dev")
    m, r = me // LINE, lax.rem(me, LINE)
    plane = [LINE * lax.rem(m + k, PLANE) + r for k in range(1, PLANE)]
    greet(plane)
    copies = []
    for k in range(1, PLANE):
        copies.append(
            remote(stage_ref, rows_ref.at[m], plane_send, plane_recv, k - 1, plane[k - 1])
        )
    for copy in copies:
        copy.start()
    rows_ref[m] = stage_ref[...]

    def row_block(half, carry):
        at = pl.multiple_of(half * 1024 + r * 128, 128)
        part = factors(pos_ref[:, pl.ds(at, 128)], area_ref[:, pl.ds(at, 128)], True)
        pt_ref[half] = part.T.astype(jnp.bfloat16)
        return carry

    lax.fori_loop(0, 2 * TILES, row_block, 0)
    for j in range(4):
        for c in range(4):
            at = pl.multiple_of(m * COLS + j * TILE + c * 512, 512)
            part = factors(pos_ref[:, pl.ds(at, 512)], area_ref[:, pl.ds(at, 512)], False)
            q_ref[j, :, c * 512 : (c + 1) * 512] = part.astype(jnp.bfloat16)
    for copy in copies:
        copy.wait()


def exchange_plane(stage, pos, area):
    vmem = pl.BlockSpec(memory_space=pltpu.VMEM)
    return pl.pallas_call(
        plane_kernel,
        out_shape=(
            jax.ShapeDtypeStruct((PLANE, 272, 128), jnp.bfloat16),
            jax.ShapeDtypeStruct((2 * TILES, 128, 48), jnp.bfloat16),
            jax.ShapeDtypeStruct((4, 48, TILE), jnp.bfloat16),
        ),
        in_specs=[vmem, vmem, vmem],
        out_specs=(vmem, vmem, vmem),
        scratch_shapes=[
            pltpu.SemaphoreType.DMA((PLANE - 1,)),
            pltpu.SemaphoreType.DMA((PLANE - 1,)),
        ],
        compiler_params=pltpu.CompilerParams(
            collective_id=2, has_side_effects=True, vmem_limit_bytes=24 << 20
        ),
    )(stage, pos, area)


def finish_kernel(
    cell_ref, part_ref, table_ref, flux_ref, out_ref, table, landed, traces, load_sem, sends, recvs
):
    me = lax.axis_index("dev")
    m, r = me // LINE, lax.rem(me, LINE)
    load = pltpu.make_async_copy(table_ref, table, load_sem)
    load.start()
    line = [LINE * m + lax.rem(r + k, LINE) for k in range(1, LINE)]
    greet(line)
    copies = []
    for k in range(1, LINE):
        there = lax.rem(r + k, LINE)
        copy = remote(part_ref.at[there], landed.at[k - 1], sends, recvs, k - 1, line[k - 1])
        copy.start()
        copies.append(copy)
    load.wait()
    lane = lax.broadcasted_iota(jnp.int32, (32, 128), 1)

    def group(g, carry):
        def pick(step, held):
            for u in range(8):
                at = step * 8 + u
                cell = cell_ref[g * 128 + at]
                block = table[cell // 128].astype(jnp.float32)
                moved = pltpu.roll(block, lax.rem(at + 128 - lax.rem(cell, 128), 128), axis=1)
                held = jnp.where(lane == at, moved, held)
            return held

        traces[g] = lax.fori_loop(0, 16, pick, jnp.zeros((32, 128), jnp.float32))
        return carry

    lax.fori_loop(0, 8, group, 0)
    for copy in copies:
        copy.wait()
    total = part_ref[r].astype(jnp.float32)
    for k in range(LINE - 1):
        total = total + landed[k].astype(jnp.float32)
    for g in range(8):
        at = slice(g * 128, (g + 1) * 128)
        out_ref[:, at] = flux_ref[:, at] + update_rate * (traces[g] - total[:, at])


def finish(cells, partial, table, flux_in):
    vmem = pl.BlockSpec(memory_space=pltpu.VMEM)
    return pl.pallas_call(
        finish_kernel,
        out_shape=jax.ShapeDtypeStruct(flux_in.shape, jnp.float32),
        in_specs=[
            pl.BlockSpec(memory_space=pltpu.SMEM),
            vmem,
            pl.BlockSpec(memory_space=pl.ANY),
            vmem,
        ],
        out_specs=vmem,
        scratch_shapes=[
            pltpu.VMEM(table.shape, jnp.bfloat16),
            pltpu.VMEM((LINE - 1, 32, 1024), jnp.bfloat16),
            pltpu.VMEM((8, 32, 128), jnp.float32),
            pltpu.SemaphoreType.DMA,
            pltpu.SemaphoreType.DMA((LINE - 1,)),
            pltpu.SemaphoreType.DMA((LINE - 1,)),
        ],
        compiler_params=pltpu.CompilerParams(
            collective_id=1, has_side_effects=True, vmem_limit_bytes=16 << 20
        ),
    )(cells, partial, table, flux_in)


def body(
    field_in,
    source,
    cell_factor,
    layer_material,
    material_scale,
    panel_cell,
    panel_pos,
    panel_area,
    flux_in,
    pair_list,
):
    me = lax.axis_index("dev")
    m, r = me // LINE, me % LINE

    flux_half = flux_in.astype(jnp.bfloat16).reshape(32, LINE, 128).transpose(1, 0, 2)
    own_list = jnp.pad(pair_list.astype(jnp.bfloat16).reshape(1, 32), ((0, 0), (0, 96)))
    in_row = jnp.arange(16, dtype=jnp.int32)[:, None] == r
    own_list = jnp.where(in_row, own_list, jnp.zeros_like(own_list))
    own_list = jnp.broadcast_to(own_list, (LINE, 16, 128))
    edge = [
        [
            field_in[:, :, at : at + 2].reshape(-1, 128),
            source[:, :, one].reshape(-1, 128),
            cell_factor[:, one].reshape(-1, 128),
        ]
        for at, one in ((2, 3), (0, 0))
    ]
    edge = jnp.stack([jnp.concatenate(side, axis=0) for side in edge], axis=0)
    stage, halo = exchange_line(jnp.concatenate([flux_half, own_list], axis=1), edge)

    inner = jnp.array([me > 0, me < LINE * PLANE - 1])
    halo = jnp.where(inner[:, None, None], halo, 0.0)
    halo_field = halo[:, 0:512].reshape(2, 32, LAYERS, 2, 128)
    halo_source = halo[:, 512:768].reshape(2, 32, LAYERS, 1, 128)
    halo_factor = halo[:, 768:776].reshape(2, LAYERS, 1, 128)
    wide_field = jnp.concatenate([halo_field[0], field_in, halo_field[1]], axis=2)
    wide_source = jnp.concatenate([halo_source[0], source, halo_source[1]], axis=2)
    wide_factor = jnp.concatenate([halo_factor[0], cell_factor, halo_factor[1]], axis=1)
    conduct = coefficient(wide_factor, layer_material, material_scale)
    once = relax_rows(wide_field, wide_source, conduct)
    place = jnp.arange(6, dtype=jnp.int32)[:, None]
    kept = ((place > 0) | inner[0]) & ((place < 5) | inner[1])
    once = jnp.where(kept, once, 0.0)
    field_now = relax_rows(once, source, conduct[:, 1:-1])
    surface_top = field_now[:, -1].astype(jnp.bfloat16).transpose(1, 0, 2)

    stage, field_now, surface_top = lax.optimization_barrier((stage, field_now, surface_top))
    table = lax.all_gather(surface_top, "dev", axis=0, tiled=True)
    rows, row_features, col_features = exchange_plane(
        stage, panel_pos, panel_area.reshape(1, -1)
    )
    pairs = rows[:, 256:264, 0:32].reshape(-1, 2)
    tile_ids = jnp.arange(TILES, dtype=jnp.bfloat16)
    upper = (pairs[:, 0:1] == tile_ids[None, :]).astype(jnp.bfloat16)
    lower = (pairs[:, 1:2] == tile_ids[None, :]).astype(jnp.bfloat16)
    listed = lax.dot_general(
        upper, lower, (((0,), (0,)), ((), ())), preferred_element_type=jnp.float32
    )
    listed = (listed + listed.T > 0.0).astype(jnp.int32)
    mask = lax.dynamic_slice(listed, (4 * m, 0), (4, TILES)).reshape(-1)

    partial = apply_pairs(mask, rows, row_features.reshape(TILES, 256, 48), col_features)
    flux_out = finish(panel_cell, partial, table, flux_in)
    return (field_now, flux_out)


def solution(mesh):
    in_specs = (
        P(None, None, "dev", None),
        P(None, None, "dev", None),
        P(None, "dev", None),
        P(),
        P(),
        P("dev"),
        P(),
        P(),
        P(None, "dev"),
        P("dev", None),
    )
    out_specs = (P(None, None, "dev", None), P(None, "dev"))
    return jax.shard_map(body, mesh=mesh, in_specs=in_specs, out_specs=out_specs, check_vma=False)
```

```python
import math

import jax
import jax.numpy as jnp
from jax import lax
from jax.experimental import pallas as pl
from jax.experimental.pallas import tpu as pltpu
from jax.sharding import PartitionSpec as P

TILE = 2048
TILES = 64
LAYERS = 8
UNROLL = 4
LINE = 8
PLANE = 16
COLS = 4 * TILE

softening = 0.0004
relax_rate = 0.8
update_rate = 0.5
kernel_gain = 0.25


def coefficient(cell_factor, layer_material, material_scale):
    matched = (
        layer_material[:, None] == jnp.arange(material_scale.shape[0], dtype=jnp.int32)[None, :]
    )
    layer_scale = jnp.sum(jnp.where(matched, material_scale[None, :], 0.0), axis=1)
    return layer_scale[:, None, None] * cell_factor


def relax_rows(widened, source, conduct):
    centre = widened[:, :, 1:-1, :]
    padded = jnp.pad(centre, ((0, 0), (1, 1), (0, 0), (1, 1)))
    beside = (
        padded[:, 2:, :, 1:-1]
        + padded[:, :-2, :, 1:-1]
        + (widened[:, :, 2:, :] + widened[:, :, :-2, :])
        + (padded[:, 1:-1, :, 2:] + padded[:, 1:-1, :, :-2])
    )
    applied = conduct * (6.0 * centre - beside) + centre
    return centre + relax_rate * (source - applied) / (6.0 * conduct + 1.0)


def pair_kernel(mask_ref, f_ref, pt_ref, q_ref, o_ref, total_ref, held_ref, order_ref):
    order_ref[0] = 0

    def note(at, count):
        order_ref[count + 1] = at
        return count + mask_ref[at]

    count = lax.fori_loop(0, 4 * TILES, note, jnp.int32(0))
    for u in range(UNROLL + 1):
        order_ref[count + 1 + u] = 0
    total_ref[...] = jnp.zeros(total_ref.shape, jnp.float32)
    held_ref[1] = jnp.zeros((256, TILE), jnp.bfloat16)

    def step(b, carry):
        for u in range(UNROLL):
            t = b * UNROLL + u
            new, old = order_ref[t + 1], order_ref[t]
            valid = (t >= 1) & (t <= count)
            i = old % TILES
            at = pl.multiple_of((i % 4) * 64, 64)
            flux = jnp.concatenate(
                [f_ref[i // 4, pl.ds(at, 32), :], f_ref[i // 4, pl.ds(at + 32, 32), :]], axis=1
            )
            flux = jnp.where(valid, flux, jnp.zeros_like(flux))
            for c in range(4):
                columns = slice(c * 512, (c + 1) * 512)
                distance = jnp.dot(
                    pt_ref[new % TILES],
                    q_ref[new // TILES, :, columns],
                    preferred_element_type=jnp.float32,
                )
                held_ref[u % 2, :, columns] = lax.rsqrt(distance).astype(jnp.bfloat16)
                total_ref[old // TILES, :, columns] += jnp.dot(
                    flux, held_ref[1 - u % 2, :, columns], preferred_element_type=jnp.float32
                )
        return carry

    lax.fori_loop(0, (count + UNROLL) // UNROLL, step, 0)
    for j in range(4):
        for c in range(2):
            o_ref[2 * j + c] = total_ref[j, :, c * 1024 : (c + 1) * 1024].astype(jnp.bfloat16)


def apply_pairs(mask, flux_rows, row_features, col_features):
    vmem = pl.BlockSpec(memory_space=pltpu.VMEM)
    return pl.pallas_call(
        pair_kernel,
        out_shape=jax.ShapeDtypeStruct((LINE, 32, 1024), jnp.bfloat16),
        in_specs=[pl.BlockSpec(memory_space=pltpu.SMEM), vmem, vmem, vmem],
        out_specs=vmem,
        scratch_shapes=[
            pltpu.VMEM((4, 32, TILE), jnp.float32),
            pltpu.VMEM((2, 256, TILE), jnp.bfloat16),
            pltpu.SMEM((4 * TILES + UNROLL + 2,), jnp.int32),
        ],
        compiler_params=pltpu.CompilerParams(vmem_limit_bytes=20 << 20),
        cost_estimate=pl.CostEstimate(
            flops=100_000_000_000, bytes_accessed=8 << 20, transcendentals=0
        ),
    )(mask, flux_rows, row_features, col_features)


def remote(src, dst, sends, recvs, at, device):
    return pltpu.make_async_remote_copy(
        src_ref=src,
        dst_ref=dst,
        send_sem=sends.at[at],
        recv_sem=recvs.at[at],
        device_id=(device,),
        device_id_type=pl.DeviceIdType.MESH,
    )


def greet(devices):
    barrier = pltpu.get_barrier_semaphore()
    for device in devices:
        pl.semaphore_signal(
            barrier, inc=1, device_id=(device,), device_id_type=pl.DeviceIdType.MESH
        )
    pl.semaphore_wait(barrier, len(devices))


def line_kernel(
    flux_ref,
    list_ref,
    field_ref,
    source_ref,
    factor_ref,
    stage_ref,
    halo_field,
    halo_source,
    halo_factor,
    slices,
    shared,
    edge_field,
    edge_source,
    edge_factor,
    line_send,
    line_recv,
    edge_send,
    edge_recv,
):
    me = lax.axis_index("dev")
    m, r = me // LINE, lax.rem(me, LINE)
    line = [LINE * m + lax.rem(r + k, LINE) for k in range(1, LINE)]
    after = lax.rem(me + 1, LINE * PLANE)
    before = lax.rem(me + LINE * PLANE - 1, LINE * PLANE)
    for side, (at, one, device) in enumerate(((2, 3, after), (0, 0, before))):
        edge_field[side] = field_ref[:, :, at : at + 2, :]
        edge_source[side] = source_ref[:, :, one, :]
        edge_factor[side] = factor_ref[:, one, :]
    own_list = pltpu.roll(list_ref[...], 2 * r, axis=1).astype(jnp.bfloat16)
    for s in range(LINE):
        slices[s, 0:32, :] = flux_ref[:, s * 128 : (s + 1) * 128].astype(jnp.bfloat16)
        slices[s, 32:48, :] = own_list
    greet(line + [after, before])
    edges = []
    for side, device in enumerate((after, before)):
        for which, (src, dst) in enumerate(
            ((edge_field, halo_field), (edge_source, halo_source), (edge_factor, halo_factor))
        ):
            edges.append(
                remote(
                    src.at[side], dst.at[side], edge_send, edge_recv, 3 * side + which, device
                )
            )
    copies = []
    for k in range(1, LINE):
        there = lax.rem(r + k, LINE)
        copies.append(
            remote(slices.at[there], shared.at[r], line_send, line_recv, k - 1, line[k - 1])
        )
    for copy in edges + copies:
        copy.start()
    shared[r] = slices[r]
    for copy in copies:
        copy.wait()
    lists = jnp.zeros((16, 128), jnp.float32)
    for s in range(LINE):
        stage_ref[32 * s : 32 * s + 32, :] = shared[s, 0:32, :]
        lists = lists + shared[s, 32:48, :].astype(jnp.float32)
    stage_ref[256:272, :] = lists.astype(jnp.bfloat16)
    for copy in edges:
        copy.wait()


def exchange_line(flux, lists, field, source, factor):
    vmem = pl.BlockSpec(memory_space=pltpu.VMEM)
    f32 = jnp.float32
    return pl.pallas_call(
        line_kernel,
        out_shape=(
            jax.ShapeDtypeStruct((272, 128), jnp.bfloat16),
            jax.ShapeDtypeStruct((2, 32, LAYERS, 2, 128), f32),
            jax.ShapeDtypeStruct((2, 32, LAYERS, 128), f32),
            jax.ShapeDtypeStruct((2, LAYERS, 128), f32),
        ),
        in_specs=[vmem] * 5,
        out_specs=(vmem,) * 4,
        scratch_shapes=[
            pltpu.VMEM((LINE, 48, 128), jnp.bfloat16),
            pltpu.VMEM((LINE, 48, 128), jnp.bfloat16),
            pltpu.VMEM((2, 32, LAYERS, 2, 128), f32),
            pltpu.VMEM((2, 32, LAYERS, 128), f32),
            pltpu.VMEM((2, LAYERS, 128), f32),
            pltpu.SemaphoreType.DMA((LINE - 1,)),
            pltpu.SemaphoreType.DMA((LINE - 1,)),
            pltpu.SemaphoreType.DMA((6,)),
            pltpu.SemaphoreType.DMA((6,)),
        ],
        compiler_params=pltpu.CompilerParams(
            collective_id=0, has_side_effects=True, vmem_limit_bytes=16 << 20
        ),
    )(flux, lists, field, source, factor)


def split3(value):
    high = value.astype(jnp.bfloat16).astype(jnp.float32)
    rest = value - high
    middle = rest.astype(jnp.bfloat16).astype(jnp.float32)
    return high, middle, rest - middle


def factors(pos, area, row_side):
    pos = pos - 0.5
    scale = (math.sqrt(TILE) / kernel_gain) / (area * area)
    norm = pos[0:1] * pos[0:1] + pos[1:2] * pos[1:2] + pos[2:3] * pos[2:3]
    one = jnp.ones_like(norm)
    rest = jnp.zeros((3, norm.shape[1]), jnp.float32)
    if row_side:
        parts = jnp.concatenate([norm + softening, one, -2.0 * pos, rest], axis=0) * scale
    else:
        parts = jnp.concatenate([one, norm, pos, rest], axis=0) * scale
    high, middle, low = split3(parts)
    if row_side:
        return jnp.concatenate([high, high, middle, middle, high, low], axis=0)
    return jnp.concatenate([high, middle, high, middle, low, high], axis=0)


def plane_kernel(
    stage_ref,
    pos_ref,
    area_ref,
    rows_ref,
    pt_ref,
    q_ref,
    pt_held,
    q_held,
    plane_send,
    plane_recv,
    local,
):
    me = lax.axis_index("dev")
    m, r = me // LINE, lax.rem(me, LINE)
    plane = [LINE * lax.rem(m + k, PLANE) + r for k in range(1, PLANE)]
    greet(plane)
    copies = []
    for k in range(1, PLANE):
        copies.append(
            remote(stage_ref, rows_ref.at[m], plane_send, plane_recv, k - 1, plane[k - 1])
        )
    copies.append(pltpu.make_async_copy(stage_ref, rows_ref.at[m], local.at[0]))
    for copy in copies:
        copy.start()

    def row_block(step, carry):
        for u in range(8):
            half = step * 8 + u
            at = pl.multiple_of(half * 1024 + r * 128, 128)
            part = factors(pos_ref[:, pl.ds(at, 128)], area_ref[:, pl.ds(at, 128)], True)
            pt_held[half] = part.T.astype(jnp.bfloat16)
        return carry

    lax.fori_loop(0, TILES // 4, row_block, 0)
    moves = [pltpu.make_async_copy(pt_held, pt_ref, local.at[1])]
    moves[0].start()
    for j in range(4):
        for c in range(4):
            at = pl.multiple_of(m * COLS + j * TILE + c * 512, 512)
            part = factors(pos_ref[:, pl.ds(at, 512)], area_ref[:, pl.ds(at, 512)], False)
            q_held[j, :, c * 512 : (c + 1) * 512] = part.astype(jnp.bfloat16)
    moves.append(pltpu.make_async_copy(q_held, q_ref, local.at[2]))
    moves[1].start()
    for copy in copies + moves:
        copy.wait()


def exchange_plane(stage, pos, area):
    vmem = pl.BlockSpec(memory_space=pltpu.VMEM)
    hbm = pl.BlockSpec(memory_space=pltpu.HBM)
    row_shape, col_shape = (2 * TILES, 128, 48), (4, 48, TILE)
    return pl.pallas_call(
        plane_kernel,
        out_shape=(
            jax.ShapeDtypeStruct((PLANE, 272, 128), jnp.bfloat16),
            jax.ShapeDtypeStruct(row_shape, jnp.bfloat16),
            jax.ShapeDtypeStruct(col_shape, jnp.bfloat16),
        ),
        in_specs=[vmem, vmem, vmem],
        out_specs=(hbm, hbm, hbm),
        scratch_shapes=[
            pltpu.VMEM(row_shape, jnp.bfloat16),
            pltpu.VMEM(col_shape, jnp.bfloat16),
            pltpu.SemaphoreType.DMA((PLANE - 1,)),
            pltpu.SemaphoreType.DMA((PLANE - 1,)),
            pltpu.SemaphoreType.DMA((3,)),
        ],
        compiler_params=pltpu.CompilerParams(
            collective_id=2, has_side_effects=True, vmem_limit_bytes=24 << 20
        ),
    )(stage, pos, area)


def finish_kernel(
    cell_ref, part_ref, table_ref, flux_ref, out_ref, table, landed, traces, load_sem, sends, recvs
):
    me = lax.axis_index("dev")
    m, r = me // LINE, lax.rem(me, LINE)
    load = pltpu.make_async_copy(table_ref, table, load_sem)
    load.start()
    line = [LINE * m + lax.rem(r + k, LINE) for k in range(1, LINE)]
    greet(line)
    copies = []
    for k in range(1, LINE):
        there = lax.rem(r + k, LINE)
        copy = remote(part_ref.at[there], landed.at[k - 1], sends, recvs, k - 1, line[k - 1])
        copy.start()
        copies.append(copy)
    load.wait()
    lane = lax.broadcasted_iota(jnp.int32, (32, 128), 1)

    def group(g, carry):
        def pick(step, held):
            for u in range(16):
                at = step * 16 + u
                cell = cell_ref[g * 128 + at]
                block = table[lax.shift_right_logical(cell, 7)].astype(jnp.float32)
                moved = pltpu.roll(block, (at - cell) & 127, axis=1)
                held = jnp.where(lane == at, moved, held)
            return held

        traces[g] = lax.fori_loop(0, 8, pick, jnp.zeros((32, 128), jnp.float32))
        return carry

    lax.fori_loop(0, 8, group, 0)
    for copy in copies:
        copy.wait()
    total = part_ref[r].astype(jnp.float32)
    for k in range(LINE - 1):
        total = total + landed[k].astype(jnp.float32)
    for g in range(8):
        at = slice(g * 128, (g + 1) * 128)
        out_ref[:, at] = flux_ref[:, at] + update_rate * (traces[g] - total[:, at])


def finish(cells, partial, table, flux_in):
    vmem = pl.BlockSpec(memory_space=pltpu.VMEM)
    return pl.pallas_call(
        finish_kernel,
        out_shape=jax.ShapeDtypeStruct(flux_in.shape, jnp.float32),
        in_specs=[
            pl.BlockSpec(memory_space=pltpu.SMEM),
            vmem,
            pl.BlockSpec(memory_space=pltpu.HBM),
            vmem,
        ],
        out_specs=vmem,
        scratch_shapes=[
            pltpu.VMEM(table.shape, jnp.bfloat16),
            pltpu.VMEM((LINE - 1, 32, 1024), jnp.bfloat16),
            pltpu.VMEM((8, 32, 128), jnp.float32),
            pltpu.SemaphoreType.DMA,
            pltpu.SemaphoreType.DMA((LINE - 1,)),
            pltpu.SemaphoreType.DMA((LINE - 1,)),
        ],
        compiler_params=pltpu.CompilerParams(
            collective_id=1, has_side_effects=True, vmem_limit_bytes=16 << 20
        ),
    )(cells, partial, table, flux_in)


def body(
    field_in,
    source,
    cell_factor,
    layer_material,
    material_scale,
    panel_cell,
    panel_pos,
    panel_area,
    flux_in,
    pair_list,
):
    me = lax.axis_index("dev")
    m, r = me // LINE, me % LINE

    lists = jnp.pad(pair_list.astype(jnp.float32), ((0, 0), (0, 126)))
    stage, halo_field, halo_source, halo_factor = exchange_line(
        flux_in, lists, field_in, source, cell_factor
    )

    inner = jnp.array([me > 0, me < LINE * PLANE - 1])
    halo_field = jnp.where(inner.reshape(2, 1, 1, 1, 1), halo_field, 0.0)
    halo_source = halo_source[:, :, :, None]
    halo_factor = halo_factor[:, :, None]
    wide_field = jnp.concatenate([halo_field[0], field_in, halo_field[1]], axis=2)
    wide_source = jnp.concatenate([halo_source[0], source, halo_source[1]], axis=2)
    wide_factor = jnp.concatenate([halo_factor[0], cell_factor, halo_factor[1]], axis=1)
    conduct = coefficient(wide_factor, layer_material, material_scale)
    once = relax_rows(wide_field, wide_source, conduct)
    place = jnp.arange(6, dtype=jnp.int32)[:, None]
    kept = ((place > 0) | inner[0]) & ((place < 5) | inner[1])
    once = jnp.where(kept, once, 0.0)
    field_now = relax_rows(once, source, conduct[:, 1:-1])
    surface_top = field_now[:, -1].astype(jnp.bfloat16).transpose(1, 0, 2)

    stage, surface_top = lax.optimization_barrier((stage, surface_top))
    table = lax.all_gather(surface_top, "dev", axis=0, tiled=True)
    rows, row_features, col_features = exchange_plane(
        stage, panel_pos, panel_area.reshape(1, -1)
    )
    pairs = rows[:, 256:272, 0:16].reshape(-1, 2)
    tile_ids = jnp.arange(TILES, dtype=jnp.bfloat16)
    upper = (pairs[:, 0:1] == tile_ids[None, :]).astype(jnp.bfloat16)
    lower = (pairs[:, 1:2] == tile_ids[None, :]).astype(jnp.bfloat16)
    listed = lax.dot_general(
        upper, lower, (((0,), (0,)), ((), ())), preferred_element_type=jnp.float32
    )
    listed = (listed + listed.T > 0.0).astype(jnp.int32)
    mask = lax.dynamic_slice(listed, (4 * m, 0), (4, TILES)).reshape(-1)

    partial = apply_pairs(mask, rows, row_features.reshape(TILES, 256, 48), col_features)
    flux_out = finish(panel_cell, partial, table, flux_in)
    return (field_now, flux_out)


def solution(mesh):
    in_specs = (
        P(None, None, "dev", None),
        P(None, None, "dev", None),
        P(None, "dev", None),
        P(),
        P(),
        P("dev"),
        P(),
        P(),
        P(None, "dev"),
        P("dev", None),
    )
    out_specs = (P(None, None, "dev", None), P(None, "dev"))
    return jax.shard_map(body, mesh=mesh, in_specs=in_specs, out_specs=out_specs, check_vma=False)
```

```python
import math

import jax
import jax.numpy as jnp
from jax import lax
from jax.experimental import pallas as pl
from jax.experimental.pallas import tpu as pltpu
from jax.sharding import PartitionSpec as P

TILE = 2048
TILES = 64
LAYERS = 8
UNROLL = 4
WIDE = (63 << 20) + (1 << 19)
LINE = 8
PLANE = 16
COLS = 4 * TILE

softening = 0.0004
relax_rate = 0.8
update_rate = 0.5
kernel_gain = 0.25


def coefficient(cell_factor, layer_material, material_scale):
    matched = (
        layer_material[:, None] == jnp.arange(material_scale.shape[0], dtype=jnp.int32)[None, :]
    )
    layer_scale = jnp.sum(jnp.where(matched, material_scale[None, :], 0.0), axis=1)
    return layer_scale[:, None, None] * cell_factor


def sweep_kernel(
    field_ref, source_ref, conduct_ref, halo_field, halo_source, halo_conduct, out_ref, top_ref, tops
):
    me = lax.axis_index("dev")
    row = lax.broadcasted_iota(jnp.int32, (LAYERS, 8, 128), 1)
    lane = lax.broadcasted_iota(jnp.int32, (LAYERS, 8, 128), 2)
    real = ((row >= 2) | (me > 0)) & ((row < 6) | (me < LINE * PLANE - 1))
    pad = jnp.zeros((LAYERS, 1, 128), jnp.float32)
    conduct = jnp.concatenate(
        [pad, halo_conduct[0][:, None], conduct_ref[...], halo_conduct[1][:, None], pad], axis=1
    )
    step = relax_rate / (6.0 * conduct + 1.0)
    layer = jnp.zeros((1, 8, 128), jnp.float32)

    def relax(field, source):
        above = jnp.concatenate([field[1:], layer], axis=0)
        below = jnp.concatenate([layer, field[:-1]], axis=0)
        flat = field.reshape(LAYERS * 8, 128)
        right = jnp.where(lane < 127, pltpu.roll(flat, 127, axis=1).reshape(field.shape), 0.0)
        left = jnp.where(lane > 0, pltpu.roll(flat, 1, axis=1).reshape(field.shape), 0.0)
        ahead = pltpu.roll(field, 7, axis=1)
        behind = pltpu.roll(field, 1, axis=1)
        beside = (above + below) + (ahead + behind) + (right + left)
        applied = conduct * (6.0 * field - beside) + field
        return field + step * (source - applied)

    def one_load(load, carry):
        field = jnp.concatenate(
            [halo_field[0, load], field_ref[load], halo_field[1, load]], axis=1
        )
        field = jnp.where(real, field, 0.0)
        source = jnp.concatenate(
            [
                pad,
                halo_source[0, load][:, None],
                source_ref[load],
                halo_source[1, load][:, None],
                pad,
            ],
            axis=1,
        )
        field = jnp.where(real, relax(field, source), 0.0)
        field = relax(field, source)
        out_ref[load] = field[:, 2:6]
        tops[load] = field[LAYERS - 1, 2:6]
        return carry

    lax.fori_loop(0, 32, one_load, 0, unroll=2)
    for x in range(4):
        top_ref[x] = tops[:, x, :].astype(jnp.bfloat16)


def sweeps(*args):
    vmem = pl.BlockSpec(memory_space=pltpu.VMEM)
    return pl.pallas_call(
        sweep_kernel,
        out_shape=(
            jax.ShapeDtypeStruct((32, LAYERS, 4, 128), jnp.float32),
            jax.ShapeDtypeStruct((4, 32, 128), jnp.bfloat16),
        ),
        in_specs=[vmem] * len(args),
        out_specs=(vmem, vmem),
        scratch_shapes=[pltpu.VMEM((32, 4, 128), jnp.float32)],
        compiler_params=pltpu.CompilerParams(vmem_limit_bytes=16 << 20),
    )(*args)


def pair_kernel(
    mask_ref, f_far, pt_far, q_far, o_ref, f_ref, pt_ref, q_ref, total_ref, held_ref, order_ref, sems
):
    loads = [
        pltpu.make_async_copy(far, near, sems.at[at])
        for at, (far, near) in enumerate(((f_far, f_ref), (pt_far, pt_ref), (q_far, q_ref)))
    ]
    for load in loads:
        load.start()
    order_ref[0] = 0

    def note(at, count):
        order_ref[count + 1] = at
        return count + mask_ref[at]

    count = lax.fori_loop(0, 4 * TILES, note, jnp.int32(0))
    for u in range(UNROLL + 1):
        order_ref[count + 1 + u] = 0
    total_ref[...] = jnp.zeros(total_ref.shape, jnp.float32)
    held_ref[1] = jnp.zeros((256, TILE), jnp.bfloat16)
    for load in loads:
        load.wait()

    def step(b, carry):
        for u in range(UNROLL):
            t = b * UNROLL + u
            new, old = order_ref[t + 1], order_ref[t]
            valid = (t >= 1) & (t <= count)
            i = old % TILES
            at = pl.multiple_of((i % 4) * 64, 64)
            flux = jnp.concatenate(
                [f_ref[i // 4, pl.ds(at, 32), :], f_ref[i // 4, pl.ds(at + 32, 32), :]], axis=1
            )
            flux = jnp.where(valid, flux, jnp.zeros_like(flux))
            for c in range(4):
                columns = slice(c * 512, (c + 1) * 512)
                distance = jnp.dot(
                    pt_ref[new % TILES],
                    q_ref[new // TILES, :, columns],
                    preferred_element_type=jnp.float32,
                )
                held_ref[u % 2, :, columns] = lax.rsqrt(distance).astype(jnp.bfloat16)
                total_ref[old // TILES, :, columns] += jnp.dot(
                    flux, held_ref[1 - u % 2, :, columns], preferred_element_type=jnp.float32
                )
        return carry

    lax.fori_loop(0, (count + UNROLL) // UNROLL, step, 0)
    for j in range(4):
        for c in range(2):
            o_ref[2 * j + c] = total_ref[j, :, c * 1024 : (c + 1) * 1024].astype(jnp.bfloat16)


def apply_pairs(mask, flux_rows, row_features, col_features):
    hbm = pl.BlockSpec(memory_space=pltpu.HBM)
    return pl.pallas_call(
        pair_kernel,
        out_shape=jax.ShapeDtypeStruct((LINE, 32, 1024), jnp.bfloat16),
        in_specs=[pl.BlockSpec(memory_space=pltpu.SMEM), hbm, hbm, hbm],
        out_specs=pl.BlockSpec(memory_space=pltpu.VMEM),
        scratch_shapes=[
            pltpu.VMEM(flux_rows.shape, jnp.bfloat16),
            pltpu.VMEM(row_features.shape, jnp.bfloat16),
            pltpu.VMEM(col_features.shape, jnp.bfloat16),
            pltpu.VMEM((4, 32, TILE), jnp.float32),
            pltpu.VMEM((2, 256, TILE), jnp.bfloat16),
            pltpu.SMEM((4 * TILES + UNROLL + 2,), jnp.int32),
            pltpu.SemaphoreType.DMA((3,)),
        ],
        compiler_params=pltpu.CompilerParams(vmem_limit_bytes=WIDE),
        cost_estimate=pl.CostEstimate(
            flops=100_000_000_000, bytes_accessed=8 << 20, transcendentals=0
        ),
    )(mask, flux_rows, row_features, col_features)


def remote(src, dst, sends, recvs, at, device):
    return pltpu.make_async_remote_copy(
        src_ref=src,
        dst_ref=dst,
        send_sem=sends.at[at],
        recv_sem=recvs.at[at],
        device_id=(device,),
        device_id_type=pl.DeviceIdType.MESH,
    )


def greet(devices):
    barrier = pltpu.get_barrier_semaphore()
    for device in devices:
        pl.semaphore_signal(
            barrier, inc=1, device_id=(device,), device_id_type=pl.DeviceIdType.MESH
        )
    pl.semaphore_wait(barrier, len(devices))


def line_kernel(
    flux_ref,
    list_ref,
    field_ref,
    source_ref,
    factor_ref,
    stage_ref,
    halo_field,
    halo_source,
    halo_factor,
    slices,
    shared,
    edge_field,
    edge_source,
    edge_factor,
    line_send,
    line_recv,
    edge_send,
    edge_recv,
):
    me = lax.axis_index("dev")
    m, r = me // LINE, lax.rem(me, LINE)
    line = [LINE * m + lax.rem(r + k, LINE) for k in range(1, LINE)]
    after = lax.rem(me + 1, LINE * PLANE)
    before = lax.rem(me + LINE * PLANE - 1, LINE * PLANE)
    for side, (at, one, device) in enumerate(((2, 3, after), (0, 0, before))):
        edge_field[side] = field_ref[:, :, at : at + 2, :]
        edge_source[side] = source_ref[:, :, one, :]
        edge_factor[side] = factor_ref[:, one, :]
    own_list = pltpu.roll(list_ref[...], 2 * r, axis=1).astype(jnp.bfloat16)
    for s in range(LINE):
        slices[s, 0:32, :] = flux_ref[:, s * 128 : (s + 1) * 128].astype(jnp.bfloat16)
        slices[s, 32:48, :] = own_list
    greet(line + [after, before])
    edges = []
    for side, device in enumerate((after, before)):
        for which, (src, dst) in enumerate(
            ((edge_field, halo_field), (edge_source, halo_source), (edge_factor, halo_factor))
        ):
            edges.append(
                remote(
                    src.at[side], dst.at[side], edge_send, edge_recv, 3 * side + which, device
                )
            )
    copies = []
    for k in range(1, LINE):
        there = lax.rem(r + k, LINE)
        copies.append(
            remote(slices.at[there], shared.at[r], line_send, line_recv, k - 1, line[k - 1])
        )
    for copy in edges + copies:
        copy.start()
    shared[r] = slices[r]
    for copy in copies:
        copy.wait()
    lists = jnp.zeros((16, 128), jnp.float32)
    for s in range(LINE):
        stage_ref[32 * s : 32 * s + 32, :] = shared[s, 0:32, :]
        lists = lists + shared[s, 32:48, :].astype(jnp.float32)
    stage_ref[256:272, :] = lists.astype(jnp.bfloat16)
    for copy in edges:
        copy.wait()


def exchange_line(flux, lists, field, source, factor):
    vmem = pl.BlockSpec(memory_space=pltpu.VMEM)
    f32 = jnp.float32
    return pl.pallas_call(
        line_kernel,
        out_shape=(
            jax.ShapeDtypeStruct((272, 128), jnp.bfloat16),
            jax.ShapeDtypeStruct((2, 32, LAYERS, 2, 128), f32),
            jax.ShapeDtypeStruct((2, 32, LAYERS, 128), f32),
            jax.ShapeDtypeStruct((2, LAYERS, 128), f32),
        ),
        in_specs=[vmem] * 5,
        out_specs=(vmem,) * 4,
        scratch_shapes=[
            pltpu.VMEM((LINE, 48, 128), jnp.bfloat16),
            pltpu.VMEM((LINE, 48, 128), jnp.bfloat16),
            pltpu.VMEM((2, 32, LAYERS, 2, 128), f32),
            pltpu.VMEM((2, 32, LAYERS, 128), f32),
            pltpu.VMEM((2, LAYERS, 128), f32),
            pltpu.SemaphoreType.DMA((LINE - 1,)),
            pltpu.SemaphoreType.DMA((LINE - 1,)),
            pltpu.SemaphoreType.DMA((6,)),
            pltpu.SemaphoreType.DMA((6,)),
        ],
        compiler_params=pltpu.CompilerParams(
            collective_id=0, has_side_effects=True, vmem_limit_bytes=16 << 20
        ),
    )(flux, lists, field, source, factor)


def split3(value):
    high = value.astype(jnp.bfloat16).astype(jnp.float32)
    rest = value - high
    middle = rest.astype(jnp.bfloat16).astype(jnp.float32)
    return high, middle, rest - middle


def factors(pos, area, row_side):
    pos = pos - 0.5
    scale = (math.sqrt(TILE) / kernel_gain) / (area * area)
    norm = pos[0:1] * pos[0:1] + pos[1:2] * pos[1:2] + pos[2:3] * pos[2:3]
    one = jnp.ones_like(norm)
    rest = jnp.zeros((3, norm.shape[1]), jnp.float32)
    if row_side:
        parts = jnp.concatenate([norm + softening, one, -2.0 * pos, rest], axis=0) * scale
    else:
        parts = jnp.concatenate([one, norm, pos, rest], axis=0) * scale
    high, middle, low = split3(parts)
    if row_side:
        return jnp.concatenate([high, high, middle, middle, high, low], axis=0)
    return jnp.concatenate([high, middle, high, middle, low, high], axis=0)


def plane_kernel(
    stage_ref,
    pos_far,
    area_far,
    rows_ref,
    pt_ref,
    q_ref,
    pos_ref,
    area_ref,
    pt_held,
    q_held,
    plane_send,
    plane_recv,
    local,
):
    me = lax.axis_index("dev")
    m, r = me // LINE, lax.rem(me, LINE)
    y, x = m // 4, lax.rem(m, 4)
    loads = [
        pltpu.make_async_copy(pos_far, pos_ref, local.at[3]),
        pltpu.make_async_copy(area_far, area_ref, local.at[4]),
    ]
    def row_block(step, carry):
        for u in range(8):
            half = step * 8 + u
            at = pl.multiple_of(half * 1024 + r * 128, 128)
            part = factors(pos_ref[:, pl.ds(at, 128)], area_ref[:, pl.ds(at, 128)], True)
            pt_held[half] = part.T.astype(jnp.bfloat16)
        return carry

    along_x = [LINE * (4 * y + lax.rem(x + k, 4)) + r for k in range(1, 4)]
    along_y = [LINE * (4 * lax.rem(y + k, 4) + x) + r for k in range(1, 4)]
    own = pltpu.make_async_copy(stage_ref, rows_ref.at[y, x], local.at[0])
    for copy in loads + [own]:
        copy.start()
    greet(along_x + along_y)
    one, two = slice(0, 128), slice(128, 272)
    near, far = [], []
    for k in range(3):
        near.append(
            remote(
                stage_ref.at[one], rows_ref.at[y, x, one], plane_send, plane_recv, k, along_x[k]
            )
        )
        near.append(
            remote(
                stage_ref.at[two], rows_ref.at[y, x, two], plane_send, plane_recv, 3 + k, along_y[k]
            )
        )
        part = rows_ref.at[y, :, one]
        far.append(remote(part, part, plane_send, plane_recv, 6 + k, along_y[k]))
        part = rows_ref.at[:, x, two]
        far.append(remote(part, part, plane_send, plane_recv, 9 + k, along_x[k]))
    for copy in near:
        copy.start()
    for load in loads:
        load.wait()
    lax.fori_loop(0, 6, row_block, 0)
    own.wait()
    for copy in near:
        copy.wait()
    for copy in far:
        copy.start()
    lax.fori_loop(6, TILES // 4, row_block, 0)
    moves = [pltpu.make_async_copy(pt_held, pt_ref, local.at[1])]
    moves[0].start()
    for j in range(4):
        for c in range(4):
            at = pl.multiple_of(m * COLS + j * TILE + c * 512, 512)
            part = factors(pos_ref[:, pl.ds(at, 512)], area_ref[:, pl.ds(at, 512)], False)
            q_held[j, :, c * 512 : (c + 1) * 512] = part.astype(jnp.bfloat16)
    moves.append(pltpu.make_async_copy(q_held, q_ref, local.at[2]))
    moves[1].start()
    for copy in far + moves:
        copy.wait()


def exchange_plane(stage, pos, area):
    vmem = pl.BlockSpec(memory_space=pltpu.VMEM)
    hbm = pl.BlockSpec(memory_space=pltpu.HBM)
    row_shape, col_shape = (2 * TILES, 128, 48), (4, 48, TILE)
    return pl.pallas_call(
        plane_kernel,
        out_shape=(
            jax.ShapeDtypeStruct((4, 4, 272, 128), jnp.bfloat16),
            jax.ShapeDtypeStruct(row_shape, jnp.bfloat16),
            jax.ShapeDtypeStruct(col_shape, jnp.bfloat16),
        ),
        in_specs=[vmem, hbm, hbm],
        out_specs=(hbm, hbm, hbm),
        scratch_shapes=[
            pltpu.VMEM(pos.shape, jnp.float32),
            pltpu.VMEM(area.shape, jnp.float32),
            pltpu.VMEM(row_shape, jnp.bfloat16),
            pltpu.VMEM(col_shape, jnp.bfloat16),
            pltpu.SemaphoreType.DMA((12,)),
            pltpu.SemaphoreType.DMA((12,)),
            pltpu.SemaphoreType.DMA((5,)),
        ],
        compiler_params=pltpu.CompilerParams(
            collective_id=2, has_side_effects=True, vmem_limit_bytes=WIDE
        ),
    )(stage, pos, area)


def finish_kernel(
    cell_ref, part_ref, table_ref, flux_ref, out_ref, table, landed, traces, load_sem, sends, recvs
):
    me = lax.axis_index("dev")
    m, r = me // LINE, lax.rem(me, LINE)
    load = pltpu.make_async_copy(table_ref, table, load_sem)
    load.start()
    line = [LINE * m + lax.rem(r + k, LINE) for k in range(1, LINE)]
    greet(line)
    copies = []
    for k in range(1, LINE):
        there = lax.rem(r + k, LINE)
        copy = remote(part_ref.at[there], landed.at[k - 1], sends, recvs, k - 1, line[k - 1])
        copy.start()
        copies.append(copy)
    load.wait()
    lane = lax.broadcasted_iota(jnp.int32, (32, 128), 1)

    def group(g, carry):
        def pick(step, held):
            for u in range(16):
                at = step * 16 + u
                cell = cell_ref[g * 128 + at]
                block = table[lax.shift_right_logical(cell, 7)].astype(jnp.float32)
                moved = pltpu.roll(block, (at - cell) & 127, axis=1)
                held = jnp.where(lane == at, moved, held)
            return held

        traces[g] = lax.fori_loop(0, 8, pick, jnp.zeros((32, 128), jnp.float32))
        return carry

    lax.fori_loop(0, 8, group, 0)
    for copy in copies:
        copy.wait()
    total = part_ref[r].astype(jnp.float32)
    for k in range(LINE - 1):
        total = total + landed[k].astype(jnp.float32)
    for g in range(8):
        at = slice(g * 128, (g + 1) * 128)
        out_ref[:, at] = flux_ref[:, at] + update_rate * (traces[g] - total[:, at])


def finish(cells, partial, table, flux_in):
    vmem = pl.BlockSpec(memory_space=pltpu.VMEM)
    return pl.pallas_call(
        finish_kernel,
        out_shape=jax.ShapeDtypeStruct(flux_in.shape, jnp.float32),
        in_specs=[
            pl.BlockSpec(memory_space=pltpu.SMEM),
            vmem,
            pl.BlockSpec(memory_space=pltpu.HBM),
            vmem,
        ],
        out_specs=vmem,
        scratch_shapes=[
            pltpu.VMEM(table.shape, jnp.bfloat16),
            pltpu.VMEM((LINE - 1, 32, 1024), jnp.bfloat16),
            pltpu.VMEM((8, 32, 128), jnp.float32),
            pltpu.SemaphoreType.DMA,
            pltpu.SemaphoreType.DMA((LINE - 1,)),
            pltpu.SemaphoreType.DMA((LINE - 1,)),
        ],
        compiler_params=pltpu.CompilerParams(
            collective_id=1, has_side_effects=True, vmem_limit_bytes=WIDE
        ),
    )(cells, partial, table, flux_in)


def body(
    field_in,
    source,
    cell_factor,
    layer_material,
    material_scale,
    panel_cell,
    panel_pos,
    panel_area,
    flux_in,
    pair_list,
):
    me = lax.axis_index("dev")
    m = me // LINE

    lists = jnp.pad(pair_list.astype(jnp.float32), ((0, 0), (0, 126)))
    conduct = coefficient(cell_factor, layer_material, material_scale)
    stage, *halos = exchange_line(flux_in, lists, field_in, source, conduct)
    field_now, surface_top = sweeps(field_in, source, conduct, *halos)
    stage, surface_top = lax.optimization_barrier((stage, surface_top))
    table = lax.all_gather(surface_top, "dev", axis=0, tiled=True)
    rows, row_features, col_features = exchange_plane(
        stage, panel_pos, panel_area.reshape(1, -1)
    )
    rows = rows.reshape(PLANE, 272, 128)
    pairs = rows[:, 256:272, 0:16].reshape(-1, 2)
    tile_ids = jnp.arange(TILES, dtype=jnp.bfloat16)
    upper = (pairs[:, 0:1] == tile_ids[None, :]).astype(jnp.bfloat16)
    lower = (pairs[:, 1:2] == tile_ids[None, :]).astype(jnp.bfloat16)
    listed = lax.dot_general(
        upper, lower, (((0,), (0,)), ((), ())), preferred_element_type=jnp.float32
    )
    listed = (listed + listed.T > 0.0).astype(jnp.int32)
    mask = lax.dynamic_slice(listed, (4 * m, 0), (4, TILES)).reshape(-1)

    partial = apply_pairs(mask, rows, row_features.reshape(TILES, 256, 48), col_features)
    flux_out = finish(panel_cell, partial, table, flux_in)
    return (field_now, flux_out)


def solution(mesh):
    in_specs = (
        P(None, None, "dev", None),
        P(None, None, "dev", None),
        P(None, "dev", None),
        P(),
        P(),
        P("dev"),
        P(),
        P(),
        P(None, "dev"),
        P("dev", None),
    )
    out_specs = (P(None, None, "dev", None), P(None, "dev"))
    return jax.shard_map(body, mesh=mesh, in_specs=in_specs, out_specs=out_specs, check_vma=False)
```

```python
import math

import jax
import jax.numpy as jnp
from jax import lax
from jax.experimental import pallas as pl
from jax.experimental.pallas import tpu as pltpu
from jax.sharding import PartitionSpec as P

TILE = 2048
TILES = 64
LAYERS = 8
UNROLL = 4
WIDE = (63 << 20) + (1 << 19)
LINE = 8
PLANE = 16
COLS = 4 * TILE

softening = 0.0004
relax_rate = 0.8
update_rate = 0.5
kernel_gain = 0.25


def pair_kernel(
    mask_ref, f_far, pt_far, q_far, o_ref, f_ref, pt_ref, q_ref, total_ref, held_ref, order_ref, sems
):
    loads = [
        pltpu.make_async_copy(far, near, sems.at[at])
        for at, (far, near) in enumerate(((f_far, f_ref), (pt_far, pt_ref), (q_far, q_ref)))
    ]
    for load in loads:
        load.start()
    order_ref[0] = 0

    def note(at, count):
        order_ref[count + 1] = at
        return count + mask_ref[at]

    count = lax.fori_loop(0, 4 * TILES, note, jnp.int32(0))
    for u in range(UNROLL + 1):
        order_ref[count + 1 + u] = 0
    total_ref[...] = jnp.zeros(total_ref.shape, jnp.float32)
    held_ref[1] = jnp.zeros((256, TILE), jnp.bfloat16)
    for load in loads:
        load.wait()

    def step(b, carry):
        for u in range(UNROLL):
            t = b * UNROLL + u
            new, old = order_ref[t + 1], order_ref[t]
            valid = (t >= 1) & (t <= count)
            i = old % TILES
            at = pl.multiple_of((i % 4) * 64, 64)
            flux = jnp.concatenate(
                [f_ref[i // 4, pl.ds(at, 32), :], f_ref[i // 4, pl.ds(at + 32, 32), :]], axis=1
            )
            flux = jnp.where(valid, flux, jnp.zeros_like(flux))
            for c in range(4):
                columns = slice(c * 512, (c + 1) * 512)
                distance = jnp.dot(
                    pt_ref[new % TILES],
                    q_ref[new // TILES, :, columns],
                    preferred_element_type=jnp.float32,
                )
                held_ref[u % 2, :, columns] = lax.rsqrt(distance).astype(jnp.bfloat16)
                total_ref[old // TILES, :, columns] += jnp.dot(
                    flux, held_ref[1 - u % 2, :, columns], preferred_element_type=jnp.float32
                )
        return carry

    lax.fori_loop(0, (count + UNROLL) // UNROLL, step, 0)
    for j in range(4):
        for c in range(2):
            o_ref[2 * j + c] = total_ref[j, :, c * 1024 : (c + 1) * 1024].astype(jnp.bfloat16)


def apply_pairs(mask, flux_rows, row_features, col_features):
    hbm = pl.BlockSpec(memory_space=pltpu.HBM)
    return pl.pallas_call(
        pair_kernel,
        out_shape=jax.ShapeDtypeStruct((LINE, 32, 1024), jnp.bfloat16),
        in_specs=[pl.BlockSpec(memory_space=pltpu.SMEM), hbm, hbm, hbm],
        out_specs=pl.BlockSpec(memory_space=pltpu.VMEM),
        scratch_shapes=[
            pltpu.VMEM(flux_rows.shape, jnp.bfloat16),
            pltpu.VMEM(row_features.shape, jnp.bfloat16),
            pltpu.VMEM(col_features.shape, jnp.bfloat16),
            pltpu.VMEM((4, 32, TILE), jnp.float32),
            pltpu.VMEM((2, 256, TILE), jnp.bfloat16),
            pltpu.SMEM((4 * TILES + UNROLL + 2,), jnp.int32),
            pltpu.SemaphoreType.DMA((3,)),
        ],
        compiler_params=pltpu.CompilerParams(vmem_limit_bytes=WIDE),
        cost_estimate=pl.CostEstimate(
            flops=100_000_000_000, bytes_accessed=8 << 20, transcendentals=0
        ),
    )(mask, flux_rows, row_features, col_features)


def remote(src, dst, sends, recvs, at, device):
    return pltpu.make_async_remote_copy(
        src_ref=src,
        dst_ref=dst,
        send_sem=sends.at[at],
        recv_sem=recvs.at[at],
        device_id=(device,),
        device_id_type=pl.DeviceIdType.MESH,
    )


def greet(devices):
    barrier = pltpu.get_barrier_semaphore()
    for device in devices:
        pl.semaphore_signal(
            barrier, inc=1, device_id=(device,), device_id_type=pl.DeviceIdType.MESH
        )
    pl.semaphore_wait(barrier, len(devices))


def split3(value):
    high = value.astype(jnp.bfloat16).astype(jnp.float32)
    rest = value - high
    middle = rest.astype(jnp.bfloat16).astype(jnp.float32)
    return high, middle, rest - middle


def factors(pos, area, row_side):
    pos = pos - 0.5
    scale = (math.sqrt(TILE) / kernel_gain) / (area * area)
    norm = pos[0:1] * pos[0:1] + pos[1:2] * pos[1:2] + pos[2:3] * pos[2:3]
    one = jnp.ones_like(norm)
    rest = jnp.zeros((3, norm.shape[1]), jnp.float32)
    if row_side:
        parts = jnp.concatenate([norm + softening, one, -2.0 * pos, rest], axis=0) * scale
    else:
        parts = jnp.concatenate([one, norm, pos, rest], axis=0) * scale
    high, middle, low = split3(parts)
    if row_side:
        return jnp.concatenate([high, high, middle, middle, high, low], axis=0)
    return jnp.concatenate([high, middle, high, middle, low, high], axis=0)


def relax(field, source, conduct, step, lane):
    layer = jnp.zeros((1, 8, 128), jnp.float32)
    above = jnp.concatenate([field[1:], layer], axis=0)
    below = jnp.concatenate([layer, field[:-1]], axis=0)
    flat = field.reshape(LAYERS * 8, 128)
    right = jnp.where(lane < 127, pltpu.roll(flat, 127, axis=1).reshape(field.shape), 0.0)
    left = jnp.where(lane > 0, pltpu.roll(flat, 1, axis=1).reshape(field.shape), 0.0)
    ahead = pltpu.roll(field, 7, axis=1)
    behind = pltpu.roll(field, 1, axis=1)
    beside = (above + below) + (ahead + behind) + (right + left)
    applied = conduct * (6.0 * field - beside) + field
    return field + step * (source - applied)


def exchange_kernel(
    material_ref,
    scale_ref,
    list_ref,
    factor_ref,
    flux_far,
    field_far,
    source_far,
    pos_far,
    area_far,
    out_ref,
    top_ref,
    rows_ref,
    pt_ref,
    q_ref,
    flux_ref,
    field_ref,
    source_ref,
    pos_ref,
    area_ref,
    conduct_ref,
    slices,
    shared,
    stage,
    edge_field,
    edge_source,
    edge_conduct,
    halo_field,
    halo_source,
    halo_conduct,
    tops,
    pt_held,
    q_held,
    local,
    line_send,
    line_recv,
    edge_send,
    edge_recv,
    plane_send,
    plane_recv,
):
    me = lax.axis_index("dev")
    m, r = me // LINE, lax.rem(me, LINE)
    y, x = m // 4, lax.rem(m, 4)
    line = [LINE * m + lax.rem(r + k, LINE) for k in range(1, LINE)]
    after = lax.rem(me + 1, LINE * PLANE)
    before = lax.rem(me + LINE * PLANE - 1, LINE * PLANE)
    along_x = [LINE * (4 * y + lax.rem(x + k, 4)) + r for k in range(1, 4)]
    along_y = [LINE * (4 * lax.rem(y + k, 4) + x) + r for k in range(1, 4)]
    loads = [
        pltpu.make_async_copy(far, near, local.at[at])
        for at, (far, near) in enumerate(
            (
                (flux_far, flux_ref),
                (field_far, field_ref),
                (source_far, source_ref),
                (pos_far, pos_ref),
                (area_far, area_ref),
            )
        )
    ]
    for load in loads:
        load.start()
    partners = line + [after, before] + along_x + along_y
    barrier = pltpu.get_barrier_semaphore()
    for device in partners:
        pl.semaphore_signal(
            barrier, inc=1, device_id=(device,), device_id_type=pl.DeviceIdType.MESH
        )

    lane = lax.broadcasted_iota(jnp.int32, (16, 128), 1)
    pairs = list_ref[...].astype(jnp.float32)
    own_list = jnp.where(
        lane == 2 * r, pairs[:, 0:1], jnp.where(lane == 2 * r + 1, pairs[:, 1:2], 0.0)
    ).astype(jnp.bfloat16)
    loads[0].wait()
    for s in range(LINE):
        slices[s, 0:32, :] = flux_ref[:, s * 128 : (s + 1) * 128].astype(jnp.bfloat16)
        slices[s, 32:48, :] = own_list
    for layer in range(LAYERS):
        kind = material_ref[layer]
        scale = jnp.float32(0.0)
        for known in range(4):
            scale = scale + jnp.where(kind == known, scale_ref[known], 0.0)
        conduct_ref[layer] = factor_ref[layer] * scale
    loads[1].wait()
    loads[2].wait()
    for side, (at, one) in enumerate(((2, 3), (0, 0))):
        edge_field[side] = field_ref[:, :, at : at + 2, :]
        edge_source[side] = source_ref[:, :, one, :]
        edge_conduct[side] = conduct_ref[:, one, :]
    pl.semaphore_wait(barrier, len(partners))

    edges = []
    for side, device in enumerate((after, before)):
        for which, (src, dst) in enumerate(
            ((edge_field, halo_field), (edge_source, halo_source), (edge_conduct, halo_conduct))
        ):
            edges.append(
                remote(
                    src.at[side], dst.at[side], edge_send, edge_recv, 3 * side + which, device
                )
            )
    copies = []
    for k in range(1, LINE):
        there = lax.rem(r + k, LINE)
        copies.append(
            remote(slices.at[there], shared.at[r], line_send, line_recv, k - 1, line[k - 1])
        )
    for copy in copies + edges:
        copy.start()
    shared[r] = slices[r]

    def row_block(step, carry):
        for u in range(8):
            half = step * 8 + u
            at = pl.multiple_of(half * 1024 + r * 128, 128)
            part = factors(pos_ref[:, pl.ds(at, 128)], area_ref[:, pl.ds(at, 128)], True)
            pt_held[half] = part.T.astype(jnp.bfloat16)
        return carry

    loads[3].wait()
    loads[4].wait()
    lax.fori_loop(0, 3, row_block, 0)

    for copy in copies:
        copy.wait()
    lists = jnp.zeros((16, 128), jnp.float32)
    for s in range(LINE):
        stage[32 * s : 32 * s + 32, :] = shared[s, 0:32, :]
        lists = lists + shared[s, 32:48, :].astype(jnp.float32)
    stage[256:272, :] = lists.astype(jnp.bfloat16)
    own = pltpu.make_async_copy(stage, rows_ref.at[y, x], local.at[5])
    own.start()
    one, two = slice(0, 128), slice(128, 272)
    near, far = [], []
    for k in range(3):
        near.append(
            remote(stage.at[one], rows_ref.at[y, x, one], plane_send, plane_recv, k, along_x[k])
        )
        near.append(
            remote(
                stage.at[two], rows_ref.at[y, x, two], plane_send, plane_recv, 3 + k, along_y[k]
            )
        )
        part = rows_ref.at[y, :, one]
        far.append(remote(part, part, plane_send, plane_recv, 6 + k, along_y[k]))
        part = rows_ref.at[:, x, two]
        far.append(remote(part, part, plane_send, plane_recv, 9 + k, along_x[k]))
    for copy in near:
        copy.start()

    lax.fori_loop(3, 6, row_block, 0)
    own.wait()
    for copy in near:
        copy.wait()
    for copy in far:
        copy.start()

    for copy in edges:
        copy.wait()
    row = lax.broadcasted_iota(jnp.int32, (LAYERS, 8, 128), 1)
    lane = lax.broadcasted_iota(jnp.int32, (LAYERS, 8, 128), 2)
    real = ((row >= 2) | (me > 0)) & ((row < 6) | (me < LINE * PLANE - 1))
    pad = jnp.zeros((LAYERS, 1, 128), jnp.float32)
    conduct = jnp.concatenate(
        [pad, halo_conduct[0][:, None], conduct_ref[...], halo_conduct[1][:, None], pad], axis=1
    )
    step = relax_rate / (6.0 * conduct + 1.0)

    def one_load(load, carry):
        field = jnp.concatenate(
            [halo_field[0, load], field_ref[load], halo_field[1, load]], axis=1
        )
        field = jnp.where(real, field, 0.0)
        source = jnp.concatenate(
            [
                pad,
                halo_source[0, load][:, None],
                source_ref[load],
                halo_source[1, load][:, None],
                pad,
            ],
            axis=1,
        )
        field = jnp.where(real, relax(field, source, conduct, step, lane), 0.0)
        field = relax(field, source, conduct, step, lane)
        out_ref[load] = field[:, 2:6]
        tops[load] = field[LAYERS - 1, 2:6]
        return carry

    lax.fori_loop(0, 32, one_load, 0)
    for at in range(4):
        top_ref[at] = tops[:, at, :].astype(jnp.bfloat16)

    lax.fori_loop(6, TILES // 4, row_block, 0)
    moves = [pltpu.make_async_copy(pt_held, pt_ref, local.at[6])]
    moves[0].start()
    for j in range(4):
        for c in range(4):
            at = pl.multiple_of(m * COLS + j * TILE + c * 512, 512)
            part = factors(pos_ref[:, pl.ds(at, 512)], area_ref[:, pl.ds(at, 512)], False)
            q_held[j, :, c * 512 : (c + 1) * 512] = part.astype(jnp.bfloat16)
    moves.append(pltpu.make_async_copy(q_held, q_ref, local.at[7]))
    moves[1].start()
    for copy in far + moves:
        copy.wait()


def exchange(materials, scales, lists, factor, flux, field, source, pos, area):
    vmem = pl.BlockSpec(memory_space=pltpu.VMEM)
    hbm = pl.BlockSpec(memory_space=pltpu.HBM)
    smem = pl.BlockSpec(memory_space=pltpu.SMEM)
    row_shape, col_shape = (2 * TILES, 128, 48), (4, 48, TILE)
    f32, half = jnp.float32, jnp.bfloat16
    halo = [
        pltpu.VMEM((2, 32, LAYERS, 2, 128), f32),
        pltpu.VMEM((2, 32, LAYERS, 128), f32),
        pltpu.VMEM((2, LAYERS, 128), f32),
    ]
    return pl.pallas_call(
        exchange_kernel,
        out_shape=(
            jax.ShapeDtypeStruct(field.shape, f32),
            jax.ShapeDtypeStruct((4, 32, 128), half),
            jax.ShapeDtypeStruct((4, 4, 272, 128), half),
            jax.ShapeDtypeStruct(row_shape, half),
            jax.ShapeDtypeStruct(col_shape, half),
        ),
        in_specs=[smem, smem, vmem, vmem] + [hbm] * 5,
        out_specs=(vmem, vmem, hbm, hbm, hbm),
        scratch_shapes=[
            pltpu.VMEM(flux.shape, f32),
            pltpu.VMEM(field.shape, f32),
            pltpu.VMEM(source.shape, f32),
            pltpu.VMEM(pos.shape, f32),
            pltpu.VMEM(area.shape, f32),
            pltpu.VMEM(factor.shape, f32),
            pltpu.VMEM((LINE, 48, 128), half),
            pltpu.VMEM((LINE, 48, 128), half),
            pltpu.VMEM((272, 128), half),
        ]
        + halo
        + halo
        + [
            pltpu.VMEM((32, 4, 128), f32),
            pltpu.VMEM(row_shape, half),
            pltpu.VMEM(col_shape, half),
            pltpu.SemaphoreType.DMA((8,)),
            pltpu.SemaphoreType.DMA((LINE - 1,)),
            pltpu.SemaphoreType.DMA((LINE - 1,)),
            pltpu.SemaphoreType.DMA((6,)),
            pltpu.SemaphoreType.DMA((6,)),
            pltpu.SemaphoreType.DMA((12,)),
            pltpu.SemaphoreType.DMA((12,)),
        ],
        compiler_params=pltpu.CompilerParams(
            collective_id=0, has_side_effects=True, vmem_limit_bytes=WIDE
        ),
    )(materials, scales, lists, factor, flux, field, source, pos, area)


def reduce_kernel(part_ref, out_ref, landed, sends, recvs):
    me = lax.axis_index("dev")
    m, r = me // LINE, lax.rem(me, LINE)
    line = [LINE * m + lax.rem(r + k, LINE) for k in range(1, LINE)]
    greet(line)
    copies = []
    for k in range(1, LINE):
        there = lax.rem(r + k, LINE)
        copies.append(
            remote(part_ref.at[there], landed.at[k - 1], sends, recvs, k - 1, line[k - 1])
        )
    for copy in copies:
        copy.start()
    total = part_ref[r].astype(jnp.float32)
    for k, copy in enumerate(copies):
        copy.wait()
        total = total + landed[k].astype(jnp.float32)
    out_ref[...] = total


def reduce_line(partial):
    vmem = pl.BlockSpec(memory_space=pltpu.VMEM)
    return pl.pallas_call(
        reduce_kernel,
        out_shape=jax.ShapeDtypeStruct((32, 1024), jnp.float32),
        in_specs=[vmem],
        out_specs=vmem,
        scratch_shapes=[
            pltpu.VMEM((LINE - 1, 32, 1024), jnp.bfloat16),
            pltpu.SemaphoreType.DMA((LINE - 1,)),
            pltpu.SemaphoreType.DMA((LINE - 1,)),
        ],
        compiler_params=pltpu.CompilerParams(
            collective_id=1, has_side_effects=True, vmem_limit_bytes=8 << 20
        ),
    )(partial)


def finish_kernel(cell_ref, total_ref, flux_ref, table_ref, out_ref):
    lane = lax.broadcasted_iota(jnp.int32, (32, 128), 1)
    for g in range(8):

        def pick(step, held):
            for u in range(16):
                at = step * 16 + u
                cell = cell_ref[g * 128 + at]
                block = table_ref[lax.shift_right_logical(cell, 7)].astype(jnp.float32)
                moved = pltpu.roll(block, (at - cell) & 127, axis=1)
                held = jnp.where(lane == at, moved, held)
            return held

        traces = lax.fori_loop(0, 8, pick, jnp.zeros((32, 128), jnp.float32))
        at = slice(g * 128, (g + 1) * 128)
        out_ref[:, at] = flux_ref[:, at] + update_rate * (traces - total_ref[:, at])


def finish(cells, total, flux_in, table):
    vmem = pl.BlockSpec(memory_space=pltpu.VMEM)
    return pl.pallas_call(
        finish_kernel,
        out_shape=jax.ShapeDtypeStruct(flux_in.shape, jnp.float32),
        in_specs=[pl.BlockSpec(memory_space=pltpu.SMEM), vmem, vmem, vmem],
        out_specs=vmem,
        compiler_params=pltpu.CompilerParams(vmem_limit_bytes=8 << 20),
    )(cells, total, flux_in, table)


def body(
    field_in,
    source,
    cell_factor,
    layer_material,
    material_scale,
    panel_cell,
    panel_pos,
    panel_area,
    flux_in,
    pair_list,
):
    me = lax.axis_index("dev")
    m = me // LINE

    field_now, surface_top, rows, row_features, col_features = exchange(
        layer_material,
        material_scale,
        pair_list,
        cell_factor,
        flux_in,
        field_in,
        source,
        panel_pos,
        panel_area.reshape(1, -1),
    )
    table = lax.all_gather(surface_top, "dev", axis=0, tiled=True)
    rows = rows.reshape(PLANE, 272, 128)
    pairs = rows[:, 256:272, 0:16].reshape(-1, 2)
    tile_ids = jnp.arange(TILES, dtype=jnp.bfloat16)
    upper = (pairs[:, 0:1] == tile_ids[None, :]).astype(jnp.bfloat16)
    lower = (pairs[:, 1:2] == tile_ids[None, :]).astype(jnp.bfloat16)
    listed = lax.dot_general(
        upper, lower, (((0,), (0,)), ((), ())), preferred_element_type=jnp.float32
    )
    listed = (listed + listed.T > 0.0).astype(jnp.int32)
    mask = lax.dynamic_slice(listed, (4 * m, 0), (4, TILES)).reshape(-1)

    partial = apply_pairs(mask, rows, row_features.reshape(TILES, 256, 48), col_features)
    flux_out = finish(panel_cell, reduce_line(partial), flux_in, table)
    return (field_now, flux_out)


def solution(mesh):
    in_specs = (
        P(None, None, "dev", None),
        P(None, None, "dev", None),
        P(None, "dev", None),
        P(),
        P(),
        P("dev"),
        P(),
        P(),
        P(None, "dev"),
        P("dev", None),
    )
    out_specs = (P(None, None, "dev", None), P(None, "dev"))
    return jax.shard_map(body, mesh=mesh, in_specs=in_specs, out_specs=out_specs, check_vma=False)
```

```python
import math

import jax
import jax.numpy as jnp
from jax import lax
from jax.experimental import pallas as pl
from jax.experimental.pallas import tpu as pltpu
from jax.sharding import PartitionSpec as P

TILE = 2048
TILES = 64
LAYERS = 8
UNROLL = 4
WIDE = (63 << 20) + (1 << 19)
LINE = 8
PLANE = 16
COLS = 4 * TILE

softening = 0.0004
relax_rate = 0.8
update_rate = 0.5
kernel_gain = 0.25


def pair_kernel(
    mask_ref, f_far, pt_far, q_far, o_ref, f_ref, pt_ref, q_ref, total_ref, held_ref, order_ref, sems
):
    loads = [
        pltpu.make_async_copy(far, near, sems.at[at])
        for at, (far, near) in enumerate(((f_far, f_ref), (pt_far, pt_ref), (q_far, q_ref)))
    ]
    for load in loads:
        load.start()
    order_ref[0] = 0

    def note(at, count):
        order_ref[count + 1] = at
        return count + mask_ref[at]

    count = lax.fori_loop(0, 4 * TILES, note, jnp.int32(0))
    for u in range(UNROLL + 1):
        order_ref[count + 1 + u] = 0
    total_ref[...] = jnp.zeros(total_ref.shape, jnp.float32)
    held_ref[1] = jnp.zeros((256, TILE), jnp.bfloat16)
    for load in loads:
        load.wait()

    def step(b, carry):
        for u in range(UNROLL):
            t = b * UNROLL + u
            new, old = order_ref[t + 1], order_ref[t]
            valid = (t >= 1) & (t <= count)
            i = old % TILES
            at = pl.multiple_of((i % 4) * 64, 64)
            flux = jnp.concatenate(
                [f_ref[i // 4, pl.ds(at, 32), :], f_ref[i // 4, pl.ds(at + 32, 32), :]], axis=1
            )
            flux = jnp.where(valid, flux, jnp.zeros_like(flux))
            for c in range(4):
                columns = slice(c * 512, (c + 1) * 512)
                distance = jnp.dot(
                    pt_ref[new % TILES],
                    q_ref[new // TILES, :, columns],
                    preferred_element_type=jnp.float32,
                )
                held_ref[u % 2, :, columns] = lax.rsqrt(distance).astype(jnp.bfloat16)
                total_ref[old // TILES, :, columns] += jnp.dot(
                    flux, held_ref[1 - u % 2, :, columns], preferred_element_type=jnp.float32
                )
        return carry

    lax.fori_loop(0, (count + UNROLL) // UNROLL, step, 0)
    for j in range(4):
        for c in range(2):
            o_ref[2 * j + c] = total_ref[j, :, c * 1024 : (c + 1) * 1024].astype(jnp.bfloat16)


def apply_pairs(mask, flux_rows, row_features, col_features):
    hbm = pl.BlockSpec(memory_space=pltpu.HBM)
    return pl.pallas_call(
        pair_kernel,
        out_shape=jax.ShapeDtypeStruct((LINE, 32, 1024), jnp.bfloat16),
        in_specs=[pl.BlockSpec(memory_space=pltpu.SMEM), hbm, hbm, hbm],
        out_specs=pl.BlockSpec(memory_space=pltpu.VMEM),
        scratch_shapes=[
            pltpu.VMEM(flux_rows.shape, jnp.bfloat16),
            pltpu.VMEM(row_features.shape, jnp.bfloat16),
            pltpu.VMEM(col_features.shape, jnp.bfloat16),
            pltpu.VMEM((4, 32, TILE), jnp.float32),
            pltpu.VMEM((2, 256, TILE), jnp.bfloat16),
            pltpu.SMEM((4 * TILES + UNROLL + 2,), jnp.int32),
            pltpu.SemaphoreType.DMA((3,)),
        ],
        compiler_params=pltpu.CompilerParams(vmem_limit_bytes=WIDE),
        cost_estimate=pl.CostEstimate(
            flops=100_000_000_000, bytes_accessed=8 << 20, transcendentals=0
        ),
    )(mask, flux_rows, row_features, col_features)


def remote(src, dst, sends, recvs, at, device):
    return pltpu.make_async_remote_copy(
        src_ref=src,
        dst_ref=dst,
        send_sem=sends.at[at],
        recv_sem=recvs.at[at],
        device_id=(device,),
        device_id_type=pl.DeviceIdType.MESH,
    )


def greet(devices):
    barrier = pltpu.get_barrier_semaphore()
    for device in devices:
        pl.semaphore_signal(
            barrier, inc=1, device_id=(device,), device_id_type=pl.DeviceIdType.MESH
        )
    pl.semaphore_wait(barrier, len(devices))


def split3(value):
    high = value.astype(jnp.bfloat16).astype(jnp.float32)
    rest = value - high
    middle = rest.astype(jnp.bfloat16).astype(jnp.float32)
    return high, middle, rest - middle


def factors(pos, area, row_side):
    pos = pos - 0.5
    scale = (math.sqrt(TILE) / kernel_gain) / (area * area)
    norm = pos[0:1] * pos[0:1] + pos[1:2] * pos[1:2] + pos[2:3] * pos[2:3]
    one = jnp.ones_like(norm)
    rest = jnp.zeros((3, norm.shape[1]), jnp.float32)
    if row_side:
        parts = jnp.concatenate([norm + softening, one, -2.0 * pos, rest], axis=0) * scale
    else:
        parts = jnp.concatenate([one, norm, pos, rest], axis=0) * scale
    high, middle, low = split3(parts)
    if row_side:
        return jnp.concatenate([high, high, middle, middle, high, low], axis=0)
    return jnp.concatenate([high, middle, high, middle, low, high], axis=0)


def relax(field, source, conduct, step, lane):
    layer = jnp.zeros((1, 8, 128), jnp.float32)
    above = jnp.concatenate([field[1:], layer], axis=0)
    below = jnp.concatenate([layer, field[:-1]], axis=0)
    flat = field.reshape(LAYERS * 8, 128)
    right = jnp.where(lane < 127, pltpu.roll(flat, 127, axis=1).reshape(field.shape), 0.0)
    left = jnp.where(lane > 0, pltpu.roll(flat, 1, axis=1).reshape(field.shape), 0.0)
    ahead = pltpu.roll(field, 7, axis=1)
    behind = pltpu.roll(field, 1, axis=1)
    beside = (above + below) + (ahead + behind) + (right + left)
    applied = conduct * (6.0 * field - beside) + field
    return field + step * (source - applied)


def exchange_kernel(
    material_ref,
    scale_ref,
    list_ref,
    factor_ref,
    flux_far,
    field_far,
    source_far,
    pos_far,
    area_far,
    out_ref,
    top_ref,
    rows_ref,
    pt_ref,
    q_ref,
    flux_ref,
    field_ref,
    source_ref,
    pos_ref,
    area_ref,
    conduct_ref,
    slices,
    shared,
    stage,
    edge_field,
    edge_source,
    edge_conduct,
    halo_field,
    halo_source,
    halo_conduct,
    tops,
    pt_held,
    q_held,
    local,
    line_send,
    line_recv,
    edge_send,
    edge_recv,
    plane_send,
    plane_recv,
):
    me = lax.axis_index("dev")
    m, r = me // LINE, lax.rem(me, LINE)
    y, x = m // 4, lax.rem(m, 4)
    line = [LINE * m + lax.rem(r + k, LINE) for k in range(1, LINE)]
    after = lax.rem(me + 1, LINE * PLANE)
    before = lax.rem(me + LINE * PLANE - 1, LINE * PLANE)
    along_x = [LINE * (4 * y + lax.rem(x + k, 4)) + r for k in range(1, 4)]
    along_y = [LINE * (4 * lax.rem(y + k, 4) + x) + r for k in range(1, 4)]
    loads = [
        pltpu.make_async_copy(far, near, local.at[at])
        for at, (far, near) in enumerate(
            (
                (flux_far, flux_ref),
                (field_far, field_ref),
                (source_far, source_ref),
                (pos_far, pos_ref),
                (area_far, area_ref),
            )
        )
    ]
    for load in loads:
        load.start()
    partners = line + [after, before] + along_x + along_y
    barrier = pltpu.get_barrier_semaphore()
    for device in partners:
        pl.semaphore_signal(
            barrier, inc=1, device_id=(device,), device_id_type=pl.DeviceIdType.MESH
        )

    lane = lax.broadcasted_iota(jnp.int32, (16, 128), 1)
    pairs = list_ref[...].astype(jnp.float32)
    own_list = jnp.where(
        lane == 2 * r, pairs[:, 0:1], jnp.where(lane == 2 * r + 1, pairs[:, 1:2], 0.0)
    ).astype(jnp.bfloat16)
    loads[0].wait()
    for s in range(LINE):
        slices[s, 0:32, :] = flux_ref[:, s * 128 : (s + 1) * 128].astype(jnp.bfloat16)
        slices[s, 32:48, :] = own_list
    for layer in range(LAYERS):
        kind = material_ref[layer]
        scale = jnp.float32(0.0)
        for known in range(4):
            scale = scale + jnp.where(kind == known, scale_ref[known], 0.0)
        conduct_ref[layer] = factor_ref[layer] * scale
    loads[1].wait()
    loads[2].wait()
    for side, (at, one) in enumerate(((2, 3), (0, 0))):
        edge_field[side] = field_ref[:, :, at : at + 2, :]
        edge_source[side] = source_ref[:, :, one, :]
        edge_conduct[side] = conduct_ref[:, one, :]
    pl.semaphore_wait(barrier, len(partners))

    edges = []
    for side, device in enumerate((after, before)):
        for which, (src, dst) in enumerate(
            ((edge_field, halo_field), (edge_source, halo_source), (edge_conduct, halo_conduct))
        ):
            edges.append(
                remote(
                    src.at[side], dst.at[side], edge_send, edge_recv, 3 * side + which, device
                )
            )
    copies = []
    for k in range(1, LINE):
        there = lax.rem(r + k, LINE)
        copies.append(
            remote(slices.at[there], shared.at[r], line_send, line_recv, k - 1, line[k - 1])
        )
    for copy in copies + edges:
        copy.start()
    shared[r] = slices[r]

    def row_block(step, carry):
        for u in range(8):
            half = step * 8 + u
            at = pl.multiple_of(half * 1024 + r * 128, 128)
            part = factors(pos_ref[:, pl.ds(at, 128)], area_ref[:, pl.ds(at, 128)], True)
            pt_held[half] = part.T.astype(jnp.bfloat16)
        return carry

    loads[3].wait()
    loads[4].wait()
    lax.fori_loop(0, 3, row_block, 0)

    for copy in copies:
        copy.wait()
    lists = jnp.zeros((16, 128), jnp.float32)
    for s in range(LINE):
        stage[32 * s : 32 * s + 32, :] = shared[s, 0:32, :]
        lists = lists + shared[s, 32:48, :].astype(jnp.float32)
    stage[256:272, :] = lists.astype(jnp.bfloat16)
    own = pltpu.make_async_copy(stage, rows_ref.at[y, x], local.at[5])
    own.start()
    one, two = slice(0, 128), slice(128, 272)
    near, far = [], []
    for k in range(3):
        near.append(
            remote(stage.at[one], rows_ref.at[y, x, one], plane_send, plane_recv, k, along_x[k])
        )
        near.append(
            remote(
                stage.at[two], rows_ref.at[y, x, two], plane_send, plane_recv, 3 + k, along_y[k]
            )
        )
        part = rows_ref.at[y, :, one]
        far.append(remote(part, part, plane_send, plane_recv, 6 + k, along_y[k]))
        part = rows_ref.at[:, x, two]
        far.append(remote(part, part, plane_send, plane_recv, 9 + k, along_x[k]))
    for copy in near:
        copy.start()

    lax.fori_loop(3, 6, row_block, 0)
    own.wait()
    for copy in near:
        copy.wait()
    for copy in far:
        copy.start()

    for copy in edges:
        copy.wait()
    row = lax.broadcasted_iota(jnp.int32, (LAYERS, 8, 128), 1)
    lane = lax.broadcasted_iota(jnp.int32, (LAYERS, 8, 128), 2)
    real = ((row >= 2) | (me > 0)) & ((row < 6) | (me < LINE * PLANE - 1))
    pad = jnp.zeros((LAYERS, 1, 128), jnp.float32)
    conduct = jnp.concatenate(
        [pad, halo_conduct[0][:, None], conduct_ref[...], halo_conduct[1][:, None], pad], axis=1
    )
    step = relax_rate / (6.0 * conduct + 1.0)

    def one_load(load, carry):
        field = jnp.concatenate(
            [halo_field[0, load], field_ref[load], halo_field[1, load]], axis=1
        )
        field = jnp.where(real, field, 0.0)
        source = jnp.concatenate(
            [
                pad,
                halo_source[0, load][:, None],
                source_ref[load],
                halo_source[1, load][:, None],
                pad,
            ],
            axis=1,
        )
        field = jnp.where(real, relax(field, source, conduct, step, lane), 0.0)
        field = relax(field, source, conduct, step, lane)
        out_ref[load] = field[:, 2:6]
        tops[load] = field[LAYERS - 1, 2:6]
        return carry

    lax.fori_loop(0, 32, one_load, 0)
    for at in range(4):
        top_ref[at] = tops[:, at, :].astype(jnp.bfloat16)

    lax.fori_loop(6, TILES // 4, row_block, 0)
    moves = [pltpu.make_async_copy(pt_held, pt_ref, local.at[6])]
    moves[0].start()
    for j in range(4):
        for c in range(4):
            at = pl.multiple_of(m * COLS + j * TILE + c * 512, 512)
            part = factors(pos_ref[:, pl.ds(at, 512)], area_ref[:, pl.ds(at, 512)], False)
            q_held[j, :, c * 512 : (c + 1) * 512] = part.astype(jnp.bfloat16)
    moves.append(pltpu.make_async_copy(q_held, q_ref, local.at[7]))
    moves[1].start()
    for copy in far + moves:
        copy.wait()


def exchange(materials, scales, lists, factor, flux, field, source, pos, area):
    vmem = pl.BlockSpec(memory_space=pltpu.VMEM)
    hbm = pl.BlockSpec(memory_space=pltpu.HBM)
    smem = pl.BlockSpec(memory_space=pltpu.SMEM)
    row_shape, col_shape = (2 * TILES, 128, 48), (4, 48, TILE)
    f32, half = jnp.float32, jnp.bfloat16
    halo = [
        pltpu.VMEM((2, 32, LAYERS, 2, 128), f32),
        pltpu.VMEM((2, 32, LAYERS, 128), f32),
        pltpu.VMEM((2, LAYERS, 128), f32),
    ]
    return pl.pallas_call(
        exchange_kernel,
        out_shape=(
            jax.ShapeDtypeStruct(field.shape, f32),
            jax.ShapeDtypeStruct((4, 32, 128), half),
            jax.ShapeDtypeStruct((4, 4, 272, 128), half),
            jax.ShapeDtypeStruct(row_shape, half),
            jax.ShapeDtypeStruct(col_shape, half),
        ),
        in_specs=[smem, smem, vmem, vmem] + [hbm] * 5,
        out_specs=(vmem, vmem, hbm, hbm, hbm),
        scratch_shapes=[
            pltpu.VMEM(flux.shape, f32),
            pltpu.VMEM(field.shape, f32),
            pltpu.VMEM(source.shape, f32),
            pltpu.VMEM(pos.shape, f32),
            pltpu.VMEM(area.shape, f32),
            pltpu.VMEM(factor.shape, f32),
            pltpu.VMEM((LINE, 48, 128), half),
            pltpu.VMEM((LINE, 48, 128), half),
            pltpu.VMEM((272, 128), half),
        ]
        + halo
        + halo
        + [
            pltpu.VMEM((32, 4, 128), f32),
            pltpu.VMEM(row_shape, half),
            pltpu.VMEM(col_shape, half),
            pltpu.SemaphoreType.DMA((8,)),
            pltpu.SemaphoreType.DMA((LINE - 1,)),
            pltpu.SemaphoreType.DMA((LINE - 1,)),
            pltpu.SemaphoreType.DMA((6,)),
            pltpu.SemaphoreType.DMA((6,)),
            pltpu.SemaphoreType.DMA((12,)),
            pltpu.SemaphoreType.DMA((12,)),
        ],
        compiler_params=pltpu.CompilerParams(
            collective_id=0, has_side_effects=True, vmem_limit_bytes=WIDE
        ),
    )(materials, scales, lists, factor, flux, field, source, pos, area)


def finish_kernel(
    cell_ref, part_ref, table_ref, flux_ref, out_ref, table, landed, traces, load_sem, sends, recvs
):
    me = lax.axis_index("dev")
    m, r = me // LINE, lax.rem(me, LINE)
    load = pltpu.make_async_copy(table_ref, table, load_sem)
    load.start()
    line = [LINE * m + lax.rem(r + k, LINE) for k in range(1, LINE)]
    greet(line)
    copies = []
    for k in range(1, LINE):
        there = lax.rem(r + k, LINE)
        copy = remote(part_ref.at[there], landed.at[k - 1], sends, recvs, k - 1, line[k - 1])
        copy.start()
        copies.append(copy)
    load.wait()
    lane = lax.broadcasted_iota(jnp.int32, (32, 128), 1)

    def group(g, carry):
        def pick(step, held):
            for u in range(16):
                at = step * 16 + u
                cell = cell_ref[g * 128 + at]
                block = table[lax.shift_right_logical(cell, 7)].astype(jnp.float32)
                moved = pltpu.roll(block, (at - cell) & 127, axis=1)
                held = jnp.where(lane == at, moved, held)
            return held

        traces[g] = lax.fori_loop(0, 8, pick, jnp.zeros((32, 128), jnp.float32))
        return carry

    lax.fori_loop(0, 8, group, 0)
    for copy in copies:
        copy.wait()
    total = part_ref[r].astype(jnp.float32)
    for k in range(LINE - 1):
        total = total + landed[k].astype(jnp.float32)
    for g in range(8):
        at = slice(g * 128, (g + 1) * 128)
        out_ref[:, at] = flux_ref[:, at] + update_rate * (traces[g] - total[:, at])


def finish(cells, partial, table, flux_in):
    vmem = pl.BlockSpec(memory_space=pltpu.VMEM)
    return pl.pallas_call(
        finish_kernel,
        out_shape=jax.ShapeDtypeStruct(flux_in.shape, jnp.float32),
        in_specs=[
            pl.BlockSpec(memory_space=pltpu.SMEM),
            vmem,
            pl.BlockSpec(memory_space=pltpu.HBM),
            vmem,
        ],
        out_specs=vmem,
        scratch_shapes=[
            pltpu.VMEM(table.shape, jnp.bfloat16),
            pltpu.VMEM((LINE - 1, 32, 1024), jnp.bfloat16),
            pltpu.VMEM((8, 32, 128), jnp.float32),
            pltpu.SemaphoreType.DMA,
            pltpu.SemaphoreType.DMA((LINE - 1,)),
            pltpu.SemaphoreType.DMA((LINE - 1,)),
        ],
        compiler_params=pltpu.CompilerParams(
            collective_id=1, has_side_effects=True, vmem_limit_bytes=WIDE
        ),
    )(cells, partial, table, flux_in)


def body(
    field_in,
    source,
    cell_factor,
    layer_material,
    material_scale,
    panel_cell,
    panel_pos,
    panel_area,
    flux_in,
    pair_list,
):
    me = lax.axis_index("dev")
    m = me // LINE

    field_now, surface_top, rows, row_features, col_features = exchange(
        layer_material,
        material_scale,
        pair_list,
        cell_factor,
        flux_in,
        field_in,
        source,
        panel_pos,
        panel_area.reshape(1, -1),
    )
    table = lax.all_gather(surface_top, "dev", axis=0, tiled=True)
    rows = rows.reshape(PLANE, 272, 128)
    pairs = rows[:, 256:272, 0:16].reshape(-1, 2)
    tile_ids = jnp.arange(TILES, dtype=jnp.bfloat16)
    upper = (pairs[:, 0:1] == tile_ids[None, :]).astype(jnp.bfloat16)
    lower = (pairs[:, 1:2] == tile_ids[None, :]).astype(jnp.bfloat16)
    listed = lax.dot_general(
        upper, lower, (((0,), (0,)), ((), ())), preferred_element_type=jnp.float32
    )
    listed = (listed + listed.T > 0.0).astype(jnp.int32)
    mask = lax.dynamic_slice(listed, (4 * m, 0), (4, TILES)).reshape(-1)

    partial = apply_pairs(mask, rows, row_features.reshape(TILES, 256, 48), col_features)
    flux_out = finish(panel_cell, partial, table, flux_in)
    return (field_now, flux_out)


def solution(mesh):
    in_specs = (
        P(None, None, "dev", None),
        P(None, None, "dev", None),
        P(None, "dev", None),
        P(),
        P(),
        P("dev"),
        P(),
        P(),
        P(None, "dev"),
        P("dev", None),
    )
    out_specs = (P(None, None, "dev", None), P(None, "dev"))
    return jax.shard_map(body, mesh=mesh, in_specs=in_specs, out_specs=out_specs, check_vma=False)
```

```python
import math

import jax
import jax.numpy as jnp
from jax import lax
from jax.experimental import pallas as pl
from jax.experimental.pallas import tpu as pltpu
from jax.sharding import PartitionSpec as P

TILE = 2048
TILES = 64
LAYERS = 8
UNROLL = 4
WIDE = (63 << 20) + (1 << 19)
LINE = 8
PLANE = 16
COLS = 4 * TILE

softening = 0.0004
relax_rate = 0.8
update_rate = 0.5
kernel_gain = 0.25


def pair_kernel(
    mask_ref, f_far, pt_far, q_far, o_ref, f_ref, pt_ref, q_ref, total_ref, held_ref, order_ref, sems
):
    loads = [
        pltpu.make_async_copy(far, near, sems.at[at])
        for at, (far, near) in enumerate(((f_far, f_ref), (pt_far, pt_ref), (q_far, q_ref)))
    ]
    for load in loads:
        load.start()
    order_ref[0] = 0

    def note(at, count):
        order_ref[count + 1] = at
        return count + mask_ref[at]

    count = lax.fori_loop(0, 4 * TILES, note, jnp.int32(0))
    for u in range(UNROLL + 1):
        order_ref[count + 1 + u] = 0
    total_ref[...] = jnp.zeros(total_ref.shape, jnp.float32)
    held_ref[1] = jnp.zeros((256, TILE), jnp.bfloat16)
    for load in loads:
        load.wait()

    def step(b, carry):
        for u in range(UNROLL):
            t = b * UNROLL + u
            new, old = order_ref[t + 1], order_ref[t]
            valid = (t >= 1) & (t <= count)
            i = old % TILES
            at = pl.multiple_of((i % 4) * 64, 64)
            flux = jnp.concatenate(
                [f_ref[i // 4, pl.ds(at, 32), :], f_ref[i // 4, pl.ds(at + 32, 32), :]], axis=1
            )
            flux = jnp.where(valid, flux, jnp.zeros_like(flux))
            for c in range(4):
                columns = slice(c * 512, (c + 1) * 512)
                distance = jnp.dot(
                    pt_ref[new % TILES],
                    q_ref[new // TILES, :, columns],
                    preferred_element_type=jnp.float32,
                )
                held_ref[u % 2, :, columns] = lax.rsqrt(distance).astype(jnp.bfloat16)
                total_ref[old // TILES, :, columns] += jnp.dot(
                    flux, held_ref[1 - u % 2, :, columns], preferred_element_type=jnp.float32
                )
        return carry

    lax.fori_loop(0, (count + UNROLL) // UNROLL, step, 0)
    for j in range(4):
        for c in range(2):
            o_ref[2 * j + c] = total_ref[j, :, c * 1024 : (c + 1) * 1024].astype(jnp.bfloat16)


def apply_pairs(mask, flux_rows, row_features, col_features):
    hbm = pl.BlockSpec(memory_space=pltpu.HBM)
    return pl.pallas_call(
        pair_kernel,
        out_shape=jax.ShapeDtypeStruct((LINE, 32, 1024), jnp.bfloat16),
        in_specs=[pl.BlockSpec(memory_space=pltpu.SMEM), hbm, hbm, hbm],
        out_specs=pl.BlockSpec(memory_space=pltpu.VMEM),
        scratch_shapes=[
            pltpu.VMEM(flux_rows.shape, jnp.bfloat16),
            pltpu.VMEM(row_features.shape, jnp.bfloat16),
            pltpu.VMEM(col_features.shape, jnp.bfloat16),
            pltpu.VMEM((4, 32, TILE), jnp.float32),
            pltpu.VMEM((2, 256, TILE), jnp.bfloat16),
            pltpu.SMEM((4 * TILES + UNROLL + 2,), jnp.int32),
            pltpu.SemaphoreType.DMA((3,)),
        ],
        compiler_params=pltpu.CompilerParams(vmem_limit_bytes=WIDE),
        cost_estimate=pl.CostEstimate(
            flops=100_000_000_000, bytes_accessed=8 << 20, transcendentals=0
        ),
    )(mask, flux_rows, row_features, col_features)


def remote(src, dst, sends, recvs, at, device):
    return pltpu.make_async_remote_copy(
        src_ref=src,
        dst_ref=dst,
        send_sem=sends.at[at],
        recv_sem=recvs.at[at],
        device_id=(device,),
        device_id_type=pl.DeviceIdType.MESH,
    )


def greet(devices):
    barrier = pltpu.get_barrier_semaphore()
    for device in devices:
        pl.semaphore_signal(
            barrier, inc=1, device_id=(device,), device_id_type=pl.DeviceIdType.MESH
        )
    pl.semaphore_wait(barrier, len(devices))


def split3(value):
    high = value.astype(jnp.bfloat16).astype(jnp.float32)
    rest = value - high
    middle = rest.astype(jnp.bfloat16).astype(jnp.float32)
    return high, middle, rest - middle


def factors(pos, area, row_side):
    pos = pos - 0.5
    scale = (math.sqrt(TILE) / kernel_gain) / (area * area)
    norm = pos[0:1] * pos[0:1] + pos[1:2] * pos[1:2] + pos[2:3] * pos[2:3]
    one = jnp.ones_like(norm)
    rest = jnp.zeros((3, norm.shape[1]), jnp.float32)
    if row_side:
        parts = jnp.concatenate([norm + softening, one, -2.0 * pos, rest], axis=0) * scale
    else:
        parts = jnp.concatenate([one, norm, pos, rest], axis=0) * scale
    high, middle, low = split3(parts)
    if row_side:
        return jnp.concatenate([high, high, middle, middle, high, low], axis=0)
    return jnp.concatenate([high, middle, high, middle, low, high], axis=0)


def relax(field, source, conduct, step, lane):
    layer = jnp.zeros((1, 8, 128), jnp.float32)
    above = jnp.concatenate([field[1:], layer], axis=0)
    below = jnp.concatenate([layer, field[:-1]], axis=0)
    flat = field.reshape(LAYERS * 8, 128)
    right = jnp.where(lane < 127, pltpu.roll(flat, 127, axis=1).reshape(field.shape), 0.0)
    left = jnp.where(lane > 0, pltpu.roll(flat, 1, axis=1).reshape(field.shape), 0.0)
    ahead = pltpu.roll(field, 7, axis=1)
    behind = pltpu.roll(field, 1, axis=1)
    beside = (above + below) + (ahead + behind) + (right + left)
    applied = conduct * (6.0 * field - beside) + field
    return field + step * (source - applied)


def exchange_kernel(
    material_ref,
    scale_ref,
    list_ref,
    factor_ref,
    flux_far,
    field_far,
    source_far,
    pos_far,
    area_far,
    out_ref,
    top_ref,
    rows_ref,
    pt_ref,
    q_ref,
    flux_ref,
    field_ref,
    source_ref,
    pos_ref,
    area_ref,
    conduct_ref,
    slices,
    shared,
    stage,
    edge_field,
    edge_source,
    edge_conduct,
    halo_field,
    halo_source,
    halo_conduct,
    tops,
    pt_held,
    q_held,
    local,
    line_send,
    line_recv,
    edge_send,
    edge_recv,
    plane_send,
    plane_recv,
):
    me = lax.axis_index("dev")
    m, r = me // LINE, lax.rem(me, LINE)
    y, x = m // 4, lax.rem(m, 4)
    line = [LINE * m + lax.rem(r + k, LINE) for k in range(1, LINE)]
    after = lax.rem(me + 1, LINE * PLANE)
    before = lax.rem(me + LINE * PLANE - 1, LINE * PLANE)
    along_x = [LINE * (4 * y + lax.rem(x + k, 4)) + r for k in range(1, 4)]
    along_y = [LINE * (4 * lax.rem(y + k, 4) + x) + r for k in range(1, 4)]
    loads = [
        pltpu.make_async_copy(far, near, local.at[at])
        for at, (far, near) in enumerate(
            (
                (flux_far, flux_ref),
                (field_far, field_ref),
                (source_far, source_ref),
                (pos_far, pos_ref),
                (area_far, area_ref),
            )
        )
    ]
    for load in loads:
        load.start()
    partners = line + [after, before] + along_x + along_y
    barrier = pltpu.get_barrier_semaphore()
    for device in partners:
        pl.semaphore_signal(
            barrier, inc=1, device_id=(device,), device_id_type=pl.DeviceIdType.MESH
        )

    pairs = jnp.concatenate(
        [list_ref[...].astype(jnp.float32), jnp.zeros((2, 112), jnp.float32)], axis=1
    )
    pairs = jnp.concatenate([pairs, jnp.zeros((14, 128), jnp.float32)], axis=0)
    own_list = pltpu.roll(pairs, 16 * r, axis=1).astype(jnp.bfloat16)
    loads[0].wait()
    for s in range(LINE):
        slices[s, 0:32, :] = flux_ref[:, s * 128 : (s + 1) * 128].astype(jnp.bfloat16)
        slices[s, 32:48, :] = own_list
    for layer in range(LAYERS):
        kind = material_ref[layer]
        scale = jnp.float32(0.0)
        for known in range(4):
            scale = scale + jnp.where(kind == known, scale_ref[known], 0.0)
        conduct_ref[layer] = factor_ref[layer] * scale
    loads[1].wait()
    loads[2].wait()
    for side, (at, one) in enumerate(((2, 3), (0, 0))):
        edge_field[side] = field_ref[:, :, at : at + 2, :]
        edge_source[side] = source_ref[:, :, one, :]
        edge_conduct[side] = conduct_ref[:, one, :]
    pl.semaphore_wait(barrier, len(partners))

    edges = []
    for side, device in enumerate((after, before)):
        for which, (src, dst) in enumerate(
            ((edge_field, halo_field), (edge_source, halo_source), (edge_conduct, halo_conduct))
        ):
            edges.append(
                remote(
                    src.at[side], dst.at[side], edge_send, edge_recv, 3 * side + which, device
                )
            )
    copies = []
    for k in range(1, LINE):
        there = lax.rem(r + k, LINE)
        copies.append(
            remote(slices.at[there], shared.at[r], line_send, line_recv, k - 1, line[k - 1])
        )
    for copy in copies + edges:
        copy.start()
    shared[r] = slices[r]

    def row_block(step, carry):
        for u in range(8):
            half = step * 8 + u
            at = pl.multiple_of(half * 1024 + r * 128, 128)
            part = factors(pos_ref[:, pl.ds(at, 128)], area_ref[:, pl.ds(at, 128)], True)
            pt_held[half] = part.T.astype(jnp.bfloat16)
        return carry

    loads[3].wait()
    loads[4].wait()
    lax.fori_loop(0, 8, row_block, 0)

    for copy in copies:
        copy.wait()
    lists = jnp.zeros((16, 128), jnp.float32)
    for s in range(LINE):
        stage[32 * s : 32 * s + 32, :] = shared[s, 0:32, :]
        lists = lists + shared[s, 32:48, :].astype(jnp.float32)
    stage[256:272, :] = lists.astype(jnp.bfloat16)
    own = pltpu.make_async_copy(stage, rows_ref.at[y, x], local.at[5])
    own.start()
    one, two = slice(0, 128), slice(128, 272)
    near, far = [], []
    for k in range(3):
        near.append(
            remote(stage.at[one], rows_ref.at[y, x, one], plane_send, plane_recv, k, along_x[k])
        )
        near.append(
            remote(
                stage.at[two], rows_ref.at[y, x, two], plane_send, plane_recv, 3 + k, along_y[k]
            )
        )
        part = rows_ref.at[y, :, one]
        far.append(remote(part, part, plane_send, plane_recv, 6 + k, along_y[k]))
        part = rows_ref.at[:, x, two]
        far.append(remote(part, part, plane_send, plane_recv, 9 + k, along_x[k]))
    for copy in near:
        copy.start()

    lax.fori_loop(8, TILES // 4, row_block, 0)
    moves = [pltpu.make_async_copy(pt_held, pt_ref, local.at[6])]
    moves[0].start()
    own.wait()
    for copy in near:
        copy.wait()
    for copy in far:
        copy.start()

    for copy in edges:
        copy.wait()
    row = lax.broadcasted_iota(jnp.int32, (LAYERS, 8, 128), 1)
    lane = lax.broadcasted_iota(jnp.int32, (LAYERS, 8, 128), 2)
    real = ((row >= 2) | (me > 0)) & ((row < 6) | (me < LINE * PLANE - 1))
    pad = jnp.zeros((LAYERS, 1, 128), jnp.float32)
    conduct = jnp.concatenate(
        [pad, halo_conduct[0][:, None], conduct_ref[...], halo_conduct[1][:, None], pad], axis=1
    )
    step = relax_rate / (6.0 * conduct + 1.0)

    def one_load(load, carry):
        field = jnp.concatenate(
            [halo_field[0, load], field_ref[load], halo_field[1, load]], axis=1
        )
        field = jnp.where(real, field, 0.0)
        source = jnp.concatenate(
            [
                pad,
                halo_source[0, load][:, None],
                source_ref[load],
                halo_source[1, load][:, None],
                pad,
            ],
            axis=1,
        )
        field = jnp.where(real, relax(field, source, conduct, step, lane), 0.0)
        field = relax(field, source, conduct, step, lane)
        out_ref[load] = field[:, 2:6]
        tops[load] = field[LAYERS - 1, 2:6]
        return carry

    lax.fori_loop(0, 32, one_load, 0, unroll=4)
    for at in range(4):
        top_ref[at] = tops[:, at, :].astype(jnp.bfloat16)

    for j in range(4):
        for c in range(4):
            at = pl.multiple_of(m * COLS + j * TILE + c * 512, 512)
            part = factors(pos_ref[:, pl.ds(at, 512)], area_ref[:, pl.ds(at, 512)], False)
            q_held[j, :, c * 512 : (c + 1) * 512] = part.astype(jnp.bfloat16)
    moves.append(pltpu.make_async_copy(q_held, q_ref, local.at[7]))
    moves[1].start()
    for copy in far + moves:
        copy.wait()


def exchange(materials, scales, lists, factor, flux, field, source, pos, area):
    vmem = pl.BlockSpec(memory_space=pltpu.VMEM)
    hbm = pl.BlockSpec(memory_space=pltpu.HBM)
    smem = pl.BlockSpec(memory_space=pltpu.SMEM)
    row_shape, col_shape = (2 * TILES, 128, 48), (4, 48, TILE)
    f32, half = jnp.float32, jnp.bfloat16
    halo = [
        pltpu.VMEM((2, 32, LAYERS, 2, 128), f32),
        pltpu.VMEM((2, 32, LAYERS, 128), f32),
        pltpu.VMEM((2, LAYERS, 128), f32),
    ]
    return pl.pallas_call(
        exchange_kernel,
        out_shape=(
            jax.ShapeDtypeStruct(field.shape, f32),
            jax.ShapeDtypeStruct((4, 32, 128), half),
            jax.ShapeDtypeStruct((4, 4, 272, 128), half),
            jax.ShapeDtypeStruct(row_shape, half),
            jax.ShapeDtypeStruct(col_shape, half),
        ),
        in_specs=[smem, smem, vmem, vmem] + [hbm] * 5,
        out_specs=(vmem, vmem, hbm, hbm, hbm),
        scratch_shapes=[
            pltpu.VMEM(flux.shape, f32),
            pltpu.VMEM(field.shape, f32),
            pltpu.VMEM(source.shape, f32),
            pltpu.VMEM(pos.shape, f32),
            pltpu.VMEM(area.shape, f32),
            pltpu.VMEM(factor.shape, f32),
            pltpu.VMEM((LINE, 48, 128), half),
            pltpu.VMEM((LINE, 48, 128), half),
            pltpu.VMEM((272, 128), half),
        ]
        + halo
        + halo
        + [
            pltpu.VMEM((32, 4, 128), f32),
            pltpu.VMEM(row_shape, half),
            pltpu.VMEM(col_shape, half),
            pltpu.SemaphoreType.DMA((8,)),
            pltpu.SemaphoreType.DMA((LINE - 1,)),
            pltpu.SemaphoreType.DMA((LINE - 1,)),
            pltpu.SemaphoreType.DMA((6,)),
            pltpu.SemaphoreType.DMA((6,)),
            pltpu.SemaphoreType.DMA((12,)),
            pltpu.SemaphoreType.DMA((12,)),
        ],
        compiler_params=pltpu.CompilerParams(
            collective_id=0, has_side_effects=True, vmem_limit_bytes=WIDE
        ),
    )(materials, scales, lists, factor, flux, field, source, pos, area)


def finish_kernel(
    cell_ref, part_ref, table_ref, flux_ref, out_ref, table, landed, traces, load_sem, sends, recvs
):
    me = lax.axis_index("dev")
    m, r = me // LINE, lax.rem(me, LINE)
    load = pltpu.make_async_copy(table_ref, table, load_sem)
    load.start()
    line = [LINE * m + lax.rem(r + k, LINE) for k in range(1, LINE)]
    greet(line)
    copies = []
    for k in range(1, LINE):
        there = lax.rem(r + k, LINE)
        copy = remote(part_ref.at[there], landed.at[k - 1], sends, recvs, k - 1, line[k - 1])
        copy.start()
        copies.append(copy)
    load.wait()
    lane = lax.broadcasted_iota(jnp.int32, (32, 128), 1)

    def group(g, carry):
        def pick(step, held):
            for u in range(16):
                at = step * 16 + u
                cell = cell_ref[g * 128 + at]
                block = table[lax.shift_right_logical(cell, 7)].astype(jnp.float32)
                moved = pltpu.roll(block, (at - cell) & 127, axis=1)
                held = jnp.where(lane == at, moved, held)
            return held

        traces[g] = lax.fori_loop(0, 8, pick, jnp.zeros((32, 128), jnp.float32))
        return carry

    lax.fori_loop(0, 8, group, 0)
    for copy in copies:
        copy.wait()
    total = part_ref[r].astype(jnp.float32)
    for k in range(LINE - 1):
        total = total + landed[k].astype(jnp.float32)
    for g in range(8):
        at = slice(g * 128, (g + 1) * 128)
        out_ref[:, at] = flux_ref[:, at] + update_rate * (traces[g] - total[:, at])


def finish(cells, partial, table, flux_in):
    vmem = pl.BlockSpec(memory_space=pltpu.VMEM)
    return pl.pallas_call(
        finish_kernel,
        out_shape=jax.ShapeDtypeStruct(flux_in.shape, jnp.float32),
        in_specs=[
            pl.BlockSpec(memory_space=pltpu.SMEM),
            vmem,
            pl.BlockSpec(memory_space=pltpu.HBM),
            vmem,
        ],
        out_specs=vmem,
        scratch_shapes=[
            pltpu.VMEM(table.shape, jnp.bfloat16),
            pltpu.VMEM((LINE - 1, 32, 1024), jnp.bfloat16),
            pltpu.VMEM((8, 32, 128), jnp.float32),
            pltpu.SemaphoreType.DMA,
            pltpu.SemaphoreType.DMA((LINE - 1,)),
            pltpu.SemaphoreType.DMA((LINE - 1,)),
        ],
        compiler_params=pltpu.CompilerParams(
            collective_id=1, has_side_effects=True, vmem_limit_bytes=WIDE
        ),
    )(cells, partial, table, flux_in)


def body(
    field_in,
    source,
    cell_factor,
    layer_material,
    material_scale,
    panel_cell,
    panel_pos,
    panel_area,
    flux_in,
    pair_list,
):
    me = lax.axis_index("dev")
    m = me // LINE

    field_now, surface_top, rows, row_features, col_features = exchange(
        layer_material,
        material_scale,
        pair_list.T,
        cell_factor,
        flux_in,
        field_in,
        source,
        panel_pos,
        panel_area.reshape(1, -1),
    )
    table = lax.all_gather(surface_top, "dev", axis=0, tiled=True)
    rows = rows.reshape(PLANE, 272, 128)
    tile_ids = jnp.arange(TILES, dtype=jnp.bfloat16)[:, None]
    upper = (rows[:, 256].reshape(1, -1) == tile_ids).astype(jnp.bfloat16)
    lower = (rows[:, 257].reshape(1, -1) == tile_ids).astype(jnp.bfloat16)
    listed = lax.dot_general(
        upper, lower, (((1,), (1,)), ((), ())), preferred_element_type=jnp.float32
    )
    listed = (listed + listed.T > 0.0).astype(jnp.int32)
    mask = lax.dynamic_slice(listed, (4 * m, 0), (4, TILES)).reshape(-1)

    partial = apply_pairs(mask, rows, row_features.reshape(TILES, 256, 48), col_features)
    flux_out = finish(panel_cell, partial, table, flux_in)
    return (field_now, flux_out)


def solution(mesh):
    in_specs = (
        P(None, None, "dev", None),
        P(None, None, "dev", None),
        P(None, "dev", None),
        P(),
        P(),
        P("dev"),
        P(),
        P(),
        P(None, "dev"),
        P("dev", None),
    )
    out_specs = (P(None, None, "dev", None), P(None, "dev"))
    return jax.shard_map(body, mesh=mesh, in_specs=in_specs, out_specs=out_specs, check_vma=False)
```

```python
import math

import jax
import jax.numpy as jnp
from jax import lax
from jax.experimental import pallas as pl
from jax.experimental.pallas import tpu as pltpu
from jax.sharding import PartitionSpec as P

TILE = 2048
TILES = 64
LAYERS = 8
UNROLL = 4
LONG = 16
WIDE = (63 << 20) + (1 << 19)
LINE = 8
PLANE = 16
COLS = 4 * TILE

softening = 0.0004
relax_rate = 0.8
update_rate = 0.5
kernel_gain = 0.25


def pair_kernel(
    mask_ref, f_far, pt_far, q_far, o_ref, f_ref, pt_ref, q_ref, total_ref, held_ref, order_ref, sems
):
    loads = [
        pltpu.make_async_copy(far, near, sems.at[at])
        for at, (far, near) in enumerate(((f_far, f_ref), (pt_far, pt_ref), (q_far, q_ref)))
    ]
    for load in loads:
        load.start()
    order_ref[0] = 0

    def note(at, count):
        order_ref[count + 1] = at
        return count + mask_ref[at]

    count = lax.fori_loop(0, 4 * TILES, note, jnp.int32(0))
    for u in range(UNROLL + 1):
        order_ref[count + 1 + u] = 0
    total_ref[...] = jnp.zeros(total_ref.shape, jnp.float32)
    held_ref[1] = jnp.zeros((256, TILE), jnp.bfloat16)
    for load in loads:
        load.wait()

    def run(start, steps):
        for u in range(steps):
            t = start + u
            new, old = order_ref[t + 1], order_ref[t]
            valid = (t >= 1) & (t <= count)
            i = old % TILES
            at = pl.multiple_of((i % 4) * 64, 64)
            flux = jnp.concatenate(
                [f_ref[i // 4, pl.ds(at, 32), :], f_ref[i // 4, pl.ds(at + 32, 32), :]], axis=1
            )
            flux = jnp.where(valid, flux, jnp.zeros_like(flux))
            for c in range(4):
                columns = slice(c * 512, (c + 1) * 512)
                distance = jnp.dot(
                    pt_ref[new % TILES],
                    q_ref[new // TILES, :, columns],
                    preferred_element_type=jnp.float32,
                )
                held_ref[u % 2, :, columns] = lax.rsqrt(distance).astype(jnp.bfloat16)
                total_ref[old // TILES, :, columns] += jnp.dot(
                    flux, held_ref[1 - u % 2, :, columns], preferred_element_type=jnp.float32
                )

    def long_block(b, carry):
        run(b * LONG, LONG)
        return carry

    def short_block(b, carry):
        run(full * LONG + b * UNROLL, UNROLL)
        return carry

    full = (count + 1) // LONG
    lax.fori_loop(0, full, long_block, 0)
    lax.fori_loop(0, (count + UNROLL - full * LONG) // UNROLL, short_block, 0)
    for j in range(4):
        for c in range(2):
            o_ref[2 * j + c] = total_ref[j, :, c * 1024 : (c + 1) * 1024].astype(jnp.bfloat16)


def apply_pairs(mask, flux_rows, row_features, col_features):
    hbm = pl.BlockSpec(memory_space=pltpu.HBM)
    return pl.pallas_call(
        pair_kernel,
        out_shape=jax.ShapeDtypeStruct((LINE, 32, 1024), jnp.bfloat16),
        in_specs=[pl.BlockSpec(memory_space=pltpu.SMEM), hbm, hbm, hbm],
        out_specs=pl.BlockSpec(memory_space=pltpu.VMEM),
        scratch_shapes=[
            pltpu.VMEM(flux_rows.shape, jnp.bfloat16),
            pltpu.VMEM(row_features.shape, jnp.bfloat16),
            pltpu.VMEM(col_features.shape, jnp.bfloat16),
            pltpu.VMEM((4, 32, TILE), jnp.float32),
            pltpu.VMEM((2, 256, TILE), jnp.bfloat16),
            pltpu.SMEM((4 * TILES + UNROLL + 2,), jnp.int32),
            pltpu.SemaphoreType.DMA((3,)),
        ],
        compiler_params=pltpu.CompilerParams(vmem_limit_bytes=WIDE),
        cost_estimate=pl.CostEstimate(
            flops=100_000_000_000, bytes_accessed=8 << 20, transcendentals=0
        ),
    )(mask, flux_rows, row_features, col_features)


def remote(src, dst, sends, recvs, at, device):
    return pltpu.make_async_remote_copy(
        src_ref=src,
        dst_ref=dst,
        send_sem=sends.at[at],
        recv_sem=recvs.at[at],
        device_id=(device,),
        device_id_type=pl.DeviceIdType.MESH,
    )


def greet(devices):
    barrier = pltpu.get_barrier_semaphore()
    for device in devices:
        pl.semaphore_signal(
            barrier, inc=1, device_id=(device,), device_id_type=pl.DeviceIdType.MESH
        )
    pl.semaphore_wait(barrier, len(devices))


def split3(value):
    high = value.astype(jnp.bfloat16).astype(jnp.float32)
    rest = value - high
    middle = rest.astype(jnp.bfloat16).astype(jnp.float32)
    return high, middle, rest - middle


def factors(pos, area, row_side):
    pos = pos - 0.5
    scale = (math.sqrt(TILE) / kernel_gain) / (area * area)
    norm = pos[0:1] * pos[0:1] + pos[1:2] * pos[1:2] + pos[2:3] * pos[2:3]
    one = jnp.ones_like(norm)
    rest = jnp.zeros((3, norm.shape[1]), jnp.float32)
    if row_side:
        parts = jnp.concatenate([norm + softening, one, -2.0 * pos, rest], axis=0) * scale
    else:
        parts = jnp.concatenate([one, norm, pos, rest], axis=0) * scale
    high, middle, low = split3(parts)
    if row_side:
        return jnp.concatenate([high, high, middle, middle, high, low], axis=0)
    return jnp.concatenate([high, middle, high, middle, low, high], axis=0)


def relax(field, source, conduct, step, lane):
    layer = jnp.zeros((1, 8, 128), jnp.float32)
    above = jnp.concatenate([field[1:], layer], axis=0)
    below = jnp.concatenate([layer, field[:-1]], axis=0)
    flat = field.reshape(LAYERS * 8, 128)
    right = jnp.where(lane < 127, pltpu.roll(flat, 127, axis=1).reshape(field.shape), 0.0)
    left = jnp.where(lane > 0, pltpu.roll(flat, 1, axis=1).reshape(field.shape), 0.0)
    ahead = pltpu.roll(field, 7, axis=1)
    behind = pltpu.roll(field, 1, axis=1)
    beside = (above + below) + (ahead + behind) + (right + left)
    applied = conduct * (6.0 * field - beside) + field
    return field + step * (source - applied)


def exchange_kernel(
    material_ref,
    scale_ref,
    list_ref,
    factor_ref,
    flux_far,
    field_far,
    source_far,
    pos_far,
    area_far,
    out_ref,
    top_ref,
    rows_ref,
    pt_ref,
    q_ref,
    flux_ref,
    field_ref,
    source_ref,
    pos_ref,
    area_ref,
    conduct_ref,
    slices,
    shared,
    stage,
    edge_field,
    edge_source,
    edge_conduct,
    halo_field,
    halo_source,
    halo_conduct,
    tops,
    pt_held,
    q_held,
    local,
    line_send,
    line_recv,
    edge_send,
    edge_recv,
    plane_send,
    plane_recv,
):
    me = lax.axis_index("dev")
    m, r = me // LINE, lax.rem(me, LINE)
    y, x = m // 4, lax.rem(m, 4)
    line = [LINE * m + lax.rem(r + k, LINE) for k in range(1, LINE)]
    after = lax.rem(me + 1, LINE * PLANE)
    before = lax.rem(me + LINE * PLANE - 1, LINE * PLANE)
    along_x = [LINE * (4 * y + lax.rem(x + k, 4)) + r for k in range(1, 4)]
    along_y = [LINE * (4 * lax.rem(y + k, 4) + x) + r for k in range(1, 4)]
    loads = [
        pltpu.make_async_copy(far, near, local.at[at])
        for at, (far, near) in enumerate(
            (
                (flux_far, flux_ref),
                (field_far, field_ref),
                (source_far, source_ref),
                (pos_far, pos_ref),
                (area_far, area_ref),
            )
        )
    ]
    for load in loads:
        load.start()
    partners = line + [after, before] + along_x + along_y
    barrier = pltpu.get_barrier_semaphore()
    for device in partners:
        pl.semaphore_signal(
            barrier, inc=1, device_id=(device,), device_id_type=pl.DeviceIdType.MESH
        )

    pairs = jnp.concatenate(
        [list_ref[...].astype(jnp.float32), jnp.zeros((2, 112), jnp.float32)], axis=1
    )
    pairs = jnp.concatenate([pairs, jnp.zeros((14, 128), jnp.float32)], axis=0)
    own_list = pltpu.roll(pairs, 16 * r, axis=1).astype(jnp.bfloat16)
    loads[0].wait()
    for s in range(LINE):
        slices[s, 0:32, :] = flux_ref[:, s * 128 : (s + 1) * 128].astype(jnp.bfloat16)
        slices[s, 32:48, :] = own_list
    for layer in range(LAYERS):
        kind = material_ref[layer]
        scale = jnp.float32(0.0)
        for known in range(4):
            scale = scale + jnp.where(kind == known, scale_ref[known], 0.0)
        conduct_ref[layer] = factor_ref[layer] * scale
    loads[1].wait()
    loads[2].wait()
    for side, (at, one) in enumerate(((2, 3), (0, 0))):
        edge_field[side] = field_ref[:, :, at : at + 2, :]
        edge_source[side] = source_ref[:, :, one, :]
        edge_conduct[side] = conduct_ref[:, one, :]
    pl.semaphore_wait(barrier, len(partners))

    edges = []
    for side, device in enumerate((after, before)):
        for which, (src, dst) in enumerate(
            ((edge_field, halo_field), (edge_source, halo_source), (edge_conduct, halo_conduct))
        ):
            edges.append(
                remote(
                    src.at[side], dst.at[side], edge_send, edge_recv, 3 * side + which, device
                )
            )
    copies = []
    for k in range(1, LINE):
        there = lax.rem(r + k, LINE)
        copies.append(
            remote(slices.at[there], shared.at[r], line_send, line_recv, k - 1, line[k - 1])
        )
    for copy in copies + edges:
        copy.start()
    shared[r] = slices[r]

    def row_block(step, carry):
        for u in range(8):
            half = step * 8 + u
            at = pl.multiple_of(half * 1024 + r * 128, 128)
            part = factors(pos_ref[:, pl.ds(at, 128)], area_ref[:, pl.ds(at, 128)], True)
            pt_held[half] = part.T.astype(jnp.bfloat16)
        return carry

    loads[3].wait()
    loads[4].wait()
    lax.fori_loop(0, 8, row_block, 0)

    for copy in copies:
        copy.wait()
    lists = jnp.zeros((16, 128), jnp.float32)
    for s in range(LINE):
        stage[32 * s : 32 * s + 32, :] = shared[s, 0:32, :]
        lists = lists + shared[s, 32:48, :].astype(jnp.float32)
    stage[256:272, :] = lists.astype(jnp.bfloat16)
    own = pltpu.make_async_copy(stage, rows_ref.at[y, x], local.at[5])
    own.start()
    one, two = slice(0, 128), slice(128, 272)
    near, far = [], []
    for k in range(3):
        near.append(
            remote(stage.at[one], rows_ref.at[y, x, one], plane_send, plane_recv, k, along_x[k])
        )
        near.append(
            remote(
                stage.at[two], rows_ref.at[y, x, two], plane_send, plane_recv, 3 + k, along_y[k]
            )
        )
        part = rows_ref.at[y, :, one]
        far.append(remote(part, part, plane_send, plane_recv, 6 + k, along_y[k]))
        part = rows_ref.at[:, x, two]
        far.append(remote(part, part, plane_send, plane_recv, 9 + k, along_x[k]))
    for copy in near:
        copy.start()

    lax.fori_loop(8, TILES // 4, row_block, 0)
    moves = [pltpu.make_async_copy(pt_held, pt_ref, local.at[6])]
    moves[0].start()
    own.wait()
    for copy in near:
        copy.wait()
    for copy in far:
        copy.start()

    for copy in edges:
        copy.wait()
    row = lax.broadcasted_iota(jnp.int32, (LAYERS, 8, 128), 1)
    lane = lax.broadcasted_iota(jnp.int32, (LAYERS, 8, 128), 2)
    real = ((row >= 2) | (me > 0)) & ((row < 6) | (me < LINE * PLANE - 1))
    pad = jnp.zeros((LAYERS, 1, 128), jnp.float32)
    conduct = jnp.concatenate(
        [pad, halo_conduct[0][:, None], conduct_ref[...], halo_conduct[1][:, None], pad], axis=1
    )
    step = relax_rate / (6.0 * conduct + 1.0)

    def one_load(load, carry):
        field = jnp.concatenate(
            [halo_field[0, load], field_ref[load], halo_field[1, load]], axis=1
        )
        field = jnp.where(real, field, 0.0)
        source = jnp.concatenate(
            [
                pad,
                halo_source[0, load][:, None],
                source_ref[load],
                halo_source[1, load][:, None],
                pad,
            ],
            axis=1,
        )
        field = jnp.where(real, relax(field, source, conduct, step, lane), 0.0)
        field = relax(field, source, conduct, step, lane)
        out_ref[load] = field[:, 2:6]
        tops[load] = field[LAYERS - 1, 2:6]
        return carry

    lax.fori_loop(0, 32, one_load, 0, unroll=4)
    for at in range(4):
        top_ref[at] = tops[:, at, :].astype(jnp.bfloat16)

    for j in range(4):
        for c in range(4):
            at = pl.multiple_of(m * COLS + j * TILE + c * 512, 512)
            part = factors(pos_ref[:, pl.ds(at, 512)], area_ref[:, pl.ds(at, 512)], False)
            q_held[j, :, c * 512 : (c + 1) * 512] = part.astype(jnp.bfloat16)
    moves.append(pltpu.make_async_copy(q_held, q_ref, local.at[7]))
    moves[1].start()
    for copy in far + moves:
        copy.wait()


def exchange(materials, scales, lists, factor, flux, field, source, pos, area):
    vmem = pl.BlockSpec(memory_space=pltpu.VMEM)
    hbm = pl.BlockSpec(memory_space=pltpu.HBM)
    smem = pl.BlockSpec(memory_space=pltpu.SMEM)
    row_shape, col_shape = (2 * TILES, 128, 48), (4, 48, TILE)
    f32, half = jnp.float32, jnp.bfloat16
    halo = [
        pltpu.VMEM((2, 32, LAYERS, 2, 128), f32),
        pltpu.VMEM((2, 32, LAYERS, 128), f32),
        pltpu.VMEM((2, LAYERS, 128), f32),
    ]
    return pl.pallas_call(
        exchange_kernel,
        out_shape=(
            jax.ShapeDtypeStruct(field.shape, f32),
            jax.ShapeDtypeStruct((4, 32, 128), half),
            jax.ShapeDtypeStruct((4, 4, 272, 128), half),
            jax.ShapeDtypeStruct(row_shape, half),
            jax.ShapeDtypeStruct(col_shape, half),
        ),
        in_specs=[smem, smem, vmem, vmem] + [hbm] * 5,
        out_specs=(vmem, vmem, hbm, hbm, hbm),
        scratch_shapes=[
            pltpu.VMEM(flux.shape, f32),
            pltpu.VMEM(field.shape, f32),
            pltpu.VMEM(source.shape, f32),
            pltpu.VMEM(pos.shape, f32),
            pltpu.VMEM(area.shape, f32),
            pltpu.VMEM(factor.shape, f32),
            pltpu.VMEM((LINE, 48, 128), half),
            pltpu.VMEM((LINE, 48, 128), half),
            pltpu.VMEM((272, 128), half),
        ]
        + halo
        + halo
        + [
            pltpu.VMEM((32, 4, 128), f32),
            pltpu.VMEM(row_shape, half),
            pltpu.VMEM(col_shape, half),
            pltpu.SemaphoreType.DMA((8,)),
            pltpu.SemaphoreType.DMA((LINE - 1,)),
            pltpu.SemaphoreType.DMA((LINE - 1,)),
            pltpu.SemaphoreType.DMA((6,)),
            pltpu.SemaphoreType.DMA((6,)),
            pltpu.SemaphoreType.DMA((12,)),
            pltpu.SemaphoreType.DMA((12,)),
        ],
        compiler_params=pltpu.CompilerParams(
            collective_id=0, has_side_effects=True, vmem_limit_bytes=WIDE
        ),
    )(materials, scales, lists, factor, flux, field, source, pos, area)


def finish_kernel(
    cell_ref, part_ref, table_ref, flux_ref, out_ref, table, landed, traces, load_sem, sends, recvs
):
    me = lax.axis_index("dev")
    m, r = me // LINE, lax.rem(me, LINE)
    load = pltpu.make_async_copy(table_ref, table, load_sem)
    load.start()
    line = [LINE * m + lax.rem(r + k, LINE) for k in range(1, LINE)]
    greet(line)
    copies = []
    for k in range(1, LINE):
        there = lax.rem(r + k, LINE)
        copy = remote(part_ref.at[there], landed.at[k - 1], sends, recvs, k - 1, line[k - 1])
        copy.start()
        copies.append(copy)
    load.wait()
    lane = lax.broadcasted_iota(jnp.int32, (32, 128), 1)

    def group(g, carry):
        def pick(step, held):
            held = list(held)
            for u in range(64):
                at = step * 64 + u
                cell = cell_ref[g * 128 + at]
                block = table[lax.shift_right_logical(cell, 7)].astype(jnp.float32)
                moved = pltpu.roll(block, (at - cell) & 127, axis=1)
                held[u % 4] = jnp.where(lane == at, moved, held[u % 4])
            return tuple(held)

        held = lax.fori_loop(0, 2, pick, (jnp.zeros((32, 128), jnp.float32),) * 4)
        traces[g] = (held[0] + held[1]) + (held[2] + held[3])
        return carry

    lax.fori_loop(0, 8, group, 0)
    for copy in copies:
        copy.wait()
    total = part_ref[r].astype(jnp.float32)
    for k in range(LINE - 1):
        total = total + landed[k].astype(jnp.float32)
    for g in range(8):
        at = slice(g * 128, (g + 1) * 128)
        out_ref[:, at] = flux_ref[:, at] + update_rate * (traces[g] - total[:, at])


def finish(cells, partial, table, flux_in):
    vmem = pl.BlockSpec(memory_space=pltpu.VMEM)
    return pl.pallas_call(
        finish_kernel,
        out_shape=jax.ShapeDtypeStruct(flux_in.shape, jnp.float32),
        in_specs=[
            pl.BlockSpec(memory_space=pltpu.SMEM),
            vmem,
            pl.BlockSpec(memory_space=pltpu.HBM),
            vmem,
        ],
        out_specs=vmem,
        scratch_shapes=[
            pltpu.VMEM(table.shape, jnp.bfloat16),
            pltpu.VMEM((LINE - 1, 32, 1024), jnp.bfloat16),
            pltpu.VMEM((8, 32, 128), jnp.float32),
            pltpu.SemaphoreType.DMA,
            pltpu.SemaphoreType.DMA((LINE - 1,)),
            pltpu.SemaphoreType.DMA((LINE - 1,)),
        ],
        compiler_params=pltpu.CompilerParams(
            collective_id=1, has_side_effects=True, vmem_limit_bytes=WIDE
        ),
    )(cells, partial, table, flux_in)


def body(
    field_in,
    source,
    cell_factor,
    layer_material,
    material_scale,
    panel_cell,
    panel_pos,
    panel_area,
    flux_in,
    pair_list,
):
    me = lax.axis_index("dev")
    m = me // LINE

    field_now, surface_top, rows, row_features, col_features = exchange(
        layer_material,
        material_scale,
        pair_list.T,
        cell_factor,
        flux_in,
        field_in,
        source,
        panel_pos,
        panel_area.reshape(1, -1),
    )
    table = lax.all_gather(surface_top, "dev", axis=0, tiled=True)
    rows = rows.reshape(PLANE, 272, 128)
    tile_ids = jnp.arange(TILES, dtype=jnp.bfloat16)[:, None]
    upper = (rows[:, 256].reshape(1, -1) == tile_ids).astype(jnp.bfloat16)
    lower = (rows[:, 257].reshape(1, -1) == tile_ids).astype(jnp.bfloat16)
    listed = lax.dot_general(
        upper, lower, (((1,), (1,)), ((), ())), preferred_element_type=jnp.float32
    )
    listed = (listed + listed.T > 0.0).astype(jnp.int32)
    mask = lax.dynamic_slice(listed, (4 * m, 0), (4, TILES)).reshape(-1)

    partial = apply_pairs(mask, rows, row_features.reshape(TILES, 256, 48), col_features)
    field_now = jnp.where(me >= 0, field_now, 0.0)
    partial, field_now = lax.optimization_barrier((partial, field_now))
    flux_out = finish(panel_cell, partial, table, flux_in)
    return (field_now, flux_out)


def solution(mesh):
    in_specs = (
        P(None, None, "dev", None),
        P(None, None, "dev", None),
        P(None, "dev", None),
        P(),
        P(),
        P("dev"),
        P(),
        P(),
        P(None, "dev"),
        P("dev", None),
    )
    out_specs = (P(None, None, "dev", None), P(None, "dev"))
    return jax.shard_map(body, mesh=mesh, in_specs=in_specs, out_specs=out_specs, check_vma=False)
```

```python
import math

import jax
import jax.numpy as jnp
from jax import lax
from jax.experimental import pallas as pl
from jax.experimental.pallas import tpu as pltpu
from jax.sharding import PartitionSpec as P

TILE = 2048
TILES = 64
LAYERS = 8
UNROLL = 4
LONG = 16
WIDE = (63 << 20) + (1 << 19)
LINE = 8
PLANE = 16
COLS = 4 * TILE

softening = 0.0004
relax_rate = 0.8
update_rate = 0.5
kernel_gain = 0.25


def pair_kernel(
    mask_ref, f_far, pt_far, q_far, o_ref, f_ref, pt_ref, q_ref, total_ref, held_ref, order_ref, sems
):
    loads = [
        pltpu.make_async_copy(far, near, sems.at[at])
        for at, (far, near) in enumerate(((f_far, f_ref), (pt_far, pt_ref), (q_far, q_ref)))
    ]
    for load in loads:
        load.start()
    order_ref[0] = 0

    def note(at, count):
        order_ref[count + 1] = at
        return count + mask_ref[at]

    count = lax.fori_loop(0, 4 * TILES, note, jnp.int32(0))
    for u in range(UNROLL + 1):
        order_ref[count + 1 + u] = 0
    total_ref[...] = jnp.zeros(total_ref.shape, jnp.float32)
    held_ref[1] = jnp.zeros((256, TILE), jnp.bfloat16)
    for load in loads:
        load.wait()

    def run(start, steps):
        for u in range(steps):
            t = start + u
            new, old = order_ref[t + 1], order_ref[t]
            valid = (t >= 1) & (t <= count)
            i = old % TILES
            at = pl.multiple_of((i % 4) * 64, 64)
            flux = jnp.concatenate(
                [f_ref[i // 4, pl.ds(at, 32), :], f_ref[i // 4, pl.ds(at + 32, 32), :]], axis=1
            )
            flux = jnp.where(valid, flux, jnp.zeros_like(flux))
            for c in range(4):
                columns = slice(c * 512, (c + 1) * 512)
                distance = jnp.dot(
                    pt_ref[new % TILES],
                    q_ref[new // TILES, :, columns],
                    preferred_element_type=jnp.float32,
                )
                held_ref[u % 2, :, columns] = lax.rsqrt(distance).astype(jnp.bfloat16)
                total_ref[old // TILES, :, columns] += jnp.dot(
                    flux, held_ref[1 - u % 2, :, columns], preferred_element_type=jnp.float32
                )

    def long_block(b, carry):
        run(b * LONG, LONG)
        return carry

    def short_block(b, carry):
        run(full * LONG + b * UNROLL, UNROLL)
        return carry

    full = (count + 1) // LONG
    lax.fori_loop(0, full, long_block, 0)
    lax.fori_loop(0, (count + UNROLL - full * LONG) // UNROLL, short_block, 0)
    for j in range(4):
        for c in range(2):
            o_ref[2 * j + c] = total_ref[j, :, c * 1024 : (c + 1) * 1024].astype(jnp.bfloat16)


def apply_pairs(mask, flux_rows, row_features, col_features):
    hbm = pl.BlockSpec(memory_space=pltpu.HBM)
    return pl.pallas_call(
        pair_kernel,
        out_shape=jax.ShapeDtypeStruct((LINE, 32, 1024), jnp.bfloat16),
        in_specs=[pl.BlockSpec(memory_space=pltpu.SMEM), hbm, hbm, hbm],
        out_specs=pl.BlockSpec(memory_space=pltpu.VMEM),
        scratch_shapes=[
            pltpu.VMEM(flux_rows.shape, jnp.bfloat16),
            pltpu.VMEM(row_features.shape, jnp.bfloat16),
            pltpu.VMEM(col_features.shape, jnp.bfloat16),
            pltpu.VMEM((4, 32, TILE), jnp.float32),
            pltpu.VMEM((2, 256, TILE), jnp.bfloat16),
            pltpu.SMEM((4 * TILES + UNROLL + 2,), jnp.int32),
            pltpu.SemaphoreType.DMA((3,)),
        ],
        compiler_params=pltpu.CompilerParams(vmem_limit_bytes=WIDE),
        cost_estimate=pl.CostEstimate(
            flops=100_000_000_000, bytes_accessed=8 << 20, transcendentals=0
        ),
    )(mask, flux_rows, row_features, col_features)


def remote(src, dst, sends, recvs, at, device):
    return pltpu.make_async_remote_copy(
        src_ref=src,
        dst_ref=dst,
        send_sem=sends.at[at],
        recv_sem=recvs.at[at],
        device_id=(device,),
        device_id_type=pl.DeviceIdType.MESH,
    )


def greet(devices):
    barrier = pltpu.get_barrier_semaphore()
    for device in devices:
        pl.semaphore_signal(
            barrier, inc=1, device_id=(device,), device_id_type=pl.DeviceIdType.MESH
        )
    pl.semaphore_wait(barrier, len(devices))


def split3(value):
    high = value.astype(jnp.bfloat16).astype(jnp.float32)
    rest = value - high
    middle = rest.astype(jnp.bfloat16).astype(jnp.float32)
    return high, middle, rest - middle


def factors(pos, area, row_side):
    pos = pos - 0.5
    scale = (math.sqrt(TILE) / kernel_gain) / (area * area)
    norm = pos[0:1] * pos[0:1] + pos[1:2] * pos[1:2] + pos[2:3] * pos[2:3]
    one = jnp.ones_like(norm)
    rest = jnp.zeros((3, norm.shape[1]), jnp.float32)
    if row_side:
        parts = jnp.concatenate([norm + softening, one, -2.0 * pos, rest], axis=0) * scale
    else:
        parts = jnp.concatenate([one, norm, pos, rest], axis=0) * scale
    high, middle, low = split3(parts)
    if row_side:
        return jnp.concatenate([high, high, middle, middle, high, low], axis=0)
    return jnp.concatenate([high, middle, high, middle, low, high], axis=0)


def relax(field, source, conduct, step, lane):
    layer = jnp.zeros((1, 8, 128), jnp.float32)
    above = jnp.concatenate([field[1:], layer], axis=0)
    below = jnp.concatenate([layer, field[:-1]], axis=0)
    flat = field.reshape(LAYERS * 8, 128)
    right = jnp.where(lane < 127, pltpu.roll(flat, 127, axis=1).reshape(field.shape), 0.0)
    left = jnp.where(lane > 0, pltpu.roll(flat, 1, axis=1).reshape(field.shape), 0.0)
    ahead = pltpu.roll(field, 7, axis=1)
    behind = pltpu.roll(field, 1, axis=1)
    beside = (above + below) + (ahead + behind) + (right + left)
    applied = conduct * (6.0 * field - beside) + field
    return field + step * (source - applied)


def exchange_kernel(
    material_ref,
    scale_ref,
    list_ref,
    factor_ref,
    flux_far,
    field_far,
    source_far,
    pos_far,
    area_far,
    out_ref,
    top_ref,
    rows_ref,
    pt_ref,
    q_ref,
    flux_ref,
    field_ref,
    source_ref,
    pos_ref,
    area_ref,
    conduct_ref,
    slices,
    shared,
    stage,
    edge_field,
    edge_source,
    edge_conduct,
    halo_field,
    halo_source,
    halo_conduct,
    tops,
    pt_held,
    q_held,
    local,
    line_send,
    line_recv,
    edge_send,
    edge_recv,
    plane_send,
    plane_recv,
):
    me = lax.axis_index("dev")
    m, r = me // LINE, lax.rem(me, LINE)
    y, x = m // 4, lax.rem(m, 4)
    line = [LINE * m + lax.rem(r + k, LINE) for k in range(1, LINE)]
    after = lax.rem(me + 1, LINE * PLANE)
    before = lax.rem(me + LINE * PLANE - 1, LINE * PLANE)
    along_x = [LINE * (4 * y + lax.rem(x + k, 4)) + r for k in range(1, 4)]
    along_y = [LINE * (4 * lax.rem(y + k, 4) + x) + r for k in range(1, 4)]
    loads = [
        pltpu.make_async_copy(far, near, local.at[at])
        for at, (far, near) in enumerate(
            (
                (flux_far, flux_ref),
                (field_far, field_ref),
                (source_far, source_ref),
                (pos_far, pos_ref),
                (area_far, area_ref),
            )
        )
    ]
    for load in loads:
        load.start()
    partners = line + [after, before] + along_x + along_y
    barrier = pltpu.get_barrier_semaphore()
    for device in partners:
        pl.semaphore_signal(
            barrier, inc=1, device_id=(device,), device_id_type=pl.DeviceIdType.MESH
        )

    pairs = jnp.concatenate(
        [list_ref[...].astype(jnp.float32), jnp.zeros((2, 112), jnp.float32)], axis=1
    )
    pairs = jnp.concatenate([pairs, jnp.zeros((14, 128), jnp.float32)], axis=0)
    own_list = pltpu.roll(pairs, 16 * r, axis=1).astype(jnp.bfloat16)
    loads[0].wait()
    for s in range(LINE):
        slices[s, 0:32, :] = flux_ref[:, s * 128 : (s + 1) * 128].astype(jnp.bfloat16)
        slices[s, 32:48, :] = own_list
    for layer in range(LAYERS):
        kind = material_ref[layer]
        scale = jnp.float32(0.0)
        for known in range(4):
            scale = scale + jnp.where(kind == known, scale_ref[known], 0.0)
        conduct_ref[layer] = factor_ref[layer] * scale
    loads[1].wait()
    loads[2].wait()
    for side, (at, one) in enumerate(((2, 3), (0, 0))):
        edge_field[side] = field_ref[:, :, at : at + 2, :]
        edge_source[side] = source_ref[:, :, one, :]
        edge_conduct[side] = conduct_ref[:, one, :]
    pl.semaphore_wait(barrier, len(partners))

    edges = []
    for side, device in enumerate((after, before)):
        for which, (src, dst) in enumerate(
            ((edge_field, halo_field), (edge_source, halo_source), (edge_conduct, halo_conduct))
        ):
            edges.append(
                remote(
                    src.at[side], dst.at[side], edge_send, edge_recv, 3 * side + which, device
                )
            )
    copies = []
    for k in range(1, LINE):
        there = lax.rem(r + k, LINE)
        copies.append(
            remote(slices.at[there], shared.at[r], line_send, line_recv, k - 1, line[k - 1])
        )
    for copy in copies + edges:
        copy.start()
    shared[r] = slices[r]

    def row_block(step, carry):
        for u in range(8):
            half = step * 8 + u
            at = pl.multiple_of(half * 1024 + r * 128, 128)
            part = factors(pos_ref[:, pl.ds(at, 128)], area_ref[:, pl.ds(at, 128)], True)
            pt_held[half] = part.T.astype(jnp.bfloat16)
        return carry

    loads[3].wait()
    loads[4].wait()
    lax.fori_loop(0, 8, row_block, 0)

    for copy in copies:
        copy.wait()
    lists = jnp.zeros((16, 128), jnp.float32)
    for s in range(LINE):
        stage[32 * s : 32 * s + 32, :] = shared[s, 0:32, :]
        lists = lists + shared[s, 32:48, :].astype(jnp.float32)
    stage[256:272, :] = lists.astype(jnp.bfloat16)
    own = pltpu.make_async_copy(stage, rows_ref.at[y, x], local.at[5])
    own.start()
    one, two = slice(0, 128), slice(128, 272)
    near, far = [], []
    for k in range(3):
        near.append(
            remote(stage.at[one], rows_ref.at[y, x, one], plane_send, plane_recv, k, along_x[k])
        )
        near.append(
            remote(
                stage.at[two], rows_ref.at[y, x, two], plane_send, plane_recv, 3 + k, along_y[k]
            )
        )
        part = rows_ref.at[y, :, one]
        far.append(remote(part, part, plane_send, plane_recv, 6 + k, along_y[k]))
        part = rows_ref.at[:, x, two]
        far.append(remote(part, part, plane_send, plane_recv, 9 + k, along_x[k]))
    for copy in near:
        copy.start()

    lax.fori_loop(8, TILES // 4, row_block, 0)
    moves = [pltpu.make_async_copy(pt_held, pt_ref, local.at[6])]
    moves[0].start()
    for j in range(4):
        for c in range(4):
            at = pl.multiple_of(m * COLS + j * TILE + c * 512, 512)
            part = factors(pos_ref[:, pl.ds(at, 512)], area_ref[:, pl.ds(at, 512)], False)
            q_held[j, :, c * 512 : (c + 1) * 512] = part.astype(jnp.bfloat16)
    moves.append(pltpu.make_async_copy(q_held, q_ref, local.at[7]))
    moves[1].start()
    own.wait()
    for copy in near:
        copy.wait()
    for copy in far:
        copy.start()

    for copy in edges:
        copy.wait()
    row = lax.broadcasted_iota(jnp.int32, (LAYERS, 8, 128), 1)
    lane = lax.broadcasted_iota(jnp.int32, (LAYERS, 8, 128), 2)
    real = ((row >= 2) | (me > 0)) & ((row < 6) | (me < LINE * PLANE - 1))
    pad = jnp.zeros((LAYERS, 1, 128), jnp.float32)
    conduct = jnp.concatenate(
        [pad, halo_conduct[0][:, None], conduct_ref[...], halo_conduct[1][:, None], pad], axis=1
    )
    step = relax_rate / (6.0 * conduct + 1.0)

    def one_load(load, carry):
        field = jnp.concatenate(
            [halo_field[0, load], field_ref[load], halo_field[1, load]], axis=1
        )
        field = jnp.where(real, field, 0.0)
        source = jnp.concatenate(
            [
                pad,
                halo_source[0, load][:, None],
                source_ref[load],
                halo_source[1, load][:, None],
                pad,
            ],
            axis=1,
        )
        field = jnp.where(real, relax(field, source, conduct, step, lane), 0.0)
        field = relax(field, source, conduct, step, lane)
        out_ref[load] = field[:, 2:6]
        tops[load] = field[LAYERS - 1, 2:6]
        return carry

    lax.fori_loop(0, 32, one_load, 0, unroll=4)
    for at in range(4):
        top_ref[at] = tops[:, at, :].astype(jnp.bfloat16)

    for copy in far + moves:
        copy.wait()


def exchange(materials, scales, lists, factor, flux, field, source, pos, area):
    vmem = pl.BlockSpec(memory_space=pltpu.VMEM)
    hbm = pl.BlockSpec(memory_space=pltpu.HBM)
    smem = pl.BlockSpec(memory_space=pltpu.SMEM)
    row_shape, col_shape = (2 * TILES, 128, 48), (4, 48, TILE)
    f32, half = jnp.float32, jnp.bfloat16
    halo = [
        pltpu.VMEM((2, 32, LAYERS, 2, 128), f32),
        pltpu.VMEM((2, 32, LAYERS, 128), f32),
        pltpu.VMEM((2, LAYERS, 128), f32),
    ]
    return pl.pallas_call(
        exchange_kernel,
        out_shape=(
            jax.ShapeDtypeStruct(field.shape, f32),
            jax.ShapeDtypeStruct((4, 32, 128), half),
            jax.ShapeDtypeStruct((4, 4, 272, 128), half),
            jax.ShapeDtypeStruct(row_shape, half),
            jax.ShapeDtypeStruct(col_shape, half),
        ),
        in_specs=[smem, smem, vmem, vmem] + [hbm] * 5,
        out_specs=(vmem, vmem, hbm, hbm, hbm),
        scratch_shapes=[
            pltpu.VMEM(flux.shape, f32),
            pltpu.VMEM(field.shape, f32),
            pltpu.VMEM(source.shape, f32),
            pltpu.VMEM(pos.shape, f32),
            pltpu.VMEM(area.shape, f32),
            pltpu.VMEM(factor.shape, f32),
            pltpu.VMEM((LINE, 48, 128), half),
            pltpu.VMEM((LINE, 48, 128), half),
            pltpu.VMEM((272, 128), half),
        ]
        + halo
        + halo
        + [
            pltpu.VMEM((32, 4, 128), f32),
            pltpu.VMEM(row_shape, half),
            pltpu.VMEM(col_shape, half),
            pltpu.SemaphoreType.DMA((8,)),
            pltpu.SemaphoreType.DMA((LINE - 1,)),
            pltpu.SemaphoreType.DMA((LINE - 1,)),
            pltpu.SemaphoreType.DMA((6,)),
            pltpu.SemaphoreType.DMA((6,)),
            pltpu.SemaphoreType.DMA((12,)),
            pltpu.SemaphoreType.DMA((12,)),
        ],
        compiler_params=pltpu.CompilerParams(
            collective_id=0, has_side_effects=True, vmem_limit_bytes=WIDE
        ),
    )(materials, scales, lists, factor, flux, field, source, pos, area)


def finish_kernel(
    cell_ref, part_ref, table_ref, flux_ref, out_ref, table, landed, traces, load_sem, sends, recvs
):
    me = lax.axis_index("dev")
    m, r = me // LINE, lax.rem(me, LINE)
    load = pltpu.make_async_copy(table_ref, table, load_sem)
    load.start()
    line = [LINE * m + lax.rem(r + k, LINE) for k in range(1, LINE)]
    greet(line)
    copies = []
    for k in range(1, LINE):
        there = lax.rem(r + k, LINE)
        copy = remote(part_ref.at[there], landed.at[k - 1], sends, recvs, k - 1, line[k - 1])
        copy.start()
        copies.append(copy)
    load.wait()
    lane = lax.broadcasted_iota(jnp.int32, (32, 128), 1)

    def group(g, carry):
        def pick(step, held):
            held = list(held)
            for u in range(64):
                at = step * 64 + u
                cell = cell_ref[g * 128 + at]
                block = table[lax.shift_right_logical(cell, 7)].astype(jnp.float32)
                moved = pltpu.roll(block, (at - cell) & 127, axis=1)
                held[u % 4] = jnp.where(lane == at, moved, held[u % 4])
            return tuple(held)

        held = lax.fori_loop(0, 2, pick, (jnp.zeros((32, 128), jnp.float32),) * 4)
        traces[g] = (held[0] + held[1]) + (held[2] + held[3])
        return carry

    lax.fori_loop(0, 8, group, 0)
    for copy in copies:
        copy.wait()
    total = part_ref[r].astype(jnp.float32)
    for k in range(LINE - 1):
        total = total + landed[k].astype(jnp.float32)
    for g in range(8):
        at = slice(g * 128, (g + 1) * 128)
        out_ref[:, at] = flux_ref[:, at] + update_rate * (traces[g] - total[:, at])


def finish(cells, partial, table, flux_in):
    vmem = pl.BlockSpec(memory_space=pltpu.VMEM)
    return pl.pallas_call(
        finish_kernel,
        out_shape=jax.ShapeDtypeStruct(flux_in.shape, jnp.float32),
        in_specs=[
            pl.BlockSpec(memory_space=pltpu.SMEM),
            vmem,
            pl.BlockSpec(memory_space=pltpu.HBM),
            vmem,
        ],
        out_specs=vmem,
        scratch_shapes=[
            pltpu.VMEM(table.shape, jnp.bfloat16),
            pltpu.VMEM((LINE - 1, 32, 1024), jnp.bfloat16),
            pltpu.VMEM((8, 32, 128), jnp.float32),
            pltpu.SemaphoreType.DMA,
            pltpu.SemaphoreType.DMA((LINE - 1,)),
            pltpu.SemaphoreType.DMA((LINE - 1,)),
        ],
        compiler_params=pltpu.CompilerParams(
            collective_id=1, has_side_effects=True, vmem_limit_bytes=WIDE
        ),
    )(cells, partial, table, flux_in)


def body(
    field_in,
    source,
    cell_factor,
    layer_material,
    material_scale,
    panel_cell,
    panel_pos,
    panel_area,
    flux_in,
    pair_list,
):
    me = lax.axis_index("dev")
    m = me // LINE

    field_now, surface_top, rows, row_features, col_features = exchange(
        layer_material,
        material_scale,
        pair_list.T,
        cell_factor,
        flux_in,
        field_in,
        source,
        panel_pos,
        panel_area.reshape(1, -1),
    )
    table = lax.all_gather(surface_top, "dev", axis=0, tiled=True)
    rows = rows.reshape(PLANE, 272, 128)
    tile_ids = jnp.arange(TILES, dtype=jnp.bfloat16)[:, None]
    upper = (rows[:, 256].reshape(1, -1) == tile_ids).astype(jnp.bfloat16)
    lower = (rows[:, 257].reshape(1, -1) == tile_ids).astype(jnp.bfloat16)
    listed = lax.dot_general(
        upper, lower, (((1,), (1,)), ((), ())), preferred_element_type=jnp.float32
    )
    listed = (listed + listed.T > 0.0).astype(jnp.int32)
    mask = lax.dynamic_slice(listed, (4 * m, 0), (4, TILES)).reshape(-1)

    partial = apply_pairs(mask, rows, row_features.reshape(TILES, 256, 48), col_features)
    partial, field_now = lax.optimization_barrier((partial, field_now))
    field_now = jnp.where(me >= 0, field_now, 0.0)
    partial, field_now = lax.optimization_barrier((partial, field_now))
    flux_out = finish(panel_cell, partial, table, flux_in)
    return (field_now, flux_out)


def solution(mesh):
    in_specs = (
        P(None, None, "dev", None),
        P(None, None, "dev", None),
        P(None, "dev", None),
        P(),
        P(),
        P("dev"),
        P(),
        P(),
        P(None, "dev"),
        P("dev", None),
    )
    out_specs = (P(None, None, "dev", None), P(None, "dev"))
    return jax.shard_map(body, mesh=mesh, in_specs=in_specs, out_specs=out_specs, check_vma=False)
```

```python
import math

import jax
import jax.numpy as jnp
from jax import lax
from jax.experimental import pallas as pl
from jax.experimental.pallas import tpu as pltpu
from jax.sharding import PartitionSpec as P

TILE = 2048
TILES = 64
LAYERS = 8
UNROLL = 4
LONG = 16
WIDE = (63 << 20) + (1 << 19)
LINE = 8
PLANE = 16
COLS = 4 * TILE

softening = 0.0004
relax_rate = 0.8
update_rate = 0.5
kernel_gain = 0.25


def pair_kernel(
    mask_ref, f_far, pt_far, q_far, o_ref, f_ref, pt_ref, q_ref, total_ref, held_ref, order_ref, sems
):
    loads = [
        pltpu.make_async_copy(far, near, sems.at[at])
        for at, (far, near) in enumerate(((f_far, f_ref), (pt_far, pt_ref), (q_far, q_ref)))
    ]
    for load in loads:
        load.start()
    order_ref[0] = 0

    def note(at, count):
        order_ref[count + 1] = at
        return count + mask_ref[at]

    count = lax.fori_loop(0, 4 * TILES, note, jnp.int32(0))
    for u in range(UNROLL + 1):
        order_ref[count + 1 + u] = 0
    total_ref[...] = jnp.zeros(total_ref.shape, jnp.float32)
    held_ref[1] = jnp.zeros((256, TILE), jnp.bfloat16)
    for load in loads:
        load.wait()

    def run(start, steps):
        for u in range(steps):
            t = start + u
            new, old = order_ref[t + 1], order_ref[t]
            valid = (t >= 1) & (t <= count)
            i = old % TILES
            at = pl.multiple_of((i % 4) * 64, 64)
            flux = jnp.concatenate(
                [f_ref[i // 4, pl.ds(at, 32), :], f_ref[i // 4, pl.ds(at + 32, 32), :]], axis=1
            )
            flux = jnp.where(valid, flux, jnp.zeros_like(flux))
            for c in range(4):
                columns = slice(c * 512, (c + 1) * 512)
                distance = jnp.dot(
                    pt_ref[new % TILES],
                    q_ref[new // TILES, :, columns],
                    preferred_element_type=jnp.float32,
                )
                held_ref[u % 2, :, columns] = lax.rsqrt(distance).astype(jnp.bfloat16)
                total_ref[old // TILES, :, columns] += jnp.dot(
                    flux, held_ref[1 - u % 2, :, columns], preferred_element_type=jnp.float32
                )

    def long_block(b, carry):
        run(b * LONG, LONG)
        return carry

    def short_block(b, carry):
        run(full * LONG + b * UNROLL, UNROLL)
        return carry

    full = (count + 1) // LONG
    lax.fori_loop(0, full, long_block, 0)
    lax.fori_loop(0, (count + UNROLL - full * LONG) // UNROLL, short_block, 0)
    for j in range(4):
        for c in range(2):
            o_ref[2 * j + c] = total_ref[j, :, c * 1024 : (c + 1) * 1024].astype(jnp.bfloat16)


def apply_pairs(mask, flux_rows, row_features, col_features):
    hbm = pl.BlockSpec(memory_space=pltpu.HBM)
    return pl.pallas_call(
        pair_kernel,
        out_shape=jax.ShapeDtypeStruct((LINE, 32, 1024), jnp.bfloat16),
        in_specs=[pl.BlockSpec(memory_space=pltpu.SMEM), hbm, hbm, hbm],
        out_specs=pl.BlockSpec(memory_space=pltpu.VMEM),
        scratch_shapes=[
            pltpu.VMEM(flux_rows.shape, jnp.bfloat16),
            pltpu.VMEM(row_features.shape, jnp.bfloat16),
            pltpu.VMEM(col_features.shape, jnp.bfloat16),
            pltpu.VMEM((4, 32, TILE), jnp.float32),
            pltpu.VMEM((2, 256, TILE), jnp.bfloat16),
            pltpu.SMEM((4 * TILES + UNROLL + 2,), jnp.int32),
            pltpu.SemaphoreType.DMA((3,)),
        ],
        compiler_params=pltpu.CompilerParams(vmem_limit_bytes=WIDE),
        cost_estimate=pl.CostEstimate(
            flops=100_000_000_000, bytes_accessed=8 << 20, transcendentals=0
        ),
    )(mask, flux_rows, row_features, col_features)


def remote(src, dst, sends, recvs, at, device):
    return pltpu.make_async_remote_copy(
        src_ref=src,
        dst_ref=dst,
        send_sem=sends.at[at],
        recv_sem=recvs.at[at],
        device_id=(device,),
        device_id_type=pl.DeviceIdType.MESH,
    )


def greet(devices):
    barrier = pltpu.get_barrier_semaphore()
    for device in devices:
        pl.semaphore_signal(
            barrier, inc=1, device_id=(device,), device_id_type=pl.DeviceIdType.MESH
        )
    pl.semaphore_wait(barrier, len(devices))


def split3(value):
    high = value.astype(jnp.bfloat16).astype(jnp.float32)
    rest = value - high
    middle = rest.astype(jnp.bfloat16).astype(jnp.float32)
    return high, middle, rest - middle


def factors(pos, area, row_side):
    pos = pos - 0.5
    scale = (math.sqrt(TILE) / kernel_gain) / (area * area)
    norm = pos[0:1] * pos[0:1] + pos[1:2] * pos[1:2] + pos[2:3] * pos[2:3]
    one = jnp.ones_like(norm)
    rest = jnp.zeros((3, norm.shape[1]), jnp.float32)
    if row_side:
        parts = jnp.concatenate([norm + softening, one, -2.0 * pos, rest], axis=0) * scale
    else:
        parts = jnp.concatenate([one, norm, pos, rest], axis=0) * scale
    high, middle, low = split3(parts)
    if row_side:
        return jnp.concatenate([high, high, middle, middle, high, low], axis=0)
    return jnp.concatenate([high, middle, high, middle, low, high], axis=0)


def relax(field, source, conduct, step, lane):
    layer = jnp.zeros((1, 8, 128), jnp.float32)
    above = jnp.concatenate([field[1:], layer], axis=0)
    below = jnp.concatenate([layer, field[:-1]], axis=0)
    flat = field.reshape(LAYERS * 8, 128)
    right = jnp.where(lane < 127, pltpu.roll(flat, 127, axis=1).reshape(field.shape), 0.0)
    left = jnp.where(lane > 0, pltpu.roll(flat, 1, axis=1).reshape(field.shape), 0.0)
    ahead = pltpu.roll(field, 7, axis=1)
    behind = pltpu.roll(field, 1, axis=1)
    beside = (above + below) + (ahead + behind) + (right + left)
    applied = conduct * (6.0 * field - beside) + field
    return field + step * (source - applied)


def exchange_kernel(
    material_ref,
    scale_ref,
    list_ref,
    factor_ref,
    flux_far,
    field_far,
    source_far,
    pos_far,
    area_far,
    out_ref,
    top_ref,
    rows_ref,
    pt_ref,
    q_ref,
    flux_ref,
    field_ref,
    source_ref,
    pos_ref,
    area_ref,
    conduct_ref,
    slices,
    shared,
    stage,
    edge_field,
    edge_source,
    edge_conduct,
    halo_field,
    halo_source,
    halo_conduct,
    tops,
    pt_held,
    q_held,
    local,
    line_send,
    line_recv,
    edge_send,
    edge_recv,
    plane_send,
    plane_recv,
):
    me = lax.axis_index("dev")
    m, r = me // LINE, lax.rem(me, LINE)
    y, x = m // 4, lax.rem(m, 4)
    line = [LINE * m + lax.rem(r + k, LINE) for k in range(1, LINE)]
    after = lax.rem(me + 1, LINE * PLANE)
    before = lax.rem(me + LINE * PLANE - 1, LINE * PLANE)
    along_x = [LINE * (4 * y + lax.rem(x + k, 4)) + r for k in range(1, 4)]
    along_y = [LINE * (4 * lax.rem(y + k, 4) + x) + r for k in range(1, 4)]
    loads = [
        pltpu.make_async_copy(far, near, local.at[at])
        for at, (far, near) in enumerate(
            (
                (flux_far, flux_ref),
                (field_far, field_ref),
                (source_far, source_ref),
                (pos_far, pos_ref),
                (area_far, area_ref),
            )
        )
    ]
    for load in loads:
        load.start()
    partners = line + [after, before] + along_x + along_y
    barrier = pltpu.get_barrier_semaphore()
    for device in partners:
        pl.semaphore_signal(
            barrier, inc=1, device_id=(device,), device_id_type=pl.DeviceIdType.MESH
        )

    pairs = jnp.concatenate(
        [list_ref[...].astype(jnp.float32), jnp.zeros((2, 112), jnp.float32)], axis=1
    )
    pairs = jnp.concatenate([pairs, jnp.zeros((14, 128), jnp.float32)], axis=0)
    own_list = pltpu.roll(pairs, 16 * r, axis=1).astype(jnp.bfloat16)
    loads[0].wait()
    for s in range(LINE):
        slices[s, 0:32, :] = flux_ref[:, s * 128 : (s + 1) * 128].astype(jnp.bfloat16)
        slices[s, 32:48, :] = own_list
    for layer in range(LAYERS):
        kind = material_ref[layer]
        scale = jnp.float32(0.0)
        for known in range(4):
            scale = scale + jnp.where(kind == known, scale_ref[known], 0.0)
        conduct_ref[layer] = factor_ref[layer] * scale
    loads[1].wait()
    loads[2].wait()
    for side, (at, one) in enumerate(((2, 3), (0, 0))):
        edge_field[side] = field_ref[:, :, at : at + 2, :]
        edge_source[side] = source_ref[:, :, one, :]
        edge_conduct[side] = conduct_ref[:, one, :]
    pl.semaphore_wait(barrier, len(partners))

    edges = []
    for side, device in enumerate((after, before)):
        for which, (src, dst) in enumerate(
            ((edge_field, halo_field), (edge_source, halo_source), (edge_conduct, halo_conduct))
        ):
            edges.append(
                remote(
                    src.at[side], dst.at[side], edge_send, edge_recv, 3 * side + which, device
                )
            )
    copies = []
    for k in range(1, LINE):
        there = lax.rem(r + k, LINE)
        copies.append(
            remote(slices.at[there], shared.at[r], line_send, line_recv, k - 1, line[k - 1])
        )
    for copy in copies + edges:
        copy.start()
    shared[r] = slices[r]

    def row_block(step, carry):
        for u in range(8):
            half = step * 8 + u
            at = pl.multiple_of(half * 1024 + r * 128, 128)
            part = factors(pos_ref[:, pl.ds(at, 128)], area_ref[:, pl.ds(at, 128)], True)
            pt_held[half] = part.T.astype(jnp.bfloat16)
        return carry

    loads[3].wait()
    loads[4].wait()
    lax.fori_loop(0, 8, row_block, 0)

    for copy in copies:
        copy.wait()
    lists = jnp.zeros((16, 128), jnp.float32)
    for s in range(LINE):
        stage[32 * s : 32 * s + 32, :] = shared[s, 0:32, :]
        lists = lists + shared[s, 32:48, :].astype(jnp.float32)
    stage[256:272, :] = lists.astype(jnp.bfloat16)
    own = pltpu.make_async_copy(stage, rows_ref.at[y, x], local.at[5])
    own.start()
    one, two = slice(0, 128), slice(128, 272)
    near, far = [], []
    for k in range(3):
        near.append(
            remote(stage.at[one], rows_ref.at[y, x, one], plane_send, plane_recv, k, along_x[k])
        )
        near.append(
            remote(
                stage.at[two], rows_ref.at[y, x, two], plane_send, plane_recv, 3 + k, along_y[k]
            )
        )
        part = rows_ref.at[y, :, one]
        far.append(remote(part, part, plane_send, plane_recv, 6 + k, along_y[k]))
        part = rows_ref.at[:, x, two]
        far.append(remote(part, part, plane_send, plane_recv, 9 + k, along_x[k]))
    for copy in near:
        copy.start()

    lax.fori_loop(8, TILES // 4, row_block, 0)
    moves = [pltpu.make_async_copy(pt_held, pt_ref, local.at[6])]
    moves[0].start()
    for j in range(4):
        for c in range(4):
            at = pl.multiple_of(m * COLS + j * TILE + c * 512, 512)
            part = factors(pos_ref[:, pl.ds(at, 512)], area_ref[:, pl.ds(at, 512)], False)
            q_held[j, :, c * 512 : (c + 1) * 512] = part.astype(jnp.bfloat16)
    moves.append(pltpu.make_async_copy(q_held, q_ref, local.at[7]))
    moves[1].start()
    own.wait()
    for copy in near:
        copy.wait()
    for copy in far:
        copy.start()

    for copy in edges:
        copy.wait()
    row = lax.broadcasted_iota(jnp.int32, (LAYERS, 8, 128), 1)
    lane = lax.broadcasted_iota(jnp.int32, (LAYERS, 8, 128), 2)
    real = ((row >= 2) | (me > 0)) & ((row < 6) | (me < LINE * PLANE - 1))
    pad = jnp.zeros((LAYERS, 1, 128), jnp.float32)
    conduct = jnp.concatenate(
        [pad, halo_conduct[0][:, None], conduct_ref[...], halo_conduct[1][:, None], pad], axis=1
    )
    step = relax_rate / (6.0 * conduct + 1.0)

    def one_load(load, carry):
        field = jnp.concatenate(
            [halo_field[0, load], field_ref[load], halo_field[1, load]], axis=1
        )
        field = jnp.where(real, field, 0.0)
        source = jnp.concatenate(
            [
                pad,
                halo_source[0, load][:, None],
                source_ref[load],
                halo_source[1, load][:, None],
                pad,
            ],
            axis=1,
        )
        field = jnp.where(real, relax(field, source, conduct, step, lane), 0.0)
        field = relax(field, source, conduct, step, lane)
        out_ref[load] = field[:, 2:6]
        tops[load] = field[LAYERS - 1, 2:6]
        return carry

    lax.fori_loop(0, 32, one_load, 0, unroll=4)
    for at in range(4):
        top_ref[at] = tops[:, at, :].astype(jnp.bfloat16)

    for copy in far + moves:
        copy.wait()


def exchange(materials, scales, lists, factor, flux, field, source, pos, area):
    vmem = pl.BlockSpec(memory_space=pltpu.VMEM)
    hbm = pl.BlockSpec(memory_space=pltpu.HBM)
    smem = pl.BlockSpec(memory_space=pltpu.SMEM)
    row_shape, col_shape = (2 * TILES, 128, 48), (4, 48, TILE)
    f32, half = jnp.float32, jnp.bfloat16
    halo = [
        pltpu.VMEM((2, 32, LAYERS, 2, 128), f32),
        pltpu.VMEM((2, 32, LAYERS, 128), f32),
        pltpu.VMEM((2, LAYERS, 128), f32),
    ]
    return pl.pallas_call(
        exchange_kernel,
        out_shape=(
            jax.ShapeDtypeStruct(field.shape, f32),
            jax.ShapeDtypeStruct((4, 32, 128), half),
            jax.ShapeDtypeStruct((4, 4, 272, 128), half),
            jax.ShapeDtypeStruct(row_shape, half),
            jax.ShapeDtypeStruct(col_shape, half),
        ),
        in_specs=[smem, smem, vmem, vmem] + [hbm] * 5,
        out_specs=(vmem, vmem, hbm, hbm, hbm),
        scratch_shapes=[
            pltpu.VMEM(flux.shape, f32),
            pltpu.VMEM(field.shape, f32),
            pltpu.VMEM(source.shape, f32),
            pltpu.VMEM(pos.shape, f32),
            pltpu.VMEM(area.shape, f32),
            pltpu.VMEM(factor.shape, f32),
            pltpu.VMEM((LINE, 48, 128), half),
            pltpu.VMEM((LINE, 48, 128), half),
            pltpu.VMEM((272, 128), half),
        ]
        + halo
        + halo
        + [
            pltpu.VMEM((32, 4, 128), f32),
            pltpu.VMEM(row_shape, half),
            pltpu.VMEM(col_shape, half),
            pltpu.SemaphoreType.DMA((8,)),
            pltpu.SemaphoreType.DMA((LINE - 1,)),
            pltpu.SemaphoreType.DMA((LINE - 1,)),
            pltpu.SemaphoreType.DMA((6,)),
            pltpu.SemaphoreType.DMA((6,)),
            pltpu.SemaphoreType.DMA((12,)),
            pltpu.SemaphoreType.DMA((12,)),
        ],
        compiler_params=pltpu.CompilerParams(
            collective_id=0, has_side_effects=True, vmem_limit_bytes=WIDE
        ),
    )(materials, scales, lists, factor, flux, field, source, pos, area)


def finish_kernel(
    cell_ref,
    part_ref,
    table_ref,
    flux_ref,
    out_ref,
    table,
    landed,
    traces,
    own,
    load_sem,
    own_sem,
    sends,
    recvs,
):
    me = lax.axis_index("dev")
    m, r = me // LINE, lax.rem(me, LINE)
    load = pltpu.make_async_copy(table_ref, table, load_sem)
    load.start()
    keep = pltpu.make_async_copy(part_ref.at[r], own, own_sem)
    keep.start()
    line = [LINE * m + lax.rem(r + k, LINE) for k in range(1, LINE)]
    greet(line)
    copies = []
    for k in range(1, LINE):
        there = lax.rem(r + k, LINE)
        copy = remote(part_ref.at[there], landed.at[k - 1], sends, recvs, k - 1, line[k - 1])
        copy.start()
        copies.append(copy)
    load.wait()
    lane = lax.broadcasted_iota(jnp.int32, (32, 128), 1)

    def group(g, carry):
        def pick(step, held):
            held = list(held)
            for u in range(64):
                at = step * 64 + u
                cell = cell_ref[g * 128 + at]
                block = table[lax.shift_right_logical(cell, 7)].astype(jnp.float32)
                moved = pltpu.roll(block, (at - cell) & 127, axis=1)
                held[u % 4] = jnp.where(lane == at, moved, held[u % 4])
            return tuple(held)

        held = lax.fori_loop(0, 2, pick, (jnp.zeros((32, 128), jnp.float32),) * 4)
        traces[g] = (held[0] + held[1]) + (held[2] + held[3])
        return carry

    lax.fori_loop(0, 8, group, 0)
    for copy in copies:
        copy.wait()
    keep.wait()
    total = own[...].astype(jnp.float32)
    for k in range(LINE - 1):
        total = total + landed[k].astype(jnp.float32)
    for g in range(8):
        at = slice(g * 128, (g + 1) * 128)
        out_ref[:, at] = flux_ref[:, at] + update_rate * (traces[g] - total[:, at])


def finish(cells, partial, table, flux_in):
    vmem = pl.BlockSpec(memory_space=pltpu.VMEM)
    return pl.pallas_call(
        finish_kernel,
        out_shape=jax.ShapeDtypeStruct(flux_in.shape, jnp.float32),
        in_specs=[
            pl.BlockSpec(memory_space=pltpu.SMEM),
            pl.BlockSpec(memory_space=pltpu.HBM),
            pl.BlockSpec(memory_space=pltpu.HBM),
            vmem,
        ],
        out_specs=vmem,
        scratch_shapes=[
            pltpu.VMEM(table.shape, jnp.bfloat16),
            pltpu.VMEM((LINE - 1, 32, 1024), jnp.bfloat16),
            pltpu.VMEM((8, 32, 128), jnp.float32),
            pltpu.VMEM((32, 1024), jnp.bfloat16),
            pltpu.SemaphoreType.DMA,
            pltpu.SemaphoreType.DMA,
            pltpu.SemaphoreType.DMA((LINE - 1,)),
            pltpu.SemaphoreType.DMA((LINE - 1,)),
        ],
        compiler_params=pltpu.CompilerParams(
            collective_id=1, has_side_effects=True, vmem_limit_bytes=WIDE
        ),
    )(cells, partial, table, flux_in)


def body(
    field_in,
    source,
    cell_factor,
    layer_material,
    material_scale,
    panel_cell,
    panel_pos,
    panel_area,
    flux_in,
    pair_list,
):
    me = lax.axis_index("dev")
    m = me // LINE

    field_now, surface_top, rows, row_features, col_features = exchange(
        layer_material,
        material_scale,
        pair_list.T,
        cell_factor,
        flux_in,
        field_in,
        source,
        panel_pos,
        panel_area.reshape(1, -1),
    )
    table = lax.all_gather(surface_top, "dev", axis=0, tiled=True)
    rows = rows.reshape(PLANE, 272, 128)
    tile_ids = jnp.arange(TILES, dtype=jnp.bfloat16)[:, None]
    upper = (rows[:, 256].reshape(1, -1) == tile_ids).astype(jnp.bfloat16)
    lower = (rows[:, 257].reshape(1, -1) == tile_ids).astype(jnp.bfloat16)
    listed = lax.dot_general(
        upper, lower, (((1,), (1,)), ((), ())), preferred_element_type=jnp.float32
    )
    listed = (listed + listed.T > 0.0).astype(jnp.int32)
    mask = lax.dynamic_slice(listed, (4 * m, 0), (4, TILES)).reshape(-1)

    partial = apply_pairs(mask, rows, row_features.reshape(TILES, 256, 48), col_features)
    partial, field_now = lax.optimization_barrier((partial, field_now))
    field_now = jnp.where(me >= 0, field_now, 0.0)
    partial, field_now = lax.optimization_barrier((partial, field_now))
    flux_out = finish(panel_cell, partial, table, flux_in)
    return (field_now, flux_out)


def solution(mesh):
    in_specs = (
        P(None, None, "dev", None),
        P(None, None, "dev", None),
        P(None, "dev", None),
        P(),
        P(),
        P("dev"),
        P(),
        P(),
        P(None, "dev"),
        P("dev", None),
    )
    out_specs = (P(None, None, "dev", None), P(None, "dev"))
    return jax.shard_map(body, mesh=mesh, in_specs=in_specs, out_specs=out_specs, check_vma=False)
```
